32 devices in a mesh: rep: 4 (over y, x), grp: 8 (over z, core).
Axes of the slice: x: 2, y: 2, z: 4, core: 2. Of those that a mesh axis runs over, the one named last changes fastest.
Arguments:
- tokens: bfloat16 [4, 2048, 768], P('rep', 'grp'), may hold values from -6 to 6
- segments: int32 [4, 2048], P('rep', 'grp'), may hold values from 0 to 5, as said below
- block_sets: int32 [4, 16, 16], P('rep'), may hold values from 0 to 1, as said below
- routes: int32 [4, 2048, 2], P('rep', 'grp'), may hold values from 0 to 7, all different within a row; in each aligned block of 256 rows (0 to 255, 256 to 511, ..., all dimensions but the last counted through in order) at most 92 rows name the same one
- qkv_weight: bfloat16 [768, 2, 3, 768], P('grp'), may hold values from -0.21875 to 0.21875
- out_weight: bfloat16 [768, 2, 768], P('grp'), may hold values from -0.875 to 0.875
- ffn_in: bfloat16 [768, 3072], P('grp'), may hold values from -0.21875 to 0.21875
- ffn_out: bfloat16 [768, 3072], P('grp'), may hold values from -0.109375 to 0.109375
- norm_gains: float32 [2, 2, 768], replicated, may hold values from 0.5 to 1.5
- rel_bias: float32 [2, 12, 32], replicated, may hold values from -4 to 4
- router: bfloat16 [768, 8], replicated, may hold values from -0.4375 to 0.4375
- expert_in: bfloat16 [8, 768, 3072], P('grp'), may hold values from -0.21875 to 0.21875
- expert_out: bfloat16 [8, 3072, 768], P('grp'), may hold values from -0.109375 to 0.109375
- cotangent: bfloat16 [4, 2048, 768], P('rep', 'grp'), may hold values from -6 to 6
Outputs:
- final_out: float32 [4, 2048, 768], P('rep', 'grp')
- tokens_grad: float32 [4, 2048, 768], P('rep', 'grp')
- qkv_grad: float32 [768, 2, 3, 768], P('grp')
- out_grad: float32 [768, 2, 768], P('grp')
- ffn_in_grad: float32 [768, 3072], P('grp')
- ffn_out_grad: float32 [768, 3072], P('grp')
- gains_grad: float32 [2, 2, 768], replicated
- bias_grad: float32 [2, 12, 32], replicated
- router_grad: float32 [768, 8], replicated
- expert_in_grad: float32 [8, 768, 3072], P('grp')
- expert_out_grad: float32 [8, 3072, 768], P('grp')
The draws below stay inside these ranges and needn't reach their ends.
Inputs may be any that keep to these rules, and one draw needn't show every extreme that they name: block_sets is 1 on the diagonal (i = j) and in the first column (j = 0), and 0 above the diagonal (j > i). segments never fall along a sequence. `routes`: each position names 2 different experts; within the 256 positions of one index of grp no expert is named more than 92 times, and some expert is named 92 times.
All inputs are finite; a program needn't handle non-finite values.
Results may differ from the reference program's by a relative error of at most 0.03.
Values may be sent and summed in bfloat16 or wider, within the bound.
No kernel may reach another device: no remote copies, remote signals or barrier semaphores. Data moves between devices by JAX's collectives and lax.ppermute only.
A program may use at most 256 MiB of HBM per device.

```python
import math
import jax
import jax.numpy as jnp
import numpy as np
from jax import lax

D = 768
HEADS = 12
HEAD = 64
FF = 3072
TOK_DEV = 256
TOP = 2
BUCKETS = 32
BLK = 128
DOCS = 6
LAYERS = 2
EXPERTS = 8
LENGTH = 2048
SEQS = 4
NB = 16
CAP = 92


def draw_block_sets(key, part):
    random_bits = jax.random.randint(key, (SEQS, NB, NB), 0, 2, dtype=jnp.int32)
    row_ids = lax.broadcasted_iota(jnp.int32, (SEQS, NB, NB), 1)
    col_ids = lax.broadcasted_iota(jnp.int32, (SEQS, NB, NB), 2)
    lower = jnp.where((col_ids == row_ids) | (col_ids == 0), 1, random_bits)
    return jnp.where(col_ids <= row_ids, lower, 0).astype(jnp.int32)


def draw_segments(key, part):
    first_end = jax.random.randint(key, (SEQS, 1), LENGTH - TOK_DEV, LENGTH - DOCS + 1, dtype=jnp.int32)
    pos_ids = lax.broadcasted_iota(jnp.int32, (SEQS, LENGTH), 1)
    tail_len = LENGTH - 1 - first_end
    tail_pos = jnp.maximum(pos_ids - first_end - 1, 0)
    tail_doc = 1 + tail_pos * (DOCS - 1) // jnp.maximum(tail_len, 1)
    return jnp.where(pos_ids <= first_end, 0, jnp.minimum(tail_doc, DOCS - 1)).astype(jnp.int32)


def block_levels(own_key, shape, split, smallest, top_value):
    def one(dim, blocks):
        heights = jax.random.uniform(jax.random.fold_in(jax.random.fold_in(own_key, 6), dim), (blocks,), jnp.float32, smallest / len(split), top_value / len(split))
        return jnp.repeat(jnp.exp(heights), shape[dim] // blocks).reshape((-1,) + (1,) * (len(shape) - dim - 1))

    gain = one(*split[0])
    for cut in split[1:]:
        gain = gain * one(*cut)
    return gain


def assign_block(own_key, own, number, rows, number_of, top, limit, slope):
    sequence = jax.random.permutation(own_key, number_of)
    crowded, usual = load_shares(number_of, rows * top, limit, slope, True), load_shares(number_of, rows * top, limit, slope, False)
    places = jnp.arange(number_of)

    def named(lengths, offset_by):
        used = int((lengths > 0).sum())
        fixed = max(1, used // 4)
        moved = fixed + (places - fixed + offset_by * (used - fixed)) % max(1, number_of - fixed)
        return jnp.zeros((number_of,), jnp.int32).at[sequence[jnp.where(places < fixed, places, moved)]].set(jnp.asarray(lengths, jnp.int32))

    lengths = jnp.where(number % 4 == 0, named(crowded, number // 4), named(usual, number - number // 4 - 1))
    mixed = jax.random.permutation(jax.random.fold_in(own, 3), number_of)
    donor, receiver = mixed[0:number_of // 2 * 2:2], mixed[1:number_of // 2 * 2:2]
    margin = jnp.minimum(lengths[donor] - 1, limit - lengths[receiver]) // 2
    margin = jnp.where((donor == sequence[0]) | (receiver == sequence[0]) | (lengths[receiver] == 0), 0, jnp.maximum(margin, 0))
    moved = jax.random.randint(jax.random.fold_in(own, 4), (number_of // 2,), 0, 1 << 20) % (margin + 1)
    lengths = lengths.at[donor].add(-moved).at[receiver].add(moved)
    items = jnp.searchsorted(jnp.cumsum(lengths), jnp.arange(rows * top), side="right").astype(jnp.int32)
    grid = items.reshape(top, rows).T
    grid = grid[jax.random.permutation(jax.random.fold_in(own, 1), rows)]
    offset_by = jax.random.randint(jax.random.fold_in(own, 2), (rows, 1), 0, top)
    return jnp.take_along_axis(grid, (jnp.arange(top)[None, :] + offset_by) % top, axis=1)


def load_shares(amount, total, reach, lean, full):
    weights = [(1 << 20) // math.isqrt(grade ** lean) + 1 for grade in range(1, amount + 1)]
    largest = reach if full else min(reach, max(-(-total // amount), total * weights[0] // sum(weights)))
    least = 1 if total - largest >= amount - 1 else 0
    holding, surplus = [largest] + [least] * (amount - 1), total - largest - least * (amount - 1)
    while surplus > 0:
        free = [i for i in range(1, amount) if holding[i] < largest] or [i for i in range(1, amount) if holding[i] < reach]
        mass, remaining = sum([weights[i] for i in free]), surplus
        for i in free:
            addition = min(reach - holding[i], max(1, remaining * weights[i] // mass), surplus)
            holding[i] = holding[i] + addition
            surplus = surplus - addition
    return np.array(holding)


def normal_values(rng, shape, spread, most, shards=(), kind=jnp.bfloat16):
    result = spread * jax.random.normal(rng, shape, jnp.float32)
    if shards:
        result = result * block_levels(rng, shape, shards, -0.22, 0.18)
    return jnp.clip(result, -most, most).astype(kind)


def setup_inputs(seed: int = 0) -> dict:
    key_of = jax.random.split(jax.random.key(seed), 15)
    tokens = normal_values(key_of[0], (SEQS, LENGTH, D), 1.0, 6.0, ((0, 4), (1, 8)))
    segments = draw_segments(jax.random.fold_in(key_of[14], 71), 0)
    block_sets = draw_block_sets(jax.random.fold_in(key_of[14], 71), 0)
    routes_keys = jax.random.split(jax.random.fold_in(key_of[3], 1), SEQS * LENGTH // TOK_DEV)
    routes_turns = jax.random.permutation(jax.random.fold_in(key_of[3], 3), SEQS * LENGTH // TOK_DEV)
    routes = jax.vmap(lambda own, number: assign_block(jax.random.fold_in(key_of[3], 2), own, number, TOK_DEV, EXPERTS, TOP, CAP, 1))(routes_keys, routes_turns).reshape((SEQS, LENGTH, TOP))
    qkv_weight = normal_values(key_of[4], (D, LAYERS, 3, D), D ** -0.5, 0.21875, ((0, 8),))
    out_weight = normal_values(key_of[5], (D, LAYERS, D), (D // 16) ** -0.5, 0.875, ((0, 8),))
    ffn_in = normal_values(key_of[6], (D, FF), D ** -0.5, 0.21875, ((0, 8),))
    ffn_out = normal_values(key_of[7], (D, FF), FF ** -0.5, 0.109375, ((0, 8),))
    norm_gains = jnp.clip(1.0 + 0.1 * jax.random.normal(key_of[8], (LAYERS, 2, D), jnp.float32), 0.5, 1.5)
    rel_bias = normal_values(key_of[9], (LAYERS, HEADS, BUCKETS), 1.0, 4.0, (), jnp.float32)
    router = normal_values(key_of[10], (D, EXPERTS), (D // 4) ** -0.5, 0.4375)
    expert_in = normal_values(key_of[11], (EXPERTS, D, FF), D ** -0.5, 0.21875, ((0, 8),))
    expert_out = normal_values(key_of[12], (EXPERTS, FF, D), FF ** -0.5, 0.109375, ((0, 8),))
    cotangent = normal_values(key_of[13], (SEQS, LENGTH, D), 1.0, 6.0, ((0, 4), (1, 8)))
    return {"tokens": tokens, "segments": segments, "block_sets": block_sets, "routes": routes, "qkv_weight": qkv_weight, "out_weight": out_weight, "ffn_in": ffn_in, "ffn_out": ffn_out, "norm_gains": norm_gains, "rel_bias": rel_bias, "router": router, "expert_in": expert_in, "expert_out": expert_out, "cotangent": cotangent}


BUCKET_EDGES = (18, 20, 23, 26, 30, 34, 39, 45, 51, 58, 66, 76, 86, 98, 112)
PRECISE = lax.Precision.HIGHEST
norm_eps = 1e-06

@jax.custom_vjp
def low(v):
    return lax.optimization_barrier(v.astype(jnp.bfloat16)).astype(jnp.float32)

@jax.custom_vjp
def low_back(v):
    return v

def low_keep(v):
    return (low(v), None)

def low_pass(kept, grad):
    return (grad,)

def back_keep(v):
    return (v, None)

def back_low(kept, grad):
    return (low(grad),)
low.defvjp(low_keep, low_pass)
low_back.defvjp(back_keep, back_low)

def norm_rows(residual, gain_vec):
    return residual * lax.rsqrt(lax.optimization_barrier(jnp.mean(residual * residual, axis=-1, keepdims=True)) + norm_eps) * gain_vec

def bucket_of(pos_gap):
    clipped = jnp.maximum(pos_gap, 0)
    bucket = jnp.minimum(clipped, 16)
    for edge_at in BUCKET_EDGES:
        bucket = bucket + (clipped >= edge_at).astype(jnp.int32)
    return bucket

def reference(tokens, segments, block_sets, routes, qkv_weight, out_weight, ffn_in, ffn_out, norm_gains, rel_bias, router, expert_in, expert_out, cotangent):
    seq_count = tokens.shape[0]
    length_all = tokens.shape[1]
    width_all = tokens.shape[2]
    experts_all = router.shape[1]
    token_total = seq_count * length_all
    pair_total = 2 * token_total
    block_count = pair_total // (2 * TOK_DEV)
    flat_ids = routes.reshape(pair_total).astype(jnp.int32)
    flat_hot = (flat_ids[:, None] == jnp.arange(experts_all, dtype=jnp.int32)[None, :]).astype(jnp.int32)
    running = jnp.cumsum(flat_hot.reshape(block_count, 2 * TOK_DEV, experts_all), axis=1).reshape(pair_total, experts_all)
    slot_ids = lax.optimization_barrier(jnp.sum((running - 1) * flat_hot, axis=1)).astype(jnp.int32)
    block_ids = jnp.arange(pair_total, dtype=jnp.int32) // (2 * TOK_DEV)
    target = ((block_ids * experts_all + flat_ids) * CAP + slot_ids).astype(jnp.int32)
    source = jnp.full((block_count * experts_all * CAP,), pair_total, dtype=jnp.int32).at[target].set(jnp.arange(pair_total, dtype=jnp.int32))
    route_pairs = routes.reshape(token_total, 2).astype(jnp.int32)
    positions = jnp.arange(length_all, dtype=jnp.int32)
    rows_step = min(512, length_all)

    def attend(residual, w_qkv, w_out, gain_vec, bias_table, seg_ids, blocks):
        normed = low(norm_rows(residual, gain_vec))
        projected = jnp.einsum('td,dcf->tcf', normed, w_qkv, precision=PRECISE)
        queries = low_back(low(projected[:, 0])).reshape(length_all, HEADS, HEAD)
        keys_all = low_back(low(projected[:, 1])).reshape(length_all, HEADS, HEAD)
        values_all = low_back(low(projected[:, 2])).reshape(length_all, HEADS, HEAD)

        def one_block(start_at):
            query_pos = start_at + jnp.arange(rows_step, dtype=jnp.int32)
            query_rows = lax.dynamic_slice_in_dim(queries, start_at, rows_step, 0)
            raw_scores = low_back(0.125 * jnp.einsum('qhd,khd->hqk', query_rows, keys_all, precision=PRECISE))
            pos_gap = query_pos[:, None] - positions[None, :]
            bias_terms = bias_table[:, bucket_of(pos_gap)]
            query_seg = lax.dynamic_slice_in_dim(seg_ids, start_at, rows_step, 0)
            block_hit = blocks[(query_pos // BLK)[:, None], (positions // BLK)[None, :]]
            allowed = (pos_gap >= 0) & (query_seg[:, None] == seg_ids[None, :]) & (block_hit == 1)
            scores = jnp.where(allowed[None], raw_scores + bias_terms, -1e+30)
            prob_rows = jax.nn.softmax(scores, axis=-1)
            return jnp.einsum('hqk,khd->qhd', low(prob_rows), values_all, precision=PRECISE)
        starts = jnp.arange(length_all // rows_step, dtype=jnp.int32) * rows_step
        context = lax.map(jax.checkpoint(one_block), starts).reshape(length_all, width_all)
        context = low_back(low(context))
        return residual + low_back(jnp.dot(context, w_out, precision=PRECISE))

    def forward(stream, w_qkv_all, w_out_all, w_in, w_down, gain_all, table_all, w_router, w_expert_in, w_expert_out):

        def attend_layer(resid_all, layer_idx):
            pieces = [attend(resid_all[seq_idx], w_qkv_all[:, layer_idx], w_out_all[:, layer_idx], gain_all[layer_idx, 0], table_all[layer_idx], segments[seq_idx], block_sets[seq_idx]) for seq_idx in range(seq_count)]
            return jnp.stack(pieces)
        first_out = attend_layer(stream, 0).reshape(token_total, width_all)
        normed = low(norm_rows(first_out, gain_all[0, 1]))
        pre_ffn = low_back(jnp.dot(normed, w_in, precision=PRECISE))
        hidden = low(jax.nn.gelu(pre_ffn))
        second_in = first_out + low_back(jnp.einsum('tf,df->td', hidden, w_down, precision=PRECISE))
        second = attend_layer(second_in.reshape(seq_count, length_all, width_all), 1).reshape(token_total, width_all)
        normed_moe = low(norm_rows(second, gain_all[1, 1]))
        logits = jnp.dot(normed_moe, w_router, precision=PRECISE)
        gate_probs = jax.nn.softmax(jnp.take_along_axis(logits, route_pairs, axis=1), axis=-1)
        paired = jnp.stack([low_back(normed_moe), low_back(normed_moe)], axis=1).reshape(pair_total, width_all)
        padded = jnp.concatenate([paired, jnp.zeros((1, width_all), paired.dtype)], axis=0)
        buffer = padded[source].reshape(block_count, experts_all, CAP, width_all)
        pre_expert = low_back(jnp.einsum('becd,edf->becf', buffer, w_expert_in, precision=PRECISE))
        hidden_expert = low(jax.nn.gelu(pre_expert))
        made_rows = low_back(low(jnp.einsum('becf,efd->becd', hidden_expert, w_expert_out, precision=PRECISE)))
        picked = made_rows.reshape(block_count * experts_all * CAP, width_all)[target].reshape(token_total, 2, width_all)
        final_out = second + lax.optimization_barrier(jnp.sum(gate_probs[:, :, None] * picked, axis=1))
        return final_out.reshape(seq_count, length_all, width_all)
    floats = (tokens.astype(jnp.float32), qkv_weight.astype(jnp.float32), out_weight.astype(jnp.float32), ffn_in.astype(jnp.float32), ffn_out.astype(jnp.float32), norm_gains.astype(jnp.float32), rel_bias.astype(jnp.float32), router.astype(jnp.float32), expert_in.astype(jnp.float32), expert_out.astype(jnp.float32))
    final_out, pull_back = jax.vjp(forward, *floats)
    all_grads = pull_back(cotangent.astype(jnp.float32))
    return (final_out, all_grads[0], all_grads[1], all_grads[2], all_grads[3], all_grads[4], all_grads[5], all_grads[6], all_grads[7], all_grads[8], all_grads[9])
```

```python
from functools import partial

import jax
import jax.numpy as jnp
from jax import lax
from jax.experimental import pallas as pl
from jax.experimental.pallas import tpu as pltpu
from jax.sharding import PartitionSpec as P

D = 768
HEADS = 12
HEAD = 64
PAIRS = 6
BLK = 128
ROWS = 256

BUCKET_EDGES = (18, 20, 23, 26, 30, 34, 39, 45, 51, 58, 66, 76, 86, 98, 112)
PRECISE = lax.Precision.HIGHEST
norm_eps = 1e-06
NEG = -1e30
VMEM_LIMIT = 60 * 1024 * 1024
F32 = jnp.float32
BF16 = jnp.bfloat16


def mm(a, b, ca, cb):
    return lax.dot_general(a, b, (((ca,), (cb,)), ((), ())), preferred_element_type=F32)


def norm_rows(residual, gain_vec):
    return (
        residual
        * lax.rsqrt(jnp.mean(residual * residual, axis=-1, keepdims=True) + norm_eps)
        * gain_vec
    )


def bucket_of(pos_gap):
    clipped = jnp.maximum(pos_gap, 0)
    bucket = jnp.minimum(clipped, 16)
    for edge_at in BUCKET_EDGES:
        bucket = bucket + (clipped >= edge_at).astype(jnp.int32)
    return bucket


def gap_hot():
    gaps = jnp.arange(2 * BLK, dtype=jnp.int32)
    return (bucket_of(gaps)[:, None] == jnp.arange(32, dtype=jnp.int32)[None, :]).astype(F32)


def pair_diag(ref, p, off):
    x = ref[128 * p : 128 * p + 128, pl.ds(off, 128)]
    z = jnp.zeros((64, 128), x.dtype)
    top = jnp.concatenate([x[:64], z], axis=0)
    low = jnp.concatenate([z, x[64:]], axis=0)
    return jnp.concatenate([top, low], axis=1)


def fill_tiles(gap_ref, far_ref, tile_ref):
    rows = lax.broadcasted_iota(jnp.int32, (128, 128), 0)
    cols = lax.broadcasted_iota(jnp.int32, (128, 128), 1)
    causal = cols >= rows
    for h in range(HEADS):
        x = jnp.broadcast_to(gap_ref[h : h + 1, :], (128, 256))
        r = pltpu.roll(x, 0, 1, stride=1, stride_axis=0)
        tile_ref[h, :, 0:128] = jnp.where(causal, r[:, :128], NEG)
        tile_ref[h, :, 128:256] = r[:, 128:]
        half = 128 * (h % 2)
        tile_ref[h, :, 256:384] = jnp.broadcast_to(
            far_ref[h // 2 : h // 2 + 1, half : half + 128], (128, 128)
        )


def seg_ok(segc_ref, segr_ref, i, j):
    kcol = segc_ref[pl.ds(pl.multiple_of(j * 128, 128), 128), :]
    qrow = segr_ref[pl.ds(i, 1), :]
    ok = kcol == qrow
    return jnp.concatenate([ok, ok], axis=1)


def pair_tile(tile_ref, p, dd):
    off = pl.multiple_of(dd * 128, 128)
    return jnp.concatenate(
        [tile_ref[2 * p, :, pl.ds(off, 128)], tile_ref[2 * p + 1, :, pl.ds(off, 128)]], axis=1
    )


def fwd_kernel(
    code_ref, me_ref, qt_ref, k_ref, vt_ref, gap_ref, far_ref, segc_ref, segr_ref,
    ctxt_ref, ctxb_ref, lse_ref, tile_ref, m_ref, l_ref, acc_ref,
):
    fill_tiles(gap_ref, far_ref, tile_ref)
    me = me_ref[0]

    def one_query(qi, _):
        i = me * 2 + qi
        qoff = pl.multiple_of(qi * 128, 128)
        m_ref[...] = jnp.full_like(m_ref, NEG)
        l_ref[...] = jnp.zeros_like(l_ref)
        acc_ref[...] = jnp.zeros_like(acc_ref)

        def visit(j, near):
            koff = pl.multiple_of(j * 128, 128)
            if near:
                dd = jnp.minimum(i - j, 2)
                ok = seg_ok(segc_ref, segr_ref, i, j)
            for p in range(PAIRS):
                kb = k_ref[pl.ds(koff, 128), 128 * p : 128 * p + 128]
                s = mm(kb, pair_diag(qt_ref, p, qoff), 1, 0)
                if near:
                    s = jnp.where(ok, s + pair_tile(tile_ref, p, dd), NEG)
                else:
                    s = s + far_ref[p : p + 1, :]
                m_old = m_ref[p : p + 1, :]
                m_new = jnp.maximum(m_old, jnp.max(s, axis=0, keepdims=True))
                w = jnp.exp(s - m_new)
                shrink = jnp.exp(m_old - m_new)
                m_ref[p : p + 1, :] = m_new
                l_ref[p : p + 1, :] = l_ref[p : p + 1, :] * shrink + jnp.sum(
                    w, axis=0, keepdims=True
                )
                o = mm(vt_ref[128 * p : 128 * p + 128, pl.ds(koff, 128)], w.astype(BF16), 1, 0)
                o = jnp.concatenate([o[:64, :128], o[64:, 128:]], axis=1)
                acc_ref[p] = acc_ref[p] * shrink + o

        visit(i, True)

        def one_key(j, _):
            code = code_ref[i, j]

            @pl.when(code == 1)
            def _():
                visit(j, False)

            @pl.when(code == 2)
            def _():
                visit(j, True)

            return 0

        lax.fori_loop(0, i, one_key, 0)
        for p in range(PAIRS):
            total = l_ref[p : p + 1, :]
            ctx = acc_ref[p] * (1.0 / total)
            both = jnp.concatenate([ctx[:, :128], ctx[:, 128:]], axis=0)
            ctxt_ref[128 * p : 128 * p + 128, pl.ds(qoff, 128)] = both
            ctxb_ref[pl.ds(qoff, 128), 128 * p : 128 * p + 128] = both.T.astype(BF16)
            lse = m_ref[p : p + 1, :] + jnp.log(total)
            lse_ref[2 * p : 2 * p + 1, pl.ds(qoff, 128)] = lse[:, :128]
            lse_ref[2 * p + 1 : 2 * p + 2, pl.ds(qoff, 128)] = lse[:, 128:]
        return 0

    lax.fori_loop(0, 2, one_query, 0)


def bwd_kernel(
    code_ref, me_ref, qt_ref, dt_ref, k_ref, kt_ref, v_ref, lse_ref, delta_ref,
    gap_ref, far_ref, segc_ref, segr_ref,
    dqkv_ref, dgap_ref, dfar_ref,
    tile_ref, near_ref, facc_ref, dq_ref, dk_ref, dv_ref,
):
    fill_tiles(gap_ref, far_ref, tile_ref)
    near_ref[...] = jnp.zeros_like(near_ref)
    facc_ref[...] = jnp.zeros_like(facc_ref)
    me = me_ref[0]

    def lanes(ref, p, i):
        g = i // 2
        off = pl.multiple_of((i % 2) * 128, 128)
        return jnp.concatenate(
            [ref[g, 2 * p : 2 * p + 1, pl.ds(off, 128)], ref[g, 2 * p + 1 : 2 * p + 2, pl.ds(off, 128)]],
            axis=1,
        )

    def grads(i, j, p, near, dd, ok):
        qoff = pl.multiple_of(i * 128, 128)
        koff = pl.multiple_of(j * 128, 128)
        qd = pair_diag(qt_ref, p, qoff)
        dd_ = pair_diag(dt_ref, p, qoff)
        s = mm(k_ref[pl.ds(koff, 128), 128 * p : 128 * p + 128], qd, 1, 0)
        lse = lanes(lse_ref, p, i)
        if near:
            w = jnp.exp(jnp.where(ok, s + pair_tile(tile_ref, p, dd) - lse, NEG))
        else:
            w = jnp.exp(s + (far_ref[p : p + 1, :] - lse))
        dp = mm(v_ref[pl.ds(koff, 128), 128 * p : 128 * p + 128], dd_, 1, 0)
        ds = w * (dp - lanes(delta_ref, p, i))
        return w, ds, qd, dd_

    def visit_query(i, j, near):
        koff = pl.multiple_of(j * 128, 128)
        dd = jnp.minimum(i - j, 2) if near else None
        ok = seg_ok(segc_ref, segr_ref, i, j) if near else None
        for p in range(PAIRS):
            _, ds, _, _ = grads(i, j, p, near, dd, ok)
            if near:
                off = pl.multiple_of(dd * 128, 128)
                near_ref[2 * p, :, pl.ds(off, 128)] += ds[:, :128]
                near_ref[2 * p + 1, :, pl.ds(off, 128)] += ds[:, 128:]
            else:
                part = ds[0:8]
                for a in range(1, 16):
                    part = part + ds[8 * a : 8 * a + 8]
                facc_ref[p] += part
            o = mm(kt_ref[128 * p : 128 * p + 128, pl.ds(koff, 128)], ds.astype(BF16), 1, 0)
            dq_ref[p] += jnp.concatenate([o[:64, :128], o[64:, 128:]], axis=1)

    def one_query(qi, _):
        i = me * 2 + qi
        qoff = pl.multiple_of(qi * 128, 128)
        dq_ref[...] = jnp.zeros_like(dq_ref)

        def one_key(j, _):
            code = code_ref[i, j]

            @pl.when(code == 1)
            def _():
                visit_query(i, j, False)

            @pl.when(code == 2)
            def _():
                visit_query(i, j, True)

            return 0

        lax.fori_loop(0, i + 1, one_key, 0)
        for p in range(PAIRS):
            x = dq_ref[p] * 0.125
            both = jnp.concatenate([x[:, :128], x[:, 128:]], axis=0)
            dqkv_ref[pl.ds(qoff, 128), 128 * p : 128 * p + 128] = both.T.astype(BF16)
        return 0

    lax.fori_loop(0, 2, one_query, 0)

    def visit_key(i, j, near):
        dd = jnp.minimum(i - j, 2) if near else None
        ok = seg_ok(segc_ref, segr_ref, i, j) if near else None
        for p in range(PAIRS):
            w, ds, qd, dd_ = grads(i, j, p, near, dd, ok)
            dv_ref[p] += mm(w.astype(BF16), dd_, 1, 1)
            dk_ref[p] += mm(ds.astype(BF16), qd, 1, 1)

    def one_own(kj, _):
        j = me * 2 + kj
        koff = pl.multiple_of(kj * 128, 128)
        dk_ref[...] = jnp.zeros_like(dk_ref)
        dv_ref[...] = jnp.zeros_like(dv_ref)

        def one_block(i, _):
            code = code_ref[i, j]

            @pl.when(code == 1)
            def _():
                visit_key(i, j, False)

            @pl.when(code == 2)
            def _():
                visit_key(i, j, True)

            return 0

        lax.fori_loop(j, code_ref.shape[0], one_block, 0)
        for p in range(PAIRS):
            at = D + 128 * p
            dqkv_ref[pl.ds(koff, 128), at : at + 128] = dk_ref[p].astype(BF16)
            dqkv_ref[pl.ds(koff, 128), D + at : D + at + 128] = dv_ref[p].astype(BF16)
        return 0

    lax.fori_loop(0, 2, one_own, 0)

    for h in range(HEADS):
        x = near_ref[h, :, 0:256]
        g = x[0:8]
        for a in range(1, 16):
            g = g + pltpu.roll(x[8 * a : 8 * a + 8], 256 - 8 * a, 1)
        total = g[0:1]
        for b in range(1, 8):
            total = total + pltpu.roll(g, 256 - b, 1)[b : b + 1]
        dgap_ref[h : h + 1, :] = total
        half = 128 * (h % 2)
        far = jnp.sum(facc_ref[h // 2, :, half : half + 128], axis=0, keepdims=True)
        far = far + jnp.sum(near_ref[h, :, 256:384], axis=0, keepdims=True)
        dfar_ref[h : h + 1, :] = far


def vmem():
    return pl.BlockSpec(memory_space=pltpu.VMEM)


def smem():
    return pl.BlockSpec(memory_space=pltpu.SMEM)


def attention_forward(code, me, qt, keys, vt, gap, far, segc, segr):
    length = keys.shape[0]
    return pl.pallas_call(
        fwd_kernel,
        name="attention_forward",
        out_shape=[
            jax.ShapeDtypeStruct((D, ROWS), F32),
            jax.ShapeDtypeStruct((ROWS, D), BF16),
            jax.ShapeDtypeStruct((HEADS, ROWS), F32),
        ],
        in_specs=[smem(), smem()] + [vmem()] * 7,
        out_specs=[vmem()] * 3,
        scratch_shapes=[
            pltpu.VMEM((HEADS, 128, 384), F32),
            pltpu.VMEM((8, 256), F32),
            pltpu.VMEM((8, 256), F32),
            pltpu.VMEM((PAIRS, 64, 256), F32),
        ],
        compiler_params=pltpu.CompilerParams(vmem_limit_bytes=VMEM_LIMIT),
        cost_estimate=pl.CostEstimate(
            flops=8 * ROWS * length * D,
            bytes_accessed=4 * length * D,
            transcendentals=HEADS * ROWS * length // 2,
        ),
    )(code, me, qt, keys, vt, gap, far, segc, segr)


def attention_backward(code, me, qt, dt, keys, kt, values, lse, delta, gap, far, segc, segr):
    length = keys.shape[0]
    return pl.pallas_call(
        bwd_kernel,
        name="attention_backward",
        out_shape=[
            jax.ShapeDtypeStruct((ROWS, 3 * D), BF16),
            jax.ShapeDtypeStruct((HEADS, 256), F32),
            jax.ShapeDtypeStruct((HEADS, 128), F32),
        ],
        in_specs=[smem(), smem()] + [vmem()] * 11,
        out_specs=[vmem()] * 3,
        scratch_shapes=[
            pltpu.VMEM((HEADS, 128, 384), F32),
            pltpu.VMEM((HEADS, 128, 384), F32),
            pltpu.VMEM((PAIRS, 8, 256), F32),
            pltpu.VMEM((PAIRS, 64, 256), F32),
            pltpu.VMEM((PAIRS, 128, 128), F32),
            pltpu.VMEM((PAIRS, 128, 128), F32),
        ],
        compiler_params=pltpu.CompilerParams(vmem_limit_bytes=VMEM_LIMIT),
        cost_estimate=pl.CostEstimate(
            flops=14 * ROWS * length * D,
            bytes_accessed=10 * length * D,
            transcendentals=HEADS * ROWS * length,
        ),
    )(code, me, qt, dt, keys, kt, values, lse, delta, gap, far, segc, segr)


def block_codes(seg_all, blocks):
    count = blocks.shape[0]
    rows = seg_all.reshape(count, BLK)
    least, most = jnp.min(rows, axis=1), jnp.max(rows, axis=1)
    ids = jnp.arange(count, dtype=jnp.int32)
    gap = ids[:, None] - ids[None, :]
    meet = (most[None, :] >= least[:, None]) & (least[None, :] <= most[:, None])
    live = (gap >= 0) & (blocks == 1) & meet
    same = (
        (least == most)[:, None] & (least == most)[None, :] & (least[:, None] == least[None, :])
    )
    return jnp.where(live, jnp.where(same & (gap >= 2), 1, 2), 0).astype(jnp.int32)


def bias_inputs(table):
    gap = jnp.dot(table, gap_hot().T, precision=PRECISE)
    far = jnp.repeat(table[:, 31].reshape(PAIRS, 2), BLK, axis=1)
    return gap, far


def bias_back(dgap, dfar):
    near = jnp.dot(dgap, gap_hot(), precision=PRECISE)
    last = (jnp.arange(32) == 31).astype(F32)[None, :]
    return near + jnp.sum(dfar, axis=1, keepdims=True) * last


def body(
    tokens, segments, block_sets, routes, qkv_weight, out_weight, ffn_in, ffn_out,
    norm_gains, rel_bias, router, expert_in, expert_out, cotangent,
):
    gather = partial(lax.all_gather, axis_name="grp", axis=0, tiled=True)
    rows = tokens.shape[1]
    me = lax.axis_index("grp").astype(jnp.int32).reshape(1)
    seg_all = gather(segments[0])
    code = block_codes(seg_all, block_sets[0])
    segc = seg_all[:, None]
    segr = seg_all.reshape(-1, BLK)
    shared = (segc, segr)

    x_all = gather(tokens[0])
    w_qkv = [gather(qkv_weight[:, 0].reshape(-1, 3 * D)), None]
    w_out = [gather(out_weight[:, 0]), None]
    full_in, full_down = gather(ffn_in), gather(ffn_out)
    w_qkv[1] = gather(qkv_weight[:, 1].reshape(-1, 3 * D))
    w_out[1] = gather(out_weight[:, 1])

    def attend(residual, normed, normed_all, layer):
        w = w_qkv[layer]
        qt = mm(w[:, :D], normed, 0, 1).astype(BF16) * jnp.asarray(0.125, BF16)
        keys = mm(normed_all, w[:, D : 2 * D], 1, 0).astype(BF16)
        vt = mm(w[:, 2 * D :], normed_all, 0, 1).astype(BF16)
        gap, far = bias_inputs(rel_bias[layer])
        ctxt, ctxb, lse = attention_forward(code, me, qt, keys, vt, gap, far, *shared)
        branch = mm(ctxb, w_out[layer], 1, 0)
        lse_all = lax.all_gather(lse, "grp", axis=0)
        return residual + branch, (residual, normed, normed_all, keys, ctxt, ctxb, lse_all, gap, far)

    def attend_back(grad_out, saved, layer):
        residual, normed, normed_all, keys, ctxt, ctxb, lse_all, gap, far = saved
        w, wo = w_qkv[layer], w_out[layer]
        grad_low = grad_out.astype(BF16)
        grad_all = gather(grad_low)
        dctx_own = mm(wo, grad_low, 1, 1).astype(BF16)
        delta = jnp.sum((dctx_own.astype(F32) * ctxt).reshape(HEADS, HEAD, rows), axis=1)
        delta_all = lax.all_gather(delta, "grp", axis=0)
        qt_all = mm(w[:, :D], normed_all, 0, 1).astype(BF16) * jnp.asarray(0.125, BF16)
        kt = mm(w[:, D : 2 * D], normed_all, 0, 1).astype(BF16)
        values = mm(normed_all, w[:, 2 * D :], 1, 0).astype(BF16)
        dt_all = mm(wo, grad_all, 1, 1).astype(BF16)
        dqkv, dgap, dfar = attention_backward(
            code, me, qt_all, dt_all, keys, kt, values, lse_all, delta_all, gap, far, *shared
        )
        out_part = mm(ctxb, grad_low, 0, 0)
        qkv_part = mm(normed, dqkv, 0, 0)
        normed_grad = mm(dqkv, w, 1, 1)
        _, pull_back = jax.vjp(norm_rows, residual, norm_gains[layer, 0])
        residual_grad, gain_grad = pull_back(normed_grad)
        return grad_out + residual_grad, qkv_part, out_part, gain_grad, bias_back(dgap, dfar)

    stream = tokens[0].astype(F32)
    own_a = norm_rows(stream, norm_gains[0, 0]).astype(BF16)
    all_a = norm_rows(x_all.astype(F32), norm_gains[0, 0]).astype(BF16)
    first_out, saved_a = attend(stream, own_a, all_a, 0)
    normed_ffn = norm_rows(first_out, norm_gains[0, 1]).astype(BF16)
    pre_ffn = mm(normed_ffn, full_in, 1, 0)
    hidden_ffn = jax.nn.gelu(pre_ffn).astype(BF16)
    after_ffn = first_out + mm(hidden_ffn, full_down, 1, 1)

    own_b = norm_rows(after_ffn, norm_gains[1, 0]).astype(BF16)
    second_out, saved_b = attend(after_ffn, own_b, gather(own_b), 1)
    normed_moe = norm_rows(second_out, norm_gains[1, 1]).astype(BF16)
    normed_wide = normed_moe.astype(F32)
    router_wide = router.astype(F32)
    logits = jnp.dot(normed_wide, router_wide, precision=PRECISE)

    experts_all = router.shape[1]
    groups = lax.axis_size("grp")
    per_group = experts_all // groups
    capacity = rows * 2 * 10 // (7 * experts_all) + 1
    slots = (capacity + 16) // 16 * 16
    chosen = routes[0]
    ids = jnp.arange(experts_all, dtype=jnp.int32)
    chosen_hot = (chosen[:, :, None] == ids[None, None, :]).astype(F32)
    flat_hot = chosen_hot.reshape(2 * rows, experts_all)
    before = jnp.tril(jnp.ones((2 * rows, 2 * rows), BF16), -1)
    earlier = mm(before, flat_hot.astype(BF16), 1, 0)
    slot_ids = jnp.sum(earlier * flat_hot, axis=1).astype(jnp.int32)
    place = (chosen.reshape(-1) * slots + slot_ids).reshape(rows, 2)
    lanes = jnp.arange(experts_all * slots, dtype=jnp.int32)
    pick = [(place[:, k][:, None] == lanes[None, :]).astype(BF16) for k in range(2)]
    both = pick[0] + pick[1]

    def exchange(x):
        return lax.all_to_all(
            x.reshape(groups, per_group * slots, D), "grp", split_axis=0, concat_axis=0, tiled=True
        )

    grad_final = cotangent[0].astype(F32)
    selected = jnp.sum(logits[:, None, :] * chosen_hot, axis=-1)
    gate_probs = jax.nn.softmax(selected, axis=-1)
    received = exchange(mm(both, normed_moe, 0, 0).astype(BF16))
    made = [(gate_probs[:, k : k + 1] * grad_final).astype(BF16) for k in range(2)]
    send_grad = (mm(pick[0], made[0], 0, 0) + mm(pick[1], made[1], 0, 0)).astype(BF16)
    recv_grad = exchange(send_grad)

    def by_expert(x):
        return x.reshape(groups, per_group, slots, -1).swapaxes(0, 1).reshape(per_group, groups * slots, -1)

    def by_source(x):
        return x.reshape(per_group, groups, slots, -1).swapaxes(0, 1).reshape(groups, per_group * slots, -1)

    def each(a, b, ca, cb):
        return lax.dot_general(a, b, (((ca,), (cb,)), ((0,), (0,))), preferred_element_type=F32)

    rows_e, dye = by_expert(received), by_expert(recv_grad)
    pre_expert = each(rows_e, expert_in, 2, 1)
    hidden_expert, gelu_expert = jax.vjp(jax.nn.gelu, pre_expert)
    hidden_expert = hidden_expert.astype(BF16)
    made_rows = each(hidden_expert, expert_out, 2, 1).astype(BF16)
    returned = exchange(by_source(made_rows)).reshape(experts_all * slots, D)
    hidden_grad = each(dye, expert_out, 2, 2)
    pre_grad = gelu_expert(hidden_grad)[0].astype(BF16)
    rows_grad = each(pre_grad, expert_in, 2, 2).astype(BF16)
    back_grad = exchange(by_source(rows_grad)).reshape(experts_all * slots, D)
    picked = [mm(pick[k], returned, 1, 0) for k in range(2)]
    final_out = second_out + gate_probs[:, 0:1] * picked[0] + gate_probs[:, 1:2] * picked[1]
    gate_grad = jnp.stack([jnp.sum(grad_final * picked[k], axis=-1) for k in range(2)], axis=-1)
    select_grad = gate_probs * (gate_grad - jnp.sum(gate_probs * gate_grad, axis=-1, keepdims=True))
    logit_grad = jnp.sum(select_grad[:, :, None] * chosen_hot, axis=1)
    router_part = jnp.dot(normed_wide.T, logit_grad, precision=PRECISE)
    normed_moe_grad = jnp.dot(logit_grad, router_wide.T, precision=PRECISE) + mm(both, back_grad, 1, 0)
    _, pull_moe = jax.vjp(norm_rows, second_out, norm_gains[1, 1])
    moe_resid_grad, moe_gain_grad = pull_moe(normed_moe_grad)
    grad_second = grad_final + moe_resid_grad

    expert_out_part = each(hidden_expert, dye, 1, 1)
    expert_in_part = each(rows_e, pre_grad, 1, 1)

    grad_ffn, qkv_part_b, out_part_b, gain_grad_b, table_grad_b = attend_back(grad_second, saved_b, 1)
    down_low = grad_ffn.astype(BF16)
    down_part = mm(down_low, hidden_ffn, 0, 0)
    hidden_ffn_grad = mm(down_low, full_down, 1, 0)
    _, gelu_dense = jax.vjp(jax.nn.gelu, pre_ffn)
    pre_ffn_grad = gelu_dense(hidden_ffn_grad)[0].astype(BF16)
    in_part = mm(normed_ffn, pre_ffn_grad, 0, 0)
    normed_ffn_grad = mm(pre_ffn_grad, full_in, 1, 1)
    _, pull_ffn = jax.vjp(norm_rows, first_out, norm_gains[0, 1])
    ffn_resid_grad, ffn_gain_grad = pull_ffn(normed_ffn_grad)
    grad_first = grad_ffn + ffn_resid_grad
    grad_tokens, qkv_part_a, out_part_a, gain_grad_a, table_grad_a = attend_back(grad_first, saved_a, 0)

    def scatter(x):
        return lax.psum_scatter(x.astype(BF16), "grp", scatter_dimension=0, tiled=True)

    def total(x):
        return lax.psum(x.astype(BF16), "rep").astype(F32)

    qkv_sum = jnp.stack([total(scatter(x)) for x in (qkv_part_a, qkv_part_b)], axis=1)
    qkv_sum = qkv_sum.reshape(qkv_weight.shape)
    out_sum = jnp.stack([total(scatter(x)) for x in (out_part_a, out_part_b)], axis=1)
    in_sum, down_sum = total(scatter(in_part)), total(scatter(down_part))
    expert_in_sum, expert_out_sum = total(expert_in_part), total(expert_out_part)
    gain_all = jnp.stack(
        [jnp.stack([gain_grad_a, ffn_gain_grad]), jnp.stack([gain_grad_b, moe_gain_grad])]
    )
    table_all = jnp.stack([table_grad_a, table_grad_b])
    gain_sum, table_sum, router_sum = lax.psum((gain_all, table_all, router_part), ("rep", "grp"))
    return (
        final_out[None], grad_tokens[None], qkv_sum, out_sum, in_sum, down_sum,
        gain_sum, table_sum, router_sum, expert_in_sum, expert_out_sum,
    )


def solution(mesh):
    return jax.shard_map(
        body,
        mesh=mesh,
        in_specs=(
            P("rep", "grp", None),
            P("rep", "grp"),
            P("rep", None, None),
            P("rep", "grp", None),
            P("grp", None, None, None),
            P("grp", None, None),
            P("grp", None),
            P("grp", None),
            P(),
            P(),
            P(),
            P("grp", None, None),
            P("grp", None, None),
            P("rep", "grp", None),
        ),
        out_specs=(
            P("rep", "grp", None),
            P("rep", "grp", None),
            P("grp", None, None, None),
            P("grp", None, None),
            P("grp", None),
            P("grp", None),
            P(),
            P(),
            P(),
            P("grp", None, None),
            P("grp", None, None),
        ),
        check_vma=False,
    )
```

```python
from functools import partial

import jax
import jax.numpy as jnp
from jax import lax
from jax.experimental import pallas as pl
from jax.experimental.pallas import tpu as pltpu
from jax.sharding import PartitionSpec as P

D = 768
HEADS = 12
HEAD = 64
PAIRS = 6
BLK = 128
ROWS = 256

BUCKET_EDGES = (18, 20, 23, 26, 30, 34, 39, 45, 51, 58, 66, 76, 86, 98, 112)
PRECISE = lax.Precision.HIGHEST
norm_eps = 1e-06
GELU_SCALE = 0.7978845608028654
GELU_CUBE = 0.044715
NEG = -1e30
VMEM_LIMIT = 60 * 1024 * 1024
F32 = jnp.float32
BF16 = jnp.bfloat16


def mm(a, b, ca, cb):
    return lax.dot_general(a, b, (((ca,), (cb,)), ((), ())), preferred_element_type=F32)


def norm_rows(residual, gain_vec):
    return (
        residual
        * lax.rsqrt(jnp.mean(residual * residual, axis=-1, keepdims=True) + norm_eps)
        * gain_vec
    )


def bucket_of(pos_gap):
    clipped = jnp.maximum(pos_gap, 0)
    bucket = jnp.minimum(clipped, 16)
    for edge_at in BUCKET_EDGES:
        bucket = bucket + (clipped >= edge_at).astype(jnp.int32)
    return bucket


def gap_hot():
    gaps = jnp.arange(2 * BLK, dtype=jnp.int32)
    return (bucket_of(gaps)[:, None] == jnp.arange(32, dtype=jnp.int32)[None, :]).astype(F32)


def pair_diag(ref, p, off):
    x = ref[128 * p : 128 * p + 128, pl.ds(off, 128)]
    z = jnp.zeros((64, 128), x.dtype)
    top = jnp.concatenate([x[:64], z], axis=0)
    low = jnp.concatenate([z, x[64:]], axis=0)
    return jnp.concatenate([top, low], axis=1)


def fill_tiles(gap_ref, far_ref, tile_ref):
    rows = lax.broadcasted_iota(jnp.int32, (128, 128), 0)
    cols = lax.broadcasted_iota(jnp.int32, (128, 128), 1)
    causal = cols >= rows
    for h in range(HEADS):
        x = jnp.broadcast_to(gap_ref[h : h + 1, :], (128, 256))
        r = pltpu.roll(x, 0, 1, stride=1, stride_axis=0)
        tile_ref[h, :, 0:128] = jnp.where(causal, r[:, :128], NEG)
        tile_ref[h, :, 128:256] = r[:, 128:]
        half = 128 * (h % 2)
        tile_ref[h, :, 256:384] = jnp.broadcast_to(
            far_ref[h // 2 : h // 2 + 1, half : half + 128], (128, 128)
        )
    tile_ref[:, :, 384:512] = jnp.full((HEADS, 128, 128), NEG, F32)


def tile_ids(code_ref, i, j):
    pick = [jnp.where(code_ref[i, j + n] == 0, 3, jnp.clip(i - j - n, 0, 2)) for n in range(2)]
    return [pl.multiple_of(t * 128, 128) for t in pick]


def pair_tiles(tile_ref, p, offs):
    cols = [
        jnp.concatenate([tile_ref[2 * p + h, :, pl.ds(off, 128)] for off in offs], axis=0)
        for h in range(2)
    ]
    return jnp.concatenate(cols, axis=1)


def seg_ok(segc_ref, segr_ref, i, j, count):
    kcol = segc_ref[pl.ds(pl.multiple_of(j * 128, 128), count), :]
    ok = kcol == segr_ref[pl.ds(i, 1), :]
    return jnp.concatenate([ok, ok], axis=1)


def split_visit(code_ref, i, j, visit):
    one, two = code_ref[i, j], code_ref[i, j + 1]
    near = (one == 2) | (two == 2)

    @pl.when(near)
    def _():
        visit(j, 2, True)

    @pl.when(jnp.logical_not(near) & (one + two == 2))
    def _():
        visit(j, 2, False)

    @pl.when(jnp.logical_not(near) & (one + two == 1))
    def _():
        visit(j + two, 1, False)


def fwd_kernel(
    code_ref, me_ref, qt_ref, k_ref, v_ref, gap_ref, far_ref, segc_ref, segr_ref,
    ctxt_ref, ctxb_ref, lse_ref, tile_ref, m_ref, l_ref, acc_ref,
):
    fill_tiles(gap_ref, far_ref, tile_ref)
    me = me_ref[0]

    def one_query(qi, _):
        i = me * 2 + qi
        qoff = pl.multiple_of(qi * 128, 128)
        m_ref[...] = jnp.full_like(m_ref, NEG)
        l_ref[...] = jnp.zeros_like(l_ref)
        acc_ref[...] = jnp.zeros_like(acc_ref)

        def visit(j, near):
            keys = pl.ds(pl.multiple_of(j * 128, 128), 128)
            if near:
                off = pl.multiple_of(jnp.minimum(i - j, 2) * 128, 128)
                ok = seg_ok(segc_ref, segr_ref, i, j, 128)
            for p in range(PAIRS):
                cols = slice(128 * p, 128 * p + 128)
                s = mm(k_ref[keys, cols], pair_diag(qt_ref, p, qoff), 1, 0)
                if near:
                    s = jnp.where(ok, s + pair_tiles(tile_ref, p, [off]), NEG)
                else:
                    s = s + far_ref[p : p + 1, :]
                m_old = m_ref[p : p + 1, :]
                m_new = jnp.maximum(m_old, jnp.max(s, axis=0, keepdims=True))
                w = jnp.exp(s - m_new)
                shrink = jnp.exp(m_old - m_new)
                m_ref[p : p + 1, :] = m_new
                l_ref[p : p + 1, :] = l_ref[p : p + 1, :] * shrink + jnp.sum(
                    w, axis=0, keepdims=True
                )
                o = mm(v_ref[keys, cols], w.astype(BF16), 0, 0)
                o = jnp.concatenate([o[:64, :128], o[64:, 128:]], axis=1)
                acc_ref[p] = acc_ref[p] * shrink + o

        visit(i, True)

        def one_key(j, _):
            code = code_ref[i, j]

            @pl.when(code == 1)
            def _():
                visit(j, False)

            @pl.when(code == 2)
            def _():
                visit(j, True)

            return 0

        lax.fori_loop(0, i, one_key, 0)
        for p in range(PAIRS):
            total = l_ref[p : p + 1, :]
            ctx = acc_ref[p] * (1.0 / total)
            both = jnp.concatenate([ctx[:, :128], ctx[:, 128:]], axis=0)
            ctxt_ref[128 * p : 128 * p + 128, pl.ds(qoff, 128)] = both
            ctxb_ref[pl.ds(qoff, 128), 128 * p : 128 * p + 128] = both.T.astype(BF16)
            lse = m_ref[p : p + 1, :] + jnp.log(total)
            lse_ref[2 * p : 2 * p + 1, pl.ds(qoff, 128)] = lse[:, :128]
            lse_ref[2 * p + 1 : 2 * p + 2, pl.ds(qoff, 128)] = lse[:, 128:]
        return 0

    lax.fori_loop(0, 2, one_query, 0)


def bwd_kernel(
    code_ref, me_ref, qt_ref, dt_ref, k_ref, v_ref, stat_ref, gap_ref, far_ref, segc_ref, segr_ref,
    dqkv_ref, dgap_ref, dfar_ref,
    tile_ref, near_ref, facc_ref, dq_ref, dk_ref, dv_ref,
):
    fill_tiles(gap_ref, far_ref, tile_ref)
    near_ref[...] = jnp.zeros_like(near_ref)
    facc_ref[...] = jnp.zeros_like(facc_ref)
    dq_ref[...] = jnp.zeros_like(dq_ref)
    dk_ref[...] = jnp.zeros_like(dk_ref)
    dv_ref[...] = jnp.zeros_like(dv_ref)
    me = me_ref[0]

    def lanes(first, p, i):
        g, at = i // 2, first + 2 * p
        off = pl.multiple_of((i % 2) * 128, 128)
        return jnp.concatenate(
            [stat_ref[g, at : at + 1, pl.ds(off, 128)], stat_ref[g, at + 1 : at + 2, pl.ds(off, 128)]],
            axis=1,
        )

    def visit(i, j, blocks, near, by_query, by_key):
        keys = pl.ds(pl.multiple_of(j * 128, 128), 128 * blocks)
        own = pl.ds(pl.multiple_of((j - 2 * me) * 128, 128), 128 * blocks)
        qoff = pl.multiple_of(i * 128, 128)
        if near:
            offs = tile_ids(code_ref, i, j)
            ok = seg_ok(segc_ref, segr_ref, i, j, 256)
        for p in range(PAIRS):
            cols = slice(128 * p, 128 * p + 128)
            qd, od = pair_diag(qt_ref, p, qoff), pair_diag(dt_ref, p, qoff)
            s = mm(k_ref[keys, cols], qd, 1, 0)
            lse = lanes(0, p, i)
            if near:
                w = jnp.exp(jnp.where(ok, s + pair_tiles(tile_ref, p, offs) - lse, NEG))
            else:
                w = jnp.exp(s + (far_ref[p : p + 1, :] - lse))
            dp = mm(v_ref[keys, cols], od, 1, 0)
            ds = w * (dp - lanes(HEADS, p, i))
            dsb = ds.astype(BF16)
            if by_key:
                dv_ref[p, own] += mm(w.astype(BF16), od, 1, 1)
                dk_ref[p, own] += mm(dsb, qd, 1, 1)
            if by_query:
                qi = i - 2 * me
                o = mm(k_ref[keys, cols], dsb, 0, 0)
                dq_ref[qi, p] += jnp.concatenate([o[:64, :128], o[64:, 128:]], axis=1)
                if near:
                    for n in range(2):
                        for h in range(2):
                            part = ds[128 * n : 128 * n + 128, 128 * h : 128 * h + 128]
                            near_ref[2 * p + h, :, pl.ds(offs[n], 128)] += part
                else:
                    part = ds[0:8]
                    for a in range(1, 16 * blocks):
                        part = part + ds[8 * a : 8 * a + 8]
                    facc_ref[p] += part

    def one_query(qi, _):
        i = me * 2 + qi
        visit(i, 2 * me, 2, True, True, True)

        def two_keys(t, _):
            split_visit(code_ref, i, 2 * t, lambda j, blocks, near: visit(i, j, blocks, near, True, False))
            return 0

        lax.fori_loop(0, me, two_keys, 0)
        for p in range(PAIRS):
            x = dq_ref[qi, p] * 0.125
            both = jnp.concatenate([x[:, :128], x[:, 128:]], axis=0)
            dqkv_ref[pl.ds(pl.multiple_of(qi * 128, 128), 128), 128 * p : 128 * p + 128] = both.T.astype(BF16)
        return 0

    lax.fori_loop(0, 2, one_query, 0)

    def later(i, _):
        split_visit(code_ref, i, 2 * me, lambda j, blocks, near: visit(i, j, blocks, near, False, True))
        return 0

    lax.fori_loop(2 * me + 2, code_ref.shape[0], later, 0)
    for p in range(PAIRS):
        at = D + 128 * p
        dqkv_ref[:, at : at + 128] = dk_ref[p].astype(BF16)
        dqkv_ref[:, D + at : D + at + 128] = dv_ref[p].astype(BF16)

    for h in range(HEADS):
        x = near_ref[h, :, 0:256]
        g = x[0:8]
        for a in range(1, 16):
            g = g + pltpu.roll(x[8 * a : 8 * a + 8], 256 - 8 * a, 1)
        total = g[0:1]
        for b in range(1, 8):
            total = total + pltpu.roll(g, 256 - b, 1)[b : b + 1]
        dgap_ref[h : h + 1, :] = total
        half = 128 * (h % 2)
        far = jnp.sum(facc_ref[h // 2, :, half : half + 128], axis=0, keepdims=True)
        far = far + jnp.sum(near_ref[h, :, 256:384], axis=0, keepdims=True)
        dfar_ref[h : h + 1, :] = far


def vmem():
    return pl.BlockSpec(memory_space=pltpu.VMEM)


def smem():
    return pl.BlockSpec(memory_space=pltpu.SMEM)


def attention_forward(code, me, qt, keys, values, gap, far, segc, segr):
    length = keys.shape[0]
    return pl.pallas_call(
        fwd_kernel,
        name="attention_forward",
        out_shape=[
            jax.ShapeDtypeStruct((D, ROWS), F32),
            jax.ShapeDtypeStruct((ROWS, D), BF16),
            jax.ShapeDtypeStruct((HEADS, ROWS), F32),
        ],
        in_specs=[smem(), smem()] + [vmem()] * 7,
        out_specs=[vmem()] * 3,
        scratch_shapes=[
            pltpu.VMEM((HEADS, 128, 512), F32),
            pltpu.VMEM((8, 256), F32),
            pltpu.VMEM((8, 256), F32),
            pltpu.VMEM((PAIRS, 64, 256), F32),
        ],
        compiler_params=pltpu.CompilerParams(vmem_limit_bytes=VMEM_LIMIT),
        cost_estimate=pl.CostEstimate(
            flops=8 * ROWS * length * D,
            bytes_accessed=32 * length * D,
            transcendentals=HEADS * ROWS * length // 2,
        ),
    )(code, me, qt, keys, values, gap, far, segc, segr)


def attention_backward(code, me, qt, dt, keys, values, stats, gap, far, segc, segr):
    length = keys.shape[0]
    return pl.pallas_call(
        bwd_kernel,
        name="attention_backward",
        out_shape=[
            jax.ShapeDtypeStruct((ROWS, 3 * D), BF16),
            jax.ShapeDtypeStruct((HEADS, 256), F32),
            jax.ShapeDtypeStruct((HEADS, 128), F32),
        ],
        in_specs=[smem(), smem()] + [vmem()] * 9,
        out_specs=[vmem()] * 3,
        scratch_shapes=[
            pltpu.VMEM((HEADS, 128, 512), F32),
            pltpu.VMEM((HEADS, 128, 512), F32),
            pltpu.VMEM((PAIRS, 8, 256), F32),
            pltpu.VMEM((2, PAIRS, 64, 256), F32),
            pltpu.VMEM((PAIRS, 256, 128), F32),
            pltpu.VMEM((PAIRS, 256, 128), F32),
        ],
        compiler_params=pltpu.CompilerParams(vmem_limit_bytes=VMEM_LIMIT),
        cost_estimate=pl.CostEstimate(
            flops=14 * ROWS * length * D,
            bytes_accessed=64 * length * D,
            transcendentals=HEADS * ROWS * length,
        ),
    )(code, me, qt, dt, keys, values, stats, gap, far, segc, segr)


def ffn_kernel(x_ref, gain_ref, own_ref, peer_ref, other_ref, out_ref, norm_ref, hidden_ref, slope_ref):
    x = x_ref[...]
    normed = norm_rows(x, gain_ref[...]).astype(BF16)
    norm_ref[...] = normed
    total = x
    piece = own_ref.shape[2] // 2
    peers = peer_ref.shape[0]
    weights = [own_ref.at[0], own_ref.at[1]]
    for k in range(peers):
        weights += [peer_ref.at[k], other_ref.at[k]]
    for n, ref in enumerate(weights):
        at = slice(n * piece, n * piece + piece)
        hidden, slope = gelu_pair(mm(normed, ref[:, :piece], 1, 0))
        hidden = hidden.astype(BF16)
        hidden_ref[:, at] = hidden
        slope_ref[:, at] = slope
        total = total + mm(hidden, ref[:, piece:], 1, 1)
    out_ref[...] = total


def ffn_forward(x, gain, own, peers, others):
    count = x.shape[0]
    width = own.shape[2] // 2 * (2 + 2 * peers.shape[0])
    return pl.pallas_call(
        ffn_kernel,
        name="ffn_forward",
        in_specs=[vmem()] * 5,
        out_specs=[vmem()] * 4,
        out_shape=[
            jax.ShapeDtypeStruct((count, D), F32),
            jax.ShapeDtypeStruct((count, D), BF16),
            jax.ShapeDtypeStruct((count, width), BF16),
            jax.ShapeDtypeStruct((count, width), F32),
        ],
        compiler_params=pltpu.CompilerParams(vmem_limit_bytes=VMEM_LIMIT),
        cost_estimate=pl.CostEstimate(
            flops=4 * count * D * width, bytes_accessed=8 * D * width, transcendentals=count * width
        ),
    )(x, gain[None, :], own, peers, others)


def gelu_pair(u):
    t = jnp.tanh(GELU_SCALE * (u + GELU_CUBE * u * u * u))
    half = 0.5 * (1.0 + t)
    slope = half + 0.5 * u * (1.0 - t * t) * (GELU_SCALE * (1.0 + 3.0 * GELU_CUBE * u * u))
    return u * half, slope


def expert_rows_kernel(rows_ref, dye_ref, cot_ref, win_ref, wout_ref, made_ref, back_ref, gate_ref, made_acc, back_acc):
    step = pl.program_id(1)

    @pl.when(step == 0)
    def _():
        made_acc[...] = jnp.zeros_like(made_acc)
        back_acc[...] = jnp.zeros_like(back_acc)

    win, wout = win_ref[0], wout_ref[0]
    half = rows_ref.shape[1] // 2
    for c in range(2):
        at = slice(half * c, half * c + half)
        hidden, slope = gelu_pair(mm(rows_ref[0, at], win, 1, 0))
        made_acc[at] += mm(hidden.astype(BF16), wout, 1, 0)
        pre_back = (mm(dye_ref[0, at], wout, 1, 1) * slope).astype(BF16)
        back_acc[at] += mm(pre_back, win, 1, 1)

    @pl.when(step == pl.num_programs(1) - 1)
    def _():
        made = made_acc[...].astype(BF16)
        made_ref[0] = made
        back_ref[0] = back_acc[...]
        gate = jnp.sum(cot_ref[0].astype(F32) * made.astype(F32), axis=1, keepdims=True)
        gate_ref[0] = jnp.broadcast_to(gate, gate_ref.shape[1:])


def expert_rows(rows, dye, cot, w_in, w_out):
    count, total, _ = rows.shape
    width, block = w_in.shape[2], 512
    whole = pl.BlockSpec((1, total, D), lambda e, i: (e, 0, 0))
    return pl.pallas_call(
        expert_rows_kernel,
        name="expert_rows",
        grid=(count, width // block),
        in_specs=[
            whole,
            whole,
            whole,
            pl.BlockSpec((1, D, block), lambda e, i: (e, 0, i)),
            pl.BlockSpec((1, block, D), lambda e, i: (e, i, 0)),
        ],
        out_specs=[whole, whole, pl.BlockSpec((1, total, 128), lambda e, i: (e, 0, 0))],
        out_shape=[
            jax.ShapeDtypeStruct(rows.shape, BF16),
            jax.ShapeDtypeStruct(rows.shape, F32),
            jax.ShapeDtypeStruct((count, total, 128), F32),
        ],
        scratch_shapes=[pltpu.VMEM((total, D), F32), pltpu.VMEM((total, D), F32)],
        compiler_params=pltpu.CompilerParams(vmem_limit_bytes=VMEM_LIMIT),
        cost_estimate=pl.CostEstimate(
            flops=8 * count * total * D * width,
            bytes_accessed=16 * count * D * width,
            transcendentals=count * total * width,
        ),
    )(rows, dye, cot, w_in, w_out)


def expert_kernel(rows_ref, dye_ref, win_ref, wout_ref, *rest):
    in_ref, out_ref = rest[-2:]
    total = rows_ref.shape[1]
    step = total // 3
    win, wout = win_ref[0], wout_ref[0]
    for c in range(3):
        rows = rows_ref[0, step * c : step * c + step]
        dye = dye_ref[0, step * c : step * c + step]
        hidden, slope = gelu_pair(mm(rows, win, 1, 0))
        pre_back = (mm(dye, wout, 1, 1) * slope).astype(BF16)
        grad_in = mm(rows, pre_back, 0, 0)
        grad_out = mm(hidden.astype(BF16), dye, 0, 0)
        if c == 0:
            in_ref[0], out_ref[0] = grad_in, grad_out
        else:
            in_ref[0] += grad_in
            out_ref[0] += grad_out


def expert_gradients(rows, dye, w_in, w_out, part, earlier):
    count, total, _ = rows.shape
    width, block = w_in.shape[2], 512
    steps = width // block // 2
    whole = pl.BlockSpec((1, total, D), lambda e, i: (e, 0, 0))
    by_in = pl.BlockSpec((1, D, block), lambda e, i: (e, 0, i + part * steps))
    by_out = pl.BlockSpec((1, block, D), lambda e, i: (e, i + part * steps, 0))
    return pl.pallas_call(
        expert_kernel,
        name=f"expert_gradients_{part}",
        grid=(count, steps),
        in_specs=[whole, whole, by_in, by_out] + [pl.BlockSpec(memory_space=pl.ANY)] * len(earlier),
        out_specs=[by_in, by_out],
        out_shape=[
            jax.ShapeDtypeStruct(w_in.shape, F32),
            jax.ShapeDtypeStruct(w_out.shape, F32),
        ],
        input_output_aliases={4 + n: n for n in range(len(earlier))},
        compiler_params=pltpu.CompilerParams(vmem_limit_bytes=VMEM_LIMIT),
        cost_estimate=pl.CostEstimate(
            flops=4 * count * total * D * width,
            bytes_accessed=32 * count * D * width,
            transcendentals=count * total * width // 2,
        ),
    )(rows, dye, w_in, w_out, *earlier)


def three_parts(x):
    parts = []
    for _ in range(3):
        parts.append(lax.reduce_precision(x, 8, 7))
        x = x - parts[-1]
    return parts


def block_codes(seg_all, blocks):
    count = blocks.shape[0]
    rows = seg_all.reshape(count, BLK)
    least, most = jnp.min(rows, axis=1), jnp.max(rows, axis=1)
    ids = jnp.arange(count, dtype=jnp.int32)
    gap = ids[:, None] - ids[None, :]
    meet = (most[None, :] >= least[:, None]) & (least[None, :] <= most[:, None])
    live = (gap >= 0) & (blocks == 1) & meet
    same = (
        (least == most)[:, None] & (least == most)[None, :] & (least[:, None] == least[None, :])
    )
    return jnp.where(live, jnp.where(same & (gap >= 2), 1, 2), 0).astype(jnp.int32)


def bias_inputs(table):
    gap = jnp.dot(table, gap_hot().T, precision=PRECISE)
    far = jnp.repeat(table[:, 31].reshape(PAIRS, 2), BLK, axis=1)
    return gap, far


def bias_back(dgap, dfar):
    near = jnp.dot(dgap, gap_hot(), precision=PRECISE)
    last = (jnp.arange(32) == 31).astype(F32)[None, :]
    return near + jnp.sum(dfar, axis=1, keepdims=True) * last


def body(
    tokens, segments, block_sets, routes, qkv_weight, out_weight, ffn_in, ffn_out,
    norm_gains, rel_bias, router, expert_in, expert_out, cotangent,
):
    gather = partial(lax.all_gather, axis_name="grp", axis=0, tiled=True)
    rows = tokens.shape[1]
    me = lax.axis_index("grp").astype(jnp.int32).reshape(1)
    replicas, groups = lax.axis_size("rep"), lax.axis_size("grp")
    mine, core = lax.axis_index("rep"), lax.axis_index("grp") % 2

    def from_replica(x, k):
        return lax.ppermute(x, "rep", [(i, i ^ k) for i in range(replicas)])

    def from_sibling(x):
        return lax.ppermute(x, "grp", [(i, i ^ 1) for i in range(groups)])

    def swapped_cores(got):
        other = from_sibling(jnp.stack(got))
        return [other[k] for k in range(replicas - 1)]

    def layer_quarter(layer, after):
        count = qkv_weight.shape[0] // replicas
        part_qkv = lax.dynamic_slice(
            qkv_weight, (mine * count, layer, 0, 0), (count, 1) + qkv_weight.shape[2:]
        )
        part_out = lax.dynamic_slice(out_weight, (mine * count, layer, 0), (count, 1, D))
        part = jnp.concatenate([part_qkv.reshape(count, 3 * D), part_out.reshape(count, D)], axis=1)
        if after is not None:
            part, _ = lax.optimization_barrier((part, after))
        return lax.all_gather(part, "grp", axis=0)

    def layer_weights(quarter):
        width = quarter.shape[2] // 2
        half = lax.dynamic_slice_in_dim(quarter, core * width, width, 2)
        got = [from_replica(half, k) for k in range(1, replicas)]
        other = swapped_cores(got)
        full = jnp.zeros((groups, replicas) + quarter.shape[1:], BF16)
        full = lax.dynamic_update_slice(full, quarter[:, None], (0, mine, 0, 0))
        for k in range(1, replicas):
            for part, which in ((got[k - 1], core), (other[k - 1], 1 - core)):
                full = lax.dynamic_update_slice(full, part[:, None], (0, mine ^ k, 0, which * width))
        full = full.reshape(-1, 2 * width)
        return full[:, : 3 * D], full[:, 3 * D :]

    quarter_first = layer_quarter(0, None)
    w_first = layer_weights(quarter_first)

    span = ffn_in.shape[1] // replicas
    piece = span // 2
    ffn_own = [lax.dynamic_slice_in_dim(w, mine * span, span, 1) for w in (ffn_in, ffn_out)]
    ffn_own = jnp.concatenate([w[:, h * piece : h * piece + piece] for h in range(2) for w in ffn_own], axis=1)
    ffn_own, quarter_first = lax.optimization_barrier((ffn_own, quarter_first))
    ffn_quarter = gather(ffn_own)
    seg_row = jnp.pad(segments.astype(BF16), ((0, 7), (0, D - rows)))
    tokens_own = jnp.concatenate([tokens[0], seg_row], axis=0)
    tokens_own, ffn_quarter = lax.optimization_barrier((tokens_own, ffn_quarter))
    tokens_all = lax.all_gather(tokens_own, "grp", axis=0)
    ffn_mine = [lax.dynamic_slice_in_dim(ffn_quarter, n * span, span, 1) for n in (core, 1 - core)]
    ffn_peers = [from_replica(ffn_mine[0], k) for k in range(1, replicas)]

    quarter_second = layer_quarter(1, tokens_all)
    x_all = tokens_all[:, :rows].reshape(-1, D)
    seg_all = tokens_all[:, rows, :rows].astype(jnp.int32).reshape(-1)
    code = block_codes(seg_all, block_sets[0])
    shared = (seg_all[:, None], seg_all.reshape(-1, BLK))
    w_qkv, w_out = [w_first[0]], [w_first[1]]

    def attend(residual, normed, normed_all, layer):
        w = w_qkv[layer]
        qt = mm(w[:, :D], normed, 0, 1).astype(BF16) * jnp.asarray(0.125, BF16)
        keys = mm(normed_all, w[:, D : 2 * D], 1, 0).astype(BF16)
        values = mm(normed_all, w[:, 2 * D :], 1, 0).astype(BF16)
        gap, far = bias_inputs(rel_bias[layer])
        ctxt, ctxb, lse = attention_forward(code, me, qt, keys, values, gap, far, *shared)
        branch = mm(ctxb, w_out[layer], 1, 0)
        saved = (residual, normed, normed_all, keys, values, ctxt, ctxb, lse, gap, far)
        return residual + branch, saved

    def attend_back(grad_out, saved, layer, qt_all, held, cover):
        residual, normed, normed_all, keys, values, ctxt, ctxb, lse, gap, far = saved
        w, wo = w_qkv[layer], w_out[layer]
        grad_low = grad_out.astype(BF16)
        dctx_own = mm(wo, grad_low, 1, 1).astype(BF16)
        delta = jnp.sum((dctx_own.astype(F32) * ctxt).reshape(HEADS, HEAD, rows), axis=1)
        stats = jnp.stack(three_parts(jnp.concatenate([lse, delta], axis=0)), axis=1)
        stats = stats.reshape(2 * HEADS, 3 * rows).astype(BF16)
        sent = jnp.concatenate([grad_low, stats, jnp.zeros((8, D), BF16)], axis=0)
        got, covered = lax.optimization_barrier((lax.all_gather(sent, "grp", axis=0), cover(sent)))
        grad_all = got[:, :rows].reshape(-1, D)
        stats_all = got[:, rows : rows + 2 * HEADS].reshape(-1, 2 * HEADS, 3, rows)
        stats_all = jnp.sum(stats_all.astype(F32), axis=2)
        dt_all = mm(wo, grad_all, 1, 1).astype(BF16)
        dt_all, held = lax.optimization_barrier((dt_all, held))
        dqkv, dgap, dfar = attention_backward(
            code, me, qt_all, dt_all, keys, values, stats_all, gap, far, *shared
        )
        out_part = mm(ctxb, grad_low, 0, 0)
        qkv_part = mm(normed, dqkv, 0, 0)
        normed_grad = mm(dqkv, w, 1, 1)
        _, pull_back = jax.vjp(norm_rows, residual, norm_gains[layer, 0])
        residual_grad, gain_grad = pull_back(normed_grad)
        table_grad = bias_back(dgap, dfar)
        return grad_out + residual_grad, qkv_part, out_part, gain_grad, table_grad, grad_all, held, covered

    experts_all = router.shape[1]
    per_group = experts_all // groups
    capacity = rows * 2 * 10 // (7 * experts_all) + 1
    slots = (capacity + 16) // 16 * 16
    chosen = routes[0]
    ids = jnp.arange(experts_all, dtype=jnp.int32)
    chosen_hot = (chosen[:, :, None] == ids[None, None, :]).astype(F32)
    flat_hot = chosen_hot.reshape(2 * rows, experts_all)
    before = jnp.tril(jnp.ones((2 * rows, 2 * rows), BF16), -1)
    earlier = mm(before, flat_hot.astype(BF16), 1, 0)
    slot_ids = jnp.sum(earlier * flat_hot, axis=1).astype(jnp.int32)
    place = (chosen.reshape(-1) * slots + slot_ids).reshape(rows, 2)
    lanes = jnp.arange(experts_all * slots, dtype=jnp.int32)
    pick = [(place[:, k][:, None] == lanes[None, :]).astype(BF16) for k in range(2)]
    both = pick[0] + pick[1]

    def exchange(x):
        return lax.all_to_all(
            x.reshape(groups, per_group * slots, D), "grp", split_axis=0, concat_axis=0, tiled=True
        )

    def by_expert(x):
        return x.reshape(groups, per_group, slots, -1).swapaxes(0, 1).reshape(per_group, groups * slots, -1)

    def by_source(x):
        return x.reshape(per_group, groups, slots, -1).swapaxes(0, 1).reshape(groups, per_group * slots, -1)

    def all_replicas(x):
        return lax.all_gather(x, "rep", axis=1, tiled=True)

    stream = tokens[0].astype(F32)
    own_a = norm_rows(stream, norm_gains[0, 0]).astype(BF16)
    all_a = norm_rows(x_all.astype(F32), norm_gains[0, 0]).astype(BF16)
    first_out, saved_a = attend(stream, own_a, all_a, 0)
    first_out, quarter_second, ffn_peers = lax.optimization_barrier(
        (first_out, quarter_second, ffn_peers)
    )
    ffn_peers = jnp.stack(ffn_peers)
    ffn_others = from_sibling(ffn_peers)
    after_ffn, normed_ffn, hidden_ffn, slope_ffn = ffn_forward(
        first_out, norm_gains[0, 1], jnp.stack(ffn_mine), ffn_peers, ffn_others
    )

    w_second = layer_weights(quarter_second)
    w_qkv.append(w_second[0])
    w_out.append(w_second[1])
    own_b = norm_rows(after_ffn, norm_gains[1, 0]).astype(BF16)
    pieces = ffn_mine + [x[k] for k in range(replicas - 1) for x in (ffn_peers, ffn_others)]
    full_in = jnp.concatenate([x[:, :piece] for x in pieces], axis=1)
    full_down = jnp.concatenate([x[:, piece:] for x in pieces], axis=1)
    all_b, cot_own, full_in, full_down = lax.optimization_barrier(
        (gather(own_b), cotangent[0], full_in, full_down)
    )
    cot_rows = by_expert(exchange(mm(both, cot_own, 0, 0).astype(BF16)))
    second_out, saved_b = attend(after_ffn, own_b, all_b, 1)
    second_out, cot_rows = lax.optimization_barrier((second_out, cot_rows))
    cot_all = all_replicas(cot_rows)
    normed_moe = norm_rows(second_out, norm_gains[1, 1]).astype(BF16)
    normed_wide = normed_moe.astype(F32)
    router_wide = router.astype(F32)
    logits = jnp.dot(normed_wide, router_wide, precision=PRECISE)

    last_row = (jnp.arange(slots) == slots - 1)[None, :, None]

    def with_scalars(rows_in, values):
        parts = [jnp.pad(part, ((0, 0), (0, 128 - slots))) for part in three_parts(values)]
        info = jnp.concatenate(parts + [jnp.zeros((values.shape[0], D - 384), F32)], axis=1)
        return jnp.where(last_row, info[:, None, :], rows_in).astype(BF16)

    def scalars_of(rows_in):
        info = rows_in[:, slots - 1, :].astype(F32)
        total = info[:, 0:slots] + info[:, 128 : 128 + slots] + info[:, 256 : 256 + slots]
        return jnp.where(jnp.arange(slots)[None, :] == slots - 1, 0.0, total)

    grad_final = cotangent[0].astype(F32)
    selected = jnp.sum(logits[:, None, :] * chosen_hot, axis=-1)
    gate_probs = jax.nn.softmax(selected, axis=-1)
    gate_slots = jnp.sum(
        jnp.where(pick[0] == 1, gate_probs[:, 0:1], 0.0) + jnp.where(pick[1] == 1, gate_probs[:, 1:2], 0.0),
        axis=0,
    ).reshape(experts_all, slots)
    sent = mm(both, normed_moe, 0, 0).reshape(experts_all, slots, D)
    rows_e = by_expert(exchange(with_scalars(sent, gate_slots)))

    def gated(rows_in, cot):
        gates = scalars_of(rows_in.reshape(-1, slots, D)).reshape(per_group, -1, 1)
        return (gates * cot.astype(F32)).astype(BF16)

    dye = gated(rows_e, cot_rows)
    made_rows, rows_grad, gate_back = expert_rows(rows_e, dye, cot_rows, expert_in, expert_out)
    rows_grad = rows_grad.reshape(per_group * groups, slots, D)
    rows_grad = with_scalars(rows_grad, gate_back[:, :, 0].reshape(-1, slots))
    queries_all = [
        mm(w_qkv[n][:, :D], all_rows, 0, 1).astype(BF16) * jnp.asarray(0.125, BF16)
        for n, all_rows in enumerate((all_a, all_b))
    ]
    back_grad, rows_all, cot_all, queries_all = lax.optimization_barrier(
        (exchange(by_source(rows_grad)), all_replicas(rows_e), cot_all, queries_all)
    )
    back_slots = scalars_of(back_grad.reshape(experts_all, slots, D)).reshape(1, -1)
    back_grad = back_grad.reshape(experts_all * slots, D)
    gate_grad = jnp.stack(
        [jnp.sum(jnp.where(pick[k] == 1, back_slots, 0.0), axis=1) for k in range(2)], axis=-1
    )
    select_grad = gate_probs * (gate_grad - jnp.sum(gate_probs * gate_grad, axis=-1, keepdims=True))
    logit_grad = jnp.sum(select_grad[:, :, None] * chosen_hot, axis=1)
    normed_moe_grad = jnp.dot(logit_grad, router_wide.T, precision=PRECISE) + mm(both, back_grad, 1, 0)
    _, pull_moe = jax.vjp(norm_rows, second_out, norm_gains[1, 1])
    moe_resid_grad, moe_gain_grad = pull_moe(normed_moe_grad)
    grad_second = grad_final + moe_resid_grad
    router_part = jnp.dot(normed_wide.T, logit_grad, precision=PRECISE)

    def finish(made):
        returned = exchange(by_source(made)).reshape(experts_all * slots, D)
        picked = [mm(pick[k], returned, 1, 0) for k in range(2)]
        return second_out + gate_probs[:, 0:1] * picked[0] + gate_probs[:, 1:2] * picked[1]

    dye_all = gated(rows_all, cot_all)

    def expert_half(part, earlier):
        def run(sent):
            rows_in, _ = lax.optimization_barrier((rows_all, sent))
            return tuple(expert_gradients(rows_in, dye_all, expert_in, expert_out, part, earlier))

        return run

    back_b = attend_back(grad_second, saved_b, 1, queries_all[1], made_rows, expert_half(0, ()))
    grad_ffn, qkv_part_b, out_part_b, gain_grad_b, table_grad_b, _, made_held, expert_sums = back_b
    final_out = finish(made_held)
    grad_ffn, final_out = lax.optimization_barrier((grad_ffn, final_out))
    down_low = grad_ffn.astype(BF16)
    down_part = mm(down_low, hidden_ffn, 0, 0)
    hidden_ffn_grad = mm(down_low, full_down, 1, 0)
    pre_ffn_grad = (hidden_ffn_grad * slope_ffn).astype(BF16)
    in_part = mm(normed_ffn, pre_ffn_grad, 0, 0)
    normed_ffn_grad = mm(pre_ffn_grad, full_in, 1, 1)
    _, pull_ffn = jax.vjp(norm_rows, first_out, norm_gains[0, 1])
    ffn_resid_grad, ffn_gain_grad = pull_ffn(normed_ffn_grad)
    grad_first = grad_ffn + ffn_resid_grad
    def packed(parts):
        return jnp.concatenate([part.astype(BF16) for part in parts], axis=1)

    def halves(k, which):
        at = k * span + which * piece
        return packed([x[:, at : at + piece] for x in (down_part, in_part)])

    theirs = from_sibling(jnp.stack([halves(k, 1) for k in range(replicas)]))
    ffn_parts = [
        (halves(k, 0).astype(F32) + theirs[k].astype(F32)).astype(BF16) for k in range(replicas)
    ]
    ffn_got = [from_replica(ffn_parts[k], k) for k in range(1, replicas)]
    back_a = attend_back(grad_first, saved_a, 0, queries_all[0], (), expert_half(1, expert_sums))
    grad_tokens, qkv_part_a, out_part_a, gain_grad_a, table_grad_a, grad_all_a, _, expert_sums = back_a
    expert_in_sum, expert_out_sum = expert_sums
    parts_b, _ = lax.optimization_barrier((packed([qkv_part_b, out_part_b]), grad_all_a))
    parts_a = packed([qkv_part_a, out_part_a])
    shard_b = lax.psum_scatter(parts_b, "grp", scatter_dimension=0, tiled=True)
    parts_a, shard_b, ffn_got = lax.optimization_barrier((parts_a, shard_b, ffn_got))

    def scatter(x):
        return lax.psum_scatter(x, "grp", scatter_dimension=0, tiled=True)

    def over_replicas(x, cut):
        half = x.shape[0] // 2

        def add(v, mask):
            return (v.astype(F32) + from_replica(v, mask).astype(F32)).astype(BF16)

        first = [1 << b for b in range(replicas.bit_length() - 1)]
        top, low = x[:half], x[half:]
        for a, b in zip(first, first[::-1]):
            top, low = add(top, a), add(low, b)
        x = jnp.concatenate([top, low], axis=0).astype(F32)
        return x[:, :cut], x[:, cut:]

    shard_a = lax.psum_scatter(parts_a, "grp", scatter_dimension=0, tiled=True)
    ffn_total = ffn_parts[0].astype(F32)
    for x in ffn_got:
        ffn_total = ffn_total + x.astype(F32)
    down_half, in_half = ffn_total[:, :piece], ffn_total[:, piece:]
    ffn_total = jnp.concatenate(
        [jnp.where(core == h, x, 0.0) for x in (in_half, down_half) for h in range(2)], axis=1
    )
    shard_a, ffn_total = lax.optimization_barrier((shard_a, ffn_total.astype(BF16)))
    ffn_shard = scatter(ffn_total)
    ffn_sums = jnp.stack([ffn_shard] + [from_replica(ffn_shard, k) for k in range(1, replicas)])
    ffn_sums = [lax.dynamic_index_in_dim(ffn_sums, mine ^ q, 0, False).astype(F32) for q in range(replicas)]
    in_sum = jnp.concatenate([x[:, :span] for x in ffn_sums], axis=1)
    down_sum = jnp.concatenate([x[:, span:] for x in ffn_sums], axis=1)
    qkv_b, out_b = over_replicas(shard_b, 3 * D)
    qkv_a, out_a = over_replicas(shard_a, 3 * D)
    qkv_sum = jnp.stack([qkv_a, qkv_b], axis=1).reshape(qkv_weight.shape)
    out_sum = jnp.stack([out_a, out_b], axis=1)
    gain_all = jnp.stack(
        [jnp.stack([gain_grad_a, ffn_gain_grad]), jnp.stack([gain_grad_b, moe_gain_grad])]
    )
    table_all = jnp.stack([table_grad_a, table_grad_b])
    small = [gain_all, table_all, router_part]
    flat = jnp.concatenate([x.reshape(-1, BLK) for x in small], axis=0)
    for axis, count in (("rep", replicas), ("grp", groups)):
        for bit in range(count.bit_length() - 1):
            flat = flat + lax.ppermute(flat, axis, [(i, i ^ (1 << bit)) for i in range(count)])
    sizes = [x.size // BLK for x in small]
    cut = [flat[sum(sizes[:n]) : sum(sizes[: n + 1])].reshape(x.shape) for n, x in enumerate(small)]
    gain_sum, table_sum, router_sum = cut
    return (
        final_out[None], grad_tokens[None], qkv_sum, out_sum, in_sum, down_sum,
        gain_sum, table_sum, router_sum, expert_in_sum, expert_out_sum,
    )


def solution(mesh):
    return jax.shard_map(
        body,
        mesh=mesh,
        in_specs=(
            P("rep", "grp", None),
            P("rep", "grp"),
            P("rep", None, None),
            P("rep", "grp", None),
            P("grp", None, None, None),
            P("grp", None, None),
            P("grp", None),
            P("grp", None),
            P(),
            P(),
            P(),
            P("grp", None, None),
            P("grp", None, None),
            P("rep", "grp", None),
        ),
        out_specs=(
            P("rep", "grp", None),
            P("rep", "grp", None),
            P("grp", None, None, None),
            P("grp", None, None),
            P("grp", None),
            P("grp", None),
            P(),
            P(),
            P(),
            P("grp", None, None),
            P("grp", None, None),
        ),
        check_vma=False,
    )
```

```python
from functools import partial

import jax
import jax.numpy as jnp
from jax import lax
from jax.experimental import pallas as pl
from jax.experimental.pallas import tpu as pltpu
from jax.sharding import PartitionSpec as P

D = 768
HEADS = 12
HEAD = 64
PAIRS = 6
BLK = 128
ROWS = 256

BUCKET_EDGES = (18, 20, 23, 26, 30, 34, 39, 45, 51, 58, 66, 76, 86, 98, 112)
PRECISE = lax.Precision.HIGHEST
norm_eps = 1e-06
GELU_SCALE = 0.7978845608028654
GELU_CUBE = 0.044715
NEG = -1e30
VMEM_LIMIT = 60 * 1024 * 1024
F32 = jnp.float32
BF16 = jnp.bfloat16


def mm(a, b, ca, cb):
    return lax.dot_general(a, b, (((ca,), (cb,)), ((), ())), preferred_element_type=F32)


def norm_rows(residual, gain_vec):
    return (
        residual
        * lax.rsqrt(jnp.mean(residual * residual, axis=-1, keepdims=True) + norm_eps)
        * gain_vec
    )


def bucket_of(pos_gap):
    clipped = jnp.maximum(pos_gap, 0)
    bucket = jnp.minimum(clipped, 16)
    for edge_at in BUCKET_EDGES:
        bucket = bucket + (clipped >= edge_at).astype(jnp.int32)
    return bucket


def gap_hot():
    gaps = jnp.arange(2 * BLK, dtype=jnp.int32)
    return (bucket_of(gaps)[:, None] == jnp.arange(32, dtype=jnp.int32)[None, :]).astype(F32)


def pair_diag(ref, p, off):
    x = ref[128 * p : 128 * p + 128, pl.ds(off, 128)]
    z = jnp.zeros((64, 128), x.dtype)
    top = jnp.concatenate([x[:64], z], axis=0)
    low = jnp.concatenate([z, x[64:]], axis=0)
    return jnp.concatenate([top, low], axis=1)


def fill_tiles(gap_ref, far_ref, tile_ref):
    rows = lax.broadcasted_iota(jnp.int32, (128, 128), 0)
    cols = lax.broadcasted_iota(jnp.int32, (128, 128), 1)
    causal = cols >= rows
    for h in range(HEADS):
        x = jnp.broadcast_to(gap_ref[h : h + 1, :], (128, 256))
        r = pltpu.roll(x, 0, 1, stride=1, stride_axis=0)
        tile_ref[h, :, 0:128] = jnp.where(causal, r[:, :128], NEG)
        tile_ref[h, :, 128:256] = r[:, 128:]
        half = 128 * (h % 2)
        tile_ref[h, :, 256:384] = jnp.broadcast_to(
            far_ref[h // 2 : h // 2 + 1, half : half + 128], (128, 128)
        )
    tile_ref[:, :, 384:512] = jnp.full((HEADS, 128, 128), NEG, F32)


def tile_ids(code_ref, i, j):
    pick = [jnp.where(code_ref[i, j + n] == 0, 3, jnp.clip(i - j - n, 0, 2)) for n in range(2)]
    return [pl.multiple_of(t * 128, 128) for t in pick]


def pair_tiles(tile_ref, p, offs):
    cols = [
        jnp.concatenate([tile_ref[2 * p + h, :, pl.ds(off, 128)] for off in offs], axis=0)
        for h in range(2)
    ]
    return jnp.concatenate(cols, axis=1)


def seg_ok(segc_ref, segr_ref, i, j, count):
    kcol = segc_ref[pl.ds(pl.multiple_of(j * 128, 128), count), :]
    ok = kcol == segr_ref[pl.ds(i, 1), :]
    return jnp.concatenate([ok, ok], axis=1)


def split_visit(code_ref, i, j, visit):
    one, two = code_ref[i, j], code_ref[i, j + 1]
    near = (one == 2) | (two == 2)

    @pl.when(near)
    def _():
        visit(j, 2, True)

    @pl.when(jnp.logical_not(near) & (one + two == 2))
    def _():
        visit(j, 2, False)

    @pl.when(jnp.logical_not(near) & (one + two == 1))
    def _():
        visit(j + two, 1, False)


def fwd_kernel(
    code_ref, me_ref, qt_ref, kv_ref, gap_ref, far_ref, segc_ref, segr_ref,
    ctxt_ref, ctxb_ref, lse_ref, tile_ref, m_ref, l_ref, acc_ref,
):
    fill_tiles(gap_ref, far_ref, tile_ref)
    me = me_ref[0]

    def one_query(qi, _):
        i = me * 2 + qi
        qoff = pl.multiple_of(qi * 128, 128)
        m_ref[...] = jnp.full_like(m_ref, NEG)
        l_ref[...] = jnp.zeros_like(l_ref)
        acc_ref[...] = jnp.zeros_like(acc_ref)

        def visit(j, near):
            keys = pl.ds(pl.multiple_of(j * 128, 128), 128)
            if near:
                off = pl.multiple_of(jnp.minimum(i - j, 2) * 128, 128)
                ok = seg_ok(segc_ref, segr_ref, i, j, 128)
            for p in range(PAIRS):
                cols = slice(128 * p, 128 * p + 128)
                vcols = slice(D + 128 * p, D + 128 * p + 128)
                s = mm(kv_ref[keys, cols], pair_diag(qt_ref, p, qoff), 1, 0)
                if near:
                    s = jnp.where(ok, s + pair_tiles(tile_ref, p, [off]), NEG)
                else:
                    s = s + far_ref[p : p + 1, :]
                m_old = m_ref[p : p + 1, :]
                m_new = jnp.maximum(m_old, jnp.max(s, axis=0, keepdims=True))
                w = jnp.exp(s - m_new)
                shrink = jnp.exp(m_old - m_new)
                m_ref[p : p + 1, :] = m_new
                l_ref[p : p + 1, :] = l_ref[p : p + 1, :] * shrink + jnp.sum(
                    w, axis=0, keepdims=True
                )
                o = mm(kv_ref[keys, vcols], w.astype(BF16), 0, 0)
                o = jnp.concatenate([o[:64, :128], o[64:, 128:]], axis=1)
                acc_ref[p] = acc_ref[p] * shrink + o

        visit(i, True)

        def one_key(j, _):
            code = code_ref[i, j]

            @pl.when(code == 1)
            def _():
                visit(j, False)

            @pl.when(code == 2)
            def _():
                visit(j, True)

            return 0

        lax.fori_loop(0, i, one_key, 0)
        for p in range(PAIRS):
            total = l_ref[p : p + 1, :]
            ctx = acc_ref[p] * (1.0 / total)
            both = jnp.concatenate([ctx[:, :128], ctx[:, 128:]], axis=0)
            ctxt_ref[128 * p : 128 * p + 128, pl.ds(qoff, 128)] = both
            ctxb_ref[pl.ds(qoff, 128), 128 * p : 128 * p + 128] = both.T.astype(BF16)
            lse = m_ref[p : p + 1, :] + jnp.log(total)
            lse_ref[2 * p : 2 * p + 1, pl.ds(qoff, 128)] = lse[:, :128]
            lse_ref[2 * p + 1 : 2 * p + 2, pl.ds(qoff, 128)] = lse[:, 128:]
        return 0

    lax.fori_loop(0, 2, one_query, 0)


def bwd_kernel(
    code_ref, me_ref, qt_ref, dt_ref, kv_ref, stat_ref, gap_ref, far_ref, segc_ref, segr_ref,
    dqkv_ref, dgap_ref, dfar_ref,
    tile_ref, near_ref, facc_ref, dq_ref, dk_ref, dv_ref,
):
    fill_tiles(gap_ref, far_ref, tile_ref)
    near_ref[...] = jnp.zeros_like(near_ref)
    facc_ref[...] = jnp.zeros_like(facc_ref)
    dq_ref[...] = jnp.zeros_like(dq_ref)
    dk_ref[...] = jnp.zeros_like(dk_ref)
    dv_ref[...] = jnp.zeros_like(dv_ref)
    me = me_ref[0]

    def lanes(first, p, i):
        g, at = i // 2, first + 2 * p
        off = pl.multiple_of((i % 2) * 128, 128)
        return jnp.concatenate(
            [stat_ref[g, at : at + 1, pl.ds(off, 128)], stat_ref[g, at + 1 : at + 2, pl.ds(off, 128)]],
            axis=1,
        )

    def visit(i, j, blocks, near, by_query, by_key):
        keys = pl.ds(pl.multiple_of(j * 128, 128), 128 * blocks)
        own = pl.ds(pl.multiple_of((j - 2 * me) * 128, 128), 128 * blocks)
        qoff = pl.multiple_of(i * 128, 128)
        if near:
            offs = tile_ids(code_ref, i, j)
            ok = seg_ok(segc_ref, segr_ref, i, j, 256)
        for p in range(PAIRS):
            cols = slice(128 * p, 128 * p + 128)
            vcols = slice(D + 128 * p, D + 128 * p + 128)
            qd, od = pair_diag(qt_ref, p, qoff), pair_diag(dt_ref, p, qoff)
            s = mm(kv_ref[keys, cols], qd, 1, 0)
            lse = lanes(0, p, i)
            if near:
                w = jnp.exp(jnp.where(ok, s + pair_tiles(tile_ref, p, offs) - lse, NEG))
            else:
                w = jnp.exp(s + (far_ref[p : p + 1, :] - lse))
            dp = mm(kv_ref[keys, vcols], od, 1, 0)
            ds = w * (dp - lanes(HEADS, p, i))
            dsb = ds.astype(BF16)
            if by_key:
                dv_ref[p, own] += mm(w.astype(BF16), od, 1, 1)
                dk_ref[p, own] += mm(dsb, qd, 1, 1)
            if by_query:
                qi = i - 2 * me
                o = mm(kv_ref[keys, cols], dsb, 0, 0)
                dq_ref[qi, p] += jnp.concatenate([o[:64, :128], o[64:, 128:]], axis=1)
                if near:
                    for n in range(2):
                        for h in range(2):
                            part = ds[128 * n : 128 * n + 128, 128 * h : 128 * h + 128]
                            near_ref[2 * p + h, :, pl.ds(offs[n], 128)] += part
                else:
                    part = ds[0:8]
                    for a in range(1, 16 * blocks):
                        part = part + ds[8 * a : 8 * a + 8]
                    facc_ref[p] += part

    def one_query(qi, _):
        i = me * 2 + qi
        visit(i, 2 * me, 2, True, True, True)

        def two_keys(t, _):
            split_visit(code_ref, i, 2 * t, lambda j, blocks, near: visit(i, j, blocks, near, True, False))
            return 0

        lax.fori_loop(0, me, two_keys, 0)
        for p in range(PAIRS):
            x = dq_ref[qi, p] * 0.125
            both = jnp.concatenate([x[:, :128], x[:, 128:]], axis=0)
            dqkv_ref[pl.ds(pl.multiple_of(qi * 128, 128), 128), 128 * p : 128 * p + 128] = both.T.astype(BF16)
        return 0

    lax.fori_loop(0, 2, one_query, 0)

    def later(i, _):
        split_visit(code_ref, i, 2 * me, lambda j, blocks, near: visit(i, j, blocks, near, False, True))
        return 0

    lax.fori_loop(2 * me + 2, code_ref.shape[0], later, 0)
    for p in range(PAIRS):
        at = D + 128 * p
        dqkv_ref[:, at : at + 128] = dk_ref[p].astype(BF16)
        dqkv_ref[:, D + at : D + at + 128] = dv_ref[p].astype(BF16)

    for h in range(HEADS):
        x = near_ref[h, :, 0:256]
        g = x[0:8]
        for a in range(1, 16):
            g = g + pltpu.roll(x[8 * a : 8 * a + 8], 256 - 8 * a, 1)
        total = g[0:1]
        for b in range(1, 8):
            total = total + pltpu.roll(g, 256 - b, 1)[b : b + 1]
        dgap_ref[h : h + 1, :] = total
        half = 128 * (h % 2)
        far = jnp.sum(facc_ref[h // 2, :, half : half + 128], axis=0, keepdims=True)
        far = far + jnp.sum(near_ref[h, :, 256:384], axis=0, keepdims=True)
        dfar_ref[h : h + 1, :] = far


def vmem():
    return pl.BlockSpec(memory_space=pltpu.VMEM)


def smem():
    return pl.BlockSpec(memory_space=pltpu.SMEM)


def attention_forward(code, me, qt, kv, gap, far, segc, segr):
    length = kv.shape[0]
    return pl.pallas_call(
        fwd_kernel,
        name="attention_forward",
        out_shape=[
            jax.ShapeDtypeStruct((D, ROWS), F32),
            jax.ShapeDtypeStruct((ROWS, D), BF16),
            jax.ShapeDtypeStruct((HEADS, ROWS), F32),
        ],
        in_specs=[smem(), smem()] + [vmem()] * 6,
        out_specs=[vmem()] * 3,
        scratch_shapes=[
            pltpu.VMEM((HEADS, 128, 512), F32),
            pltpu.VMEM((8, 256), F32),
            pltpu.VMEM((8, 256), F32),
            pltpu.VMEM((PAIRS, 64, 256), F32),
        ],
        compiler_params=pltpu.CompilerParams(vmem_limit_bytes=VMEM_LIMIT),
        cost_estimate=pl.CostEstimate(
            flops=8 * ROWS * length * D,
            bytes_accessed=32 * length * D,
            transcendentals=HEADS * ROWS * length // 2,
        ),
    )(code, me, qt, kv, gap, far, segc, segr)


def attention_backward(code, me, qt, dt, kv, stats, gap, far, segc, segr):
    length = kv.shape[0]
    return pl.pallas_call(
        bwd_kernel,
        name="attention_backward",
        out_shape=[
            jax.ShapeDtypeStruct((ROWS, 3 * D), BF16),
            jax.ShapeDtypeStruct((HEADS, 256), F32),
            jax.ShapeDtypeStruct((HEADS, 128), F32),
        ],
        in_specs=[smem(), smem()] + [vmem()] * 8,
        out_specs=[vmem()] * 3,
        scratch_shapes=[
            pltpu.VMEM((HEADS, 128, 512), F32),
            pltpu.VMEM((HEADS, 128, 512), F32),
            pltpu.VMEM((PAIRS, 8, 256), F32),
            pltpu.VMEM((2, PAIRS, 64, 256), F32),
            pltpu.VMEM((PAIRS, 256, 128), F32),
            pltpu.VMEM((PAIRS, 256, 128), F32),
        ],
        compiler_params=pltpu.CompilerParams(vmem_limit_bytes=VMEM_LIMIT),
        cost_estimate=pl.CostEstimate(
            flops=14 * ROWS * length * D,
            bytes_accessed=64 * length * D,
            transcendentals=HEADS * ROWS * length,
        ),
    )(code, me, qt, dt, kv, stats, gap, far, segc, segr)


def ffn_kernel(x_ref, gain_ref, *refs):
    weights, (out_ref, norm_ref, hidden_ref, slope_ref) = refs[:-4], refs[-4:]
    x = x_ref[...]
    normed = norm_rows(x, gain_ref[...]).astype(BF16)
    norm_ref[...] = normed
    total = x
    piece = weights[0].shape[1] // 2
    for n, ref in enumerate(weights):
        at = slice(n * piece, n * piece + piece)
        hidden, slope = gelu_pair(mm(normed, ref[:, :piece], 1, 0))
        hidden = hidden.astype(BF16)
        hidden_ref[:, at] = hidden
        slope_ref[:, at] = slope
        total = total + mm(hidden, ref[:, piece:], 1, 1)
    out_ref[...] = total


def ffn_forward(x, gain, pieces):
    count = x.shape[0]
    width = sum(w.shape[1] // 2 for w in pieces)
    return pl.pallas_call(
        ffn_kernel,
        name="ffn_forward",
        in_specs=[vmem()] * (2 + len(pieces)),
        out_specs=[vmem()] * 4,
        out_shape=[
            jax.ShapeDtypeStruct((count, D), F32),
            jax.ShapeDtypeStruct((count, D), BF16),
            jax.ShapeDtypeStruct((count, width), BF16),
            jax.ShapeDtypeStruct((count, width), F32),
        ],
        compiler_params=pltpu.CompilerParams(vmem_limit_bytes=VMEM_LIMIT),
        cost_estimate=pl.CostEstimate(
            flops=4 * count * D * width, bytes_accessed=8 * D * width, transcendentals=count * width
        ),
    )(x, gain[None, :], *pieces)


def gelu_pair(u):
    t = jnp.tanh(GELU_SCALE * (u + GELU_CUBE * u * u * u))
    half = 0.5 * (1.0 + t)
    slope = half + 0.5 * u * (1.0 - t * t) * (GELU_SCALE * (1.0 + 3.0 * GELU_CUBE * u * u))
    return u * half, slope


def expert_rows_kernel(rows_ref, dye_ref, cot_ref, win_ref, wout_ref, made_ref, back_ref, gate_ref, made_acc, back_acc):
    step = pl.program_id(1)

    @pl.when(step == 0)
    def _():
        made_acc[...] = jnp.zeros_like(made_acc)
        back_acc[...] = jnp.zeros_like(back_acc)

    win, wout = win_ref[0], wout_ref[0]
    half = rows_ref.shape[1] // 2
    for c in range(2):
        at = slice(half * c, half * c + half)
        hidden, slope = gelu_pair(mm(rows_ref[0, at], win, 1, 0))
        made_acc[at] += mm(hidden.astype(BF16), wout, 1, 0)
        pre_back = (mm(dye_ref[0, at], wout, 1, 1) * slope).astype(BF16)
        back_acc[at] += mm(pre_back, win, 1, 1)

    @pl.when(step == pl.num_programs(1) - 1)
    def _():
        made = made_acc[...].astype(BF16)
        made_ref[0] = made
        back_ref[0] = back_acc[...]
        gate = jnp.sum(cot_ref[0].astype(F32) * made.astype(F32), axis=1, keepdims=True)
        gate_ref[0] = jnp.broadcast_to(gate, gate_ref.shape[1:])


def expert_rows(rows, dye, cot, w_in, w_out):
    count, total, _ = rows.shape
    width, block = w_in.shape[2], 512
    whole = pl.BlockSpec((1, total, D), lambda e, i: (e, 0, 0))
    return pl.pallas_call(
        expert_rows_kernel,
        name="expert_rows",
        grid=(count, width // block),
        in_specs=[
            whole,
            whole,
            whole,
            pl.BlockSpec((1, D, block), lambda e, i: (e, 0, i)),
            pl.BlockSpec((1, block, D), lambda e, i: (e, i, 0)),
        ],
        out_specs=[whole, whole, pl.BlockSpec((1, total, 128), lambda e, i: (e, 0, 0))],
        out_shape=[
            jax.ShapeDtypeStruct(rows.shape, BF16),
            jax.ShapeDtypeStruct(rows.shape, F32),
            jax.ShapeDtypeStruct((count, total, 128), F32),
        ],
        scratch_shapes=[pltpu.VMEM((total, D), F32), pltpu.VMEM((total, D), F32)],
        compiler_params=pltpu.CompilerParams(vmem_limit_bytes=VMEM_LIMIT),
        cost_estimate=pl.CostEstimate(
            flops=8 * count * total * D * width,
            bytes_accessed=16 * count * D * width,
            transcendentals=count * total * width,
        ),
    )(rows, dye, cot, w_in, w_out)


def expert_kernel(rows_ref, dye_ref, win_ref, wout_ref, *rest):
    in_ref, out_ref = rest[-2:]
    total = rows_ref.shape[1]
    step = total // 3
    win, wout = win_ref[0], wout_ref[0]
    for c in range(3):
        rows = rows_ref[0, step * c : step * c + step]
        dye = dye_ref[0, step * c : step * c + step]
        hidden, slope = gelu_pair(mm(rows, win, 1, 0))
        pre_back = (mm(dye, wout, 1, 1) * slope).astype(BF16)
        grad_in = mm(rows, pre_back, 0, 0)
        grad_out = mm(hidden.astype(BF16), dye, 0, 0)
        if c == 0:
            in_ref[0], out_ref[0] = grad_in, grad_out
        else:
            in_ref[0] += grad_in
            out_ref[0] += grad_out


def expert_gradients(rows, dye, w_in, w_out, part, earlier):
    count, total, _ = rows.shape
    width, block = w_in.shape[2], 512
    blocks = width // block
    edges = (0, blocks // 2, blocks - blocks // 6, blocks)
    first, steps = edges[part], edges[part + 1] - edges[part]
    whole = pl.BlockSpec((1, total, D), lambda e, i: (e, 0, 0))
    by_in = pl.BlockSpec((1, D, block), lambda e, i: (e, 0, i + first))
    by_out = pl.BlockSpec((1, block, D), lambda e, i: (e, i + first, 0))
    return pl.pallas_call(
        expert_kernel,
        name=f"expert_gradients_{part}",
        grid=(count, steps),
        in_specs=[whole, whole, by_in, by_out] + [pl.BlockSpec(memory_space=pl.ANY)] * len(earlier),
        out_specs=[by_in, by_out],
        out_shape=[
            jax.ShapeDtypeStruct(w_in.shape, F32),
            jax.ShapeDtypeStruct(w_out.shape, F32),
        ],
        input_output_aliases={4 + n: n for n in range(len(earlier))},
        compiler_params=pltpu.CompilerParams(vmem_limit_bytes=VMEM_LIMIT),
        cost_estimate=pl.CostEstimate(
            flops=8 * count * total * D * block * steps,
            bytes_accessed=64 * count * D * block * steps,
            transcendentals=count * total * block * steps,
        ),
    )(rows, dye, w_in, w_out, *earlier)


def three_parts(x):
    parts = []
    for _ in range(3):
        parts.append(lax.reduce_precision(x, 8, 7))
        x = x - parts[-1]
    return parts


def block_codes(seg_all, blocks):
    count = blocks.shape[0]
    rows = seg_all.reshape(count, BLK)
    least, most = jnp.min(rows, axis=1), jnp.max(rows, axis=1)
    ids = jnp.arange(count, dtype=jnp.int32)
    gap = ids[:, None] - ids[None, :]
    meet = (most[None, :] >= least[:, None]) & (least[None, :] <= most[:, None])
    live = (gap >= 0) & (blocks == 1) & meet
    same = (
        (least == most)[:, None] & (least == most)[None, :] & (least[:, None] == least[None, :])
    )
    return jnp.where(live, jnp.where(same & (gap >= 2), 1, 2), 0).astype(jnp.int32)


def bias_inputs(table):
    gap = jnp.dot(table, gap_hot().T, precision=PRECISE)
    far = jnp.repeat(table[:, 31].reshape(PAIRS, 2), BLK, axis=1)
    return gap, far


def bias_back(dgap, dfar):
    near = jnp.dot(dgap, gap_hot(), precision=PRECISE)
    last = (jnp.arange(32) == 31).astype(F32)[None, :]
    return near + jnp.sum(dfar, axis=1, keepdims=True) * last


def body(
    tokens, segments, block_sets, routes, qkv_weight, out_weight, ffn_in, ffn_out,
    norm_gains, rel_bias, router, expert_in, expert_out, cotangent,
):
    gather = partial(lax.all_gather, axis_name="grp", axis=0, tiled=True)
    rows = tokens.shape[1]
    me = lax.axis_index("grp").astype(jnp.int32).reshape(1)
    replicas, groups = lax.axis_size("rep"), lax.axis_size("grp")
    mine, core = lax.axis_index("rep"), lax.axis_index("grp") % 2

    def from_replica(x, k):
        return lax.ppermute(x, "rep", [(i, i ^ k) for i in range(replicas)])

    def from_sibling(x):
        return lax.ppermute(x, "grp", [(i, i ^ 1) for i in range(groups)])

    def swapped_cores(got):
        other = from_sibling(jnp.stack(got))
        return [other[k] for k in range(replicas - 1)]

    def layer_quarter(layer, after):
        count = qkv_weight.shape[0] // replicas
        part_qkv = lax.dynamic_slice(
            qkv_weight, (mine * count, layer, 0, 0), (count, 1) + qkv_weight.shape[2:]
        )
        part_out = lax.dynamic_slice(out_weight, (mine * count, layer, 0), (count, 1, D))
        part = jnp.concatenate([part_qkv.reshape(count, 3 * D), part_out.reshape(count, D)], axis=1)
        if after is not None:
            part, _ = lax.optimization_barrier((part, after))
        return lax.all_gather(part, "grp", axis=0)

    def layer_weights(quarter):
        width = quarter.shape[2] // 2
        half = lax.dynamic_slice_in_dim(quarter, core * width, width, 2)
        got = [from_replica(half, k) for k in range(1, replicas)]
        other = swapped_cores(got)
        full = jnp.zeros((groups, replicas) + quarter.shape[1:], BF16)
        full = lax.dynamic_update_slice(full, quarter[:, None], (0, mine, 0, 0))
        for k in range(1, replicas):
            for part, which in ((got[k - 1], core), (other[k - 1], 1 - core)):
                full = lax.dynamic_update_slice(full, part[:, None], (0, mine ^ k, 0, which * width))
        full = full.reshape(-1, 2 * width)
        return full[:, : 3 * D], full[:, 3 * D :]

    quarter_first = layer_quarter(0, None)
    w_first = layer_weights(quarter_first)

    span = ffn_in.shape[1] // replicas
    piece = span // 2
    ffn_own = [lax.dynamic_slice_in_dim(w, mine * span, span, 1) for w in (ffn_in, ffn_out)]
    ffn_own = jnp.concatenate([w[:, h * piece : h * piece + piece] for h in range(2) for w in ffn_own], axis=1)
    seg_row = jnp.pad(segments.astype(BF16), ((0, 7), (0, ffn_own.shape[1] - rows)))
    ffn_own = jnp.concatenate([ffn_own, seg_row], axis=0)
    ffn_own, quarter_first = lax.optimization_barrier((ffn_own, quarter_first))
    ffn_quarter = lax.all_gather(ffn_own, "grp", axis=0)
    seg_all = ffn_quarter[:, ffn_in.shape[0], :rows].astype(jnp.int32).reshape(-1)
    tokens_own, ffn_quarter = lax.optimization_barrier((tokens[0], ffn_quarter))
    x_all = gather(tokens_own)
    ffn_mine = [
        lax.dynamic_slice(ffn_quarter, (0, 0, n * span), (groups, ffn_in.shape[0], span)).reshape(-1, span)
        for n in (core, 1 - core)
    ]
    ffn_peers = [from_replica(ffn_mine[0], k) for k in range(1, replicas)]

    quarter_second = layer_quarter(1, x_all)
    code = block_codes(seg_all, block_sets[0])
    shared = (seg_all[:, None], seg_all.reshape(-1, BLK))
    w_qkv, w_out = [w_first[0]], [w_first[1]]

    def attend(residual, normed, normed_all, layer):
        w = w_qkv[layer]
        qt = mm(w[:, :D], normed, 0, 1).astype(BF16) * jnp.asarray(0.125, BF16)
        kv = mm(normed_all, w[:, D:], 1, 0).astype(BF16)
        gap, far = bias_inputs(rel_bias[layer])
        ctxt, ctxb, lse = attention_forward(code, me, qt, kv, gap, far, *shared)
        branch = mm(ctxb, w_out[layer], 1, 0)
        saved = (residual, normed, normed_all, kv, ctxt, ctxb, lse, gap, far)
        return residual + branch, saved

    def attend_back(grad_out, saved, layer, qt_all, held, cover):
        residual, normed, normed_all, kv, ctxt, ctxb, lse, gap, far = saved
        w, wo = w_qkv[layer], w_out[layer]
        grad_low = grad_out.astype(BF16)
        dctx_own = mm(wo, grad_low, 1, 1).astype(BF16)
        delta = jnp.sum((dctx_own.astype(F32) * ctxt).reshape(HEADS, HEAD, rows), axis=1)
        stats = jnp.stack(three_parts(jnp.concatenate([lse, delta], axis=0)), axis=1)
        stats = stats.reshape(2 * HEADS, 3 * rows).astype(BF16)
        sent = jnp.concatenate([grad_low, stats, jnp.zeros((8, D), BF16)], axis=0)
        got, covered = lax.optimization_barrier((lax.all_gather(sent, "grp", axis=0), cover(sent)))
        grad_all = got[:, :rows].reshape(-1, D)
        stats_all = got[:, rows : rows + 2 * HEADS].reshape(-1, 2 * HEADS, 3, rows)
        stats_all = jnp.sum(stats_all.astype(F32), axis=2)
        dt_all = mm(wo, grad_all, 1, 1).astype(BF16)
        dt_all, held = lax.optimization_barrier((dt_all, held))
        dqkv, dgap, dfar = attention_backward(
            code, me, qt_all, dt_all, kv, stats_all, gap, far, *shared
        )
        out_part = mm(ctxb, grad_low, 0, 0) if layer else None
        qkv_part = mm(normed, dqkv, 0, 0)
        normed_grad = mm(dqkv, w, 1, 1)
        _, pull_back = jax.vjp(norm_rows, residual, norm_gains[layer, 0])
        residual_grad, gain_grad = pull_back(normed_grad)
        table_grad = bias_back(dgap, dfar)
        return grad_out + residual_grad, qkv_part, out_part, gain_grad, table_grad, grad_all, held, covered

    experts_all = router.shape[1]
    per_group = experts_all // groups
    capacity = rows * 2 * 10 // (7 * experts_all) + 1
    slots = (capacity + 16) // 16 * 16
    chosen = routes[0]
    ids = jnp.arange(experts_all, dtype=jnp.int32)
    chosen_hot = (chosen[:, :, None] == ids[None, None, :]).astype(F32)
    flat_hot = chosen_hot.reshape(2 * rows, experts_all)
    before = jnp.tril(jnp.ones((2 * rows, 2 * rows), BF16), -1)
    earlier = mm(before, flat_hot.astype(BF16), 1, 0)
    slot_ids = jnp.sum(earlier * flat_hot, axis=1).astype(jnp.int32)
    place = (chosen.reshape(-1) * slots + slot_ids).reshape(rows, 2)
    lanes = jnp.arange(experts_all * slots, dtype=jnp.int32)
    pick = [(place[:, k][:, None] == lanes[None, :]).astype(BF16) for k in range(2)]
    both = pick[0] + pick[1]

    def exchange(x):
        return lax.all_to_all(
            x.reshape(groups, per_group * slots, D), "grp", split_axis=0, concat_axis=0, tiled=True
        )

    def by_expert(x):
        return x.reshape(groups, per_group, slots, -1).swapaxes(0, 1).reshape(per_group, groups * slots, -1)

    def by_source(x):
        return x.reshape(per_group, groups, slots, -1).swapaxes(0, 1).reshape(groups, per_group * slots, -1)

    def all_replicas(x):
        return lax.all_gather(x, "rep", axis=1, tiled=True)

    x_all, cot_own = lax.optimization_barrier((x_all, cotangent[0]))
    cot_rows = by_expert(exchange(mm(both, cot_own, 0, 0).astype(BF16)))

    stream = tokens[0].astype(F32)
    own_a = norm_rows(stream, norm_gains[0, 0]).astype(BF16)
    all_a = norm_rows(x_all.astype(F32), norm_gains[0, 0]).astype(BF16)
    first_out, saved_a = attend(stream, own_a, all_a, 0)
    first_out, quarter_second, ffn_peers = lax.optimization_barrier(
        (first_out, quarter_second, ffn_peers)
    )
    ffn_others = [from_sibling(x) for x in ffn_peers]
    pieces = ffn_mine + [x for pair in zip(ffn_peers, ffn_others) for x in pair]
    after_ffn, normed_ffn, hidden_ffn, slope_ffn = ffn_forward(first_out, norm_gains[0, 1], pieces)
    after_ffn, cot_rows = lax.optimization_barrier((after_ffn, cot_rows))

    own_b = norm_rows(after_ffn, norm_gains[1, 0]).astype(BF16)
    own_b, quarter_second = lax.optimization_barrier((own_b, quarter_second))
    w_second = layer_weights(quarter_second)
    w_qkv.append(w_second[0])
    w_out.append(w_second[1])
    full_in = jnp.concatenate([x[:, :piece] for x in pieces], axis=1)
    full_down = jnp.concatenate([x[:, piece:] for x in pieces], axis=1)
    all_b, cot_rows, full_in, full_down = lax.optimization_barrier(
        (gather(own_b), cot_rows, full_in, full_down)
    )
    cot_all = all_replicas(cot_rows)
    second_out, saved_b = attend(after_ffn, own_b, all_b, 1)
    normed_moe = norm_rows(second_out, norm_gains[1, 1]).astype(BF16)
    normed_wide = normed_moe.astype(F32)
    router_wide = router.astype(F32)
    logits = jnp.dot(normed_wide, router_wide, precision=PRECISE)

    last_row = (jnp.arange(slots) == slots - 1)[None, :, None]

    def with_scalars(rows_in, values):
        parts = [jnp.pad(part, ((0, 0), (0, 128 - slots))) for part in three_parts(values)]
        info = jnp.concatenate(parts + [jnp.zeros((values.shape[0], D - 384), F32)], axis=1)
        return jnp.where(last_row, info[:, None, :], rows_in).astype(BF16)

    def scalars_of(rows_in):
        info = rows_in[:, slots - 1, :].astype(F32)
        total = info[:, 0:slots] + info[:, 128 : 128 + slots] + info[:, 256 : 256 + slots]
        return jnp.where(jnp.arange(slots)[None, :] == slots - 1, 0.0, total)

    grad_final = cotangent[0].astype(F32)
    selected = jnp.sum(logits[:, None, :] * chosen_hot, axis=-1)
    gate_probs = jax.nn.softmax(selected, axis=-1)
    gate_slots = jnp.sum(
        jnp.where(pick[0] == 1, gate_probs[:, 0:1], 0.0) + jnp.where(pick[1] == 1, gate_probs[:, 1:2], 0.0),
        axis=0,
    ).reshape(experts_all, slots)
    sent = mm(both, normed_moe, 0, 0).reshape(experts_all, slots, D)
    rows_e = by_expert(exchange(with_scalars(sent, gate_slots)))

    def gated(rows_in, cot):
        gates = scalars_of(rows_in.reshape(-1, slots, D)).reshape(per_group, -1, 1)
        return (gates * cot.astype(F32)).astype(BF16)

    dye = gated(rows_e, cot_rows)
    made_rows, rows_grad, gate_back = expert_rows(rows_e, dye, cot_rows, expert_in, expert_out)
    rows_grad = rows_grad.reshape(per_group * groups, slots, D)
    rows_grad = with_scalars(rows_grad, gate_back[:, :, 0].reshape(-1, slots))
    queries_all = [
        mm(w_qkv[n][:, :D], all_rows, 0, 1).astype(BF16) * jnp.asarray(0.125, BF16)
        for n, all_rows in enumerate((all_a, all_b))
    ]
    rows_e, cot_all = lax.optimization_barrier((rows_e, cot_all))
    rows_all = all_replicas(rows_e)
    dye_all = gated(rows_all, cot_all)
    back_grad, queries_all, dye_all = lax.optimization_barrier(
        (exchange(by_source(rows_grad)), queries_all, dye_all)
    )
    back_slots = scalars_of(back_grad.reshape(experts_all, slots, D)).reshape(1, -1)
    back_grad = back_grad.reshape(experts_all * slots, D)
    gate_grad = jnp.stack(
        [jnp.sum(jnp.where(pick[k] == 1, back_slots, 0.0), axis=1) for k in range(2)], axis=-1
    )
    select_grad = gate_probs * (gate_grad - jnp.sum(gate_probs * gate_grad, axis=-1, keepdims=True))
    logit_grad = jnp.sum(select_grad[:, :, None] * chosen_hot, axis=1)
    normed_moe_grad = jnp.dot(logit_grad, router_wide.T, precision=PRECISE) + mm(both, back_grad, 1, 0)
    _, pull_moe = jax.vjp(norm_rows, second_out, norm_gains[1, 1])
    moe_resid_grad, moe_gain_grad = pull_moe(normed_moe_grad)
    grad_second = grad_final + moe_resid_grad
    router_part = jnp.dot(normed_wide.T, logit_grad, precision=PRECISE)

    def finish(made):
        returned = exchange(by_source(made)).reshape(experts_all * slots, D)
        picked = [mm(pick[k], returned, 1, 0) for k in range(2)]
        return second_out + gate_probs[:, 0:1] * picked[0] + gate_probs[:, 1:2] * picked[1]


    def expert_half(part, earlier):
        def run(sent):
            rows_in, _ = lax.optimization_barrier((rows_all, sent))
            return tuple(expert_gradients(rows_in, dye_all, expert_in, expert_out, part, earlier))

        return run

    back_b = attend_back(grad_second, saved_b, 1, queries_all[1], made_rows, expert_half(0, ()))
    grad_ffn, qkv_part_b, out_part_b, gain_grad_b, table_grad_b, _, made_held, expert_sums = back_b
    final_out = finish(made_held)
    grad_ffn, final_out = lax.optimization_barrier((grad_ffn, final_out))
    down_low = grad_ffn.astype(BF16)
    down_part = mm(down_low, hidden_ffn, 0, 0)
    hidden_ffn_grad = mm(down_low, full_down, 1, 0)
    pre_ffn_grad = (hidden_ffn_grad * slope_ffn).astype(BF16)
    in_part = mm(normed_ffn, pre_ffn_grad, 0, 0)
    normed_ffn_grad = mm(pre_ffn_grad, full_in, 1, 1)
    _, pull_ffn = jax.vjp(norm_rows, first_out, norm_gains[0, 1])
    ffn_resid_grad, ffn_gain_grad = pull_ffn(normed_ffn_grad)
    grad_first = grad_ffn + ffn_resid_grad
    def packed(parts):
        return jnp.concatenate([part.astype(BF16) for part in parts], axis=1)

    def halves(k, which):
        at = k * span + which * piece
        return packed([x[:, at : at + piece] for x in (down_part, in_part)])

    theirs = from_sibling(jnp.stack([halves(k, 1) for k in range(replicas)]))
    ffn_parts = [
        (halves(k, 0).astype(F32) + theirs[k].astype(F32)).astype(BF16) for k in range(replicas)
    ]
    ffn_got = [from_replica(ffn_parts[k], k) for k in range(1, replicas)]
    back_a = attend_back(grad_first, saved_a, 0, queries_all[0], (), expert_half(1, expert_sums))
    grad_tokens, qkv_part_a, out_part_a, gain_grad_a, table_grad_a, grad_all_a, _, expert_sums = back_a
    out_part_a = mm(saved_a[5], grad_first.astype(BF16), 0, 0)
    parts_b, _ = lax.optimization_barrier((packed([qkv_part_b, out_part_b, out_part_a]), grad_all_a))
    parts_a = qkv_part_a.astype(BF16)
    shard_b = lax.psum_scatter(parts_b, "grp", scatter_dimension=0, tiled=True)
    parts_a, shard_b, ffn_got = lax.optimization_barrier((parts_a, shard_b, ffn_got))
    shard_a = lax.psum_scatter(parts_a, "grp", scatter_dimension=0, tiled=True)
    expert_in_sum, expert_out_sum = expert_half(2, expert_sums)(parts_a)

    def over_replicas(x):
        half = x.shape[0] // 2

        def add(v, mask):
            return (v.astype(F32) + from_replica(v, mask).astype(F32)).astype(BF16)

        first = [1 << b for b in range(replicas.bit_length() - 1)]
        top, low = x[:half], x[half:]
        for a, b in zip(first, first[::-1]):
            top, low = add(top, a), add(low, b)
        return jnp.concatenate([top, low], axis=0).astype(F32)

    ffn_total = ffn_parts[0].astype(F32)
    for x in ffn_got:
        ffn_total = ffn_total + x.astype(F32)
    ffn_total = ffn_total.astype(BF16)
    shard_a, ffn_total = lax.optimization_barrier((shard_a, ffn_total))
    same_core = [list(range(c, groups, 2)) for c in range(2)]
    band = lax.psum_scatter(
        ffn_total, "grp", scatter_dimension=0, tiled=True, axis_index_groups=same_core
    )
    band = band.reshape(2, -1, band.shape[1])
    kept = lax.dynamic_index_in_dim(band, core, 0, False)
    other = from_sibling(lax.dynamic_index_in_dim(band, 1 - core, 0, False))
    low, high = jnp.where(core == 0, kept, other), jnp.where(core == 0, other, kept)
    ffn_shard = jnp.concatenate([low[:, piece:], high[:, piece:], low[:, :piece], high[:, :piece]], axis=1)
    ffn_peers = [ffn_shard] + [from_replica(ffn_shard, k) for k in range(1, replicas)]

    def quarter_of(q):
        x = ffn_peers[0]
        for k in range(1, replicas):
            x = jnp.where(mine ^ k == q, ffn_peers[k], x)
        return x.astype(F32)

    ffn_sums = [quarter_of(q) for q in range(replicas)]
    in_sum = jnp.concatenate([x[:, :span] for x in ffn_sums], axis=1)
    down_sum = jnp.concatenate([x[:, span:] for x in ffn_sums], axis=1)
    total_b = shard_b.astype(F32)
    for k in range(1, replicas):
        total_b = total_b + from_replica(shard_b, k).astype(F32)
    qkv_b, out_b, out_a = total_b[:, : 3 * D], total_b[:, 3 * D : 4 * D], total_b[:, 4 * D :]
    qkv_a = over_replicas(shard_a)
    qkv_sum = jnp.stack([qkv_a, qkv_b], axis=1).reshape(qkv_weight.shape)
    out_sum = jnp.stack([out_a, out_b], axis=1)
    gain_all = jnp.stack(
        [jnp.stack([gain_grad_a, ffn_gain_grad]), jnp.stack([gain_grad_b, moe_gain_grad])]
    )
    table_all = jnp.stack([table_grad_a, table_grad_b])
    small = [gain_all, table_all, router_part]
    flat = jnp.concatenate([x.reshape(-1, BLK) for x in small], axis=0)
    for axis, count in (("rep", replicas), ("grp", groups)):
        for bit in range(count.bit_length() - 1):
            flat = flat + lax.ppermute(flat, axis, [(i, i ^ (1 << bit)) for i in range(count)])
    sizes = [x.size // BLK for x in small]
    cut = [flat[sum(sizes[:n]) : sum(sizes[: n + 1])].reshape(x.shape) for n, x in enumerate(small)]
    gain_sum, table_sum, router_sum = cut
    return (
        final_out[None], grad_tokens[None], qkv_sum, out_sum, in_sum, down_sum,
        gain_sum, table_sum, router_sum, expert_in_sum, expert_out_sum,
    )


def solution(mesh):
    return jax.shard_map(
        body,
        mesh=mesh,
        in_specs=(
            P("rep", "grp", None),
            P("rep", "grp"),
            P("rep", None, None),
            P("rep", "grp", None),
            P("grp", None, None, None),
            P("grp", None, None),
            P("grp", None),
            P("grp", None),
            P(),
            P(),
            P(),
            P("grp", None, None),
            P("grp", None, None),
            P("rep", "grp", None),
        ),
        out_specs=(
            P("rep", "grp", None),
            P("rep", "grp", None),
            P("grp", None, None, None),
            P("grp", None, None),
            P("grp", None),
            P("grp", None),
            P(),
            P(),
            P(),
            P("grp", None, None),
            P("grp", None, None),
        ),
        check_vma=False,
    )
```

```python
from functools import partial

import jax
import jax.numpy as jnp
from jax import lax
from jax.experimental import pallas as pl
from jax.experimental.pallas import tpu as pltpu
from jax.sharding import PartitionSpec as P

D = 768
HEADS = 12
HEAD = 64
PAIRS = 6
BLK = 128
ROWS = 256

BUCKET_EDGES = (18, 20, 23, 26, 30, 34, 39, 45, 51, 58, 66, 76, 86, 98, 112)
PRECISE = lax.Precision.HIGHEST
norm_eps = 1e-06
GELU_SCALE = 0.7978845608028654
GELU_CUBE = 0.044715
NEG = -1e30
VMEM_LIMIT = 60 * 1024 * 1024
F32 = jnp.float32
BF16 = jnp.bfloat16


def mm(a, b, ca, cb):
    return lax.dot_general(a, b, (((ca,), (cb,)), ((), ())), preferred_element_type=F32)


def norm_rows(residual, gain_vec):
    return (
        residual
        * lax.rsqrt(jnp.mean(residual * residual, axis=-1, keepdims=True) + norm_eps)
        * gain_vec
    )


def bucket_of(pos_gap):
    clipped = jnp.maximum(pos_gap, 0)
    bucket = jnp.minimum(clipped, 16)
    for edge_at in BUCKET_EDGES:
        bucket = bucket + (clipped >= edge_at).astype(jnp.int32)
    return bucket


def gap_hot():
    gaps = jnp.arange(2 * BLK, dtype=jnp.int32)
    return (bucket_of(gaps)[:, None] == jnp.arange(32, dtype=jnp.int32)[None, :]).astype(F32)


def pair_diag(ref, p, off):
    x = ref[128 * p : 128 * p + 128, pl.ds(off, 128)]
    z = jnp.zeros((64, 128), x.dtype)
    top = jnp.concatenate([x[:64], z], axis=0)
    low = jnp.concatenate([z, x[64:]], axis=0)
    return jnp.concatenate([top, low], axis=1)


def fill_tiles(gap_ref, far_ref, tile_ref):
    rows = lax.broadcasted_iota(jnp.int32, (128, 128), 0)
    cols = lax.broadcasted_iota(jnp.int32, (128, 128), 1)
    causal = cols >= rows
    for h in range(HEADS):
        x = jnp.broadcast_to(gap_ref[h : h + 1, :], (128, 256))
        r = pltpu.roll(x, 0, 1, stride=1, stride_axis=0)
        tile_ref[h, :, 0:128] = jnp.where(causal, r[:, :128], NEG)
        tile_ref[h, :, 128:256] = r[:, 128:]
        half = 128 * (h % 2)
        tile_ref[h, :, 256:384] = jnp.broadcast_to(
            far_ref[h // 2 : h // 2 + 1, half : half + 128], (128, 128)
        )
    tile_ref[:, :, 384:512] = jnp.full((HEADS, 128, 128), NEG, F32)


def tile_ids(code_ref, i, j):
    pick = [jnp.where(code_ref[i, j + n] == 0, 3, jnp.clip(i - j - n, 0, 2)) for n in range(2)]
    return [pl.multiple_of(t * 128, 128) for t in pick]


def pair_tiles(tile_ref, p, offs):
    cols = [
        jnp.concatenate([tile_ref[2 * p + h, :, pl.ds(off, 128)] for off in offs], axis=0)
        for h in range(2)
    ]
    return jnp.concatenate(cols, axis=1)


def seg_ok(segc_ref, segr_ref, i, j, count):
    kcol = segc_ref[pl.ds(pl.multiple_of(j * 128, 128), count), :]
    ok = kcol == segr_ref[pl.ds(i, 1), :]
    return jnp.concatenate([ok, ok], axis=1)


def split_visit(code_ref, i, j, visit):
    one, two = code_ref[i, j], code_ref[i, j + 1]
    near = (one == 2) | (two == 2)

    @pl.when(near)
    def _():
        visit(j, 2, True)

    @pl.when(jnp.logical_not(near) & (one + two == 2))
    def _():
        visit(j, 2, False)

    @pl.when(jnp.logical_not(near) & (one + two == 1))
    def _():
        visit(j + two, 1, False)


def fwd_kernel(
    code_ref, me_ref, qt_ref, kv_ref, gap_ref, far_ref, segc_ref, segr_ref,
    ctxt_ref, ctxb_ref, lse_ref, tile_ref, m_ref, l_ref, acc_ref,
):
    fill_tiles(gap_ref, far_ref, tile_ref)
    me = me_ref[0]

    def one_query(qi, _):
        i = me * 2 + qi
        qoff = pl.multiple_of(qi * 128, 128)
        m_ref[...] = jnp.full_like(m_ref, NEG)
        l_ref[...] = jnp.zeros_like(l_ref)
        acc_ref[...] = jnp.zeros_like(acc_ref)

        def visit(j, near):
            keys = pl.ds(pl.multiple_of(j * 128, 128), 128)
            if near:
                off = pl.multiple_of(jnp.minimum(i - j, 2) * 128, 128)
                ok = seg_ok(segc_ref, segr_ref, i, j, 128)
            for p in range(PAIRS):
                cols = slice(128 * p, 128 * p + 128)
                vcols = slice(D + 128 * p, D + 128 * p + 128)
                s = mm(kv_ref[keys, cols], pair_diag(qt_ref, p, qoff), 1, 0)
                if near:
                    s = jnp.where(ok, s + pair_tiles(tile_ref, p, [off]), NEG)
                else:
                    s = s + far_ref[p : p + 1, :]
                m_old = m_ref[p : p + 1, :]
                m_new = jnp.maximum(m_old, jnp.max(s, axis=0, keepdims=True))
                w = jnp.exp(s - m_new)
                shrink = jnp.exp(m_old - m_new)
                m_ref[p : p + 1, :] = m_new
                l_ref[p : p + 1, :] = l_ref[p : p + 1, :] * shrink + jnp.sum(
                    w, axis=0, keepdims=True
                )
                o = mm(kv_ref[keys, vcols], w.astype(BF16), 0, 0)
                o = jnp.concatenate([o[:64, :128], o[64:, 128:]], axis=1)
                acc_ref[p] = acc_ref[p] * shrink + o

        visit(i, True)

        def one_key(j, _):
            code = code_ref[i, j]

            @pl.when(code == 1)
            def _():
                visit(j, False)

            @pl.when(code == 2)
            def _():
                visit(j, True)

            return 0

        lax.fori_loop(0, i, one_key, 0)
        for p in range(PAIRS):
            total = l_ref[p : p + 1, :]
            ctx = acc_ref[p] * (1.0 / total)
            both = jnp.concatenate([ctx[:, :128], ctx[:, 128:]], axis=0)
            ctxt_ref[128 * p : 128 * p + 128, pl.ds(qoff, 128)] = both
            ctxb_ref[pl.ds(qoff, 128), 128 * p : 128 * p + 128] = both.T.astype(BF16)
            lse = m_ref[p : p + 1, :] + jnp.log(total)
            lse_ref[2 * p : 2 * p + 1, pl.ds(qoff, 128)] = lse[:, :128]
            lse_ref[2 * p + 1 : 2 * p + 2, pl.ds(qoff, 128)] = lse[:, 128:]
        return 0

    lax.fori_loop(0, 2, one_query, 0)


def bwd_kernel(
    code_ref, me_ref, qt_ref, dt_ref, kv_ref, stat_ref, gap_ref, far_ref, segc_ref, segr_ref,
    dqkv_ref, dgap_ref, dfar_ref,
    tile_ref, near_ref, facc_ref, dq_ref, dk_ref, dv_ref,
):
    fill_tiles(gap_ref, far_ref, tile_ref)
    near_ref[...] = jnp.zeros_like(near_ref)
    facc_ref[...] = jnp.zeros_like(facc_ref)
    dq_ref[...] = jnp.zeros_like(dq_ref)
    dk_ref[...] = jnp.zeros_like(dk_ref)
    dv_ref[...] = jnp.zeros_like(dv_ref)
    me = me_ref[0]

    def lanes(first, p, i):
        g, at = i // 2, first + 2 * p
        off = pl.multiple_of((i % 2) * 128, 128)
        return jnp.concatenate(
            [stat_ref[g, at : at + 1, pl.ds(off, 128)], stat_ref[g, at + 1 : at + 2, pl.ds(off, 128)]],
            axis=1,
        )

    def visit(i, j, blocks, near, by_query, by_key):
        keys = pl.ds(pl.multiple_of(j * 128, 128), 128 * blocks)
        own = pl.ds(pl.multiple_of((j - 2 * me) * 128, 128), 128 * blocks)
        qoff = pl.multiple_of(i * 128, 128)
        if near:
            offs = tile_ids(code_ref, i, j)
            ok = seg_ok(segc_ref, segr_ref, i, j, 256)
        for p in range(PAIRS):
            cols = slice(128 * p, 128 * p + 128)
            vcols = slice(D + 128 * p, D + 128 * p + 128)
            qd, od = pair_diag(qt_ref, p, qoff), pair_diag(dt_ref, p, qoff)
            s = mm(kv_ref[keys, cols], qd, 1, 0)
            lse = lanes(0, p, i)
            if near:
                w = jnp.exp(jnp.where(ok, s + pair_tiles(tile_ref, p, offs) - lse, NEG))
            else:
                w = jnp.exp(s + (far_ref[p : p + 1, :] - lse))
            dp = mm(kv_ref[keys, vcols], od, 1, 0)
            ds = w * (dp - lanes(HEADS, p, i))
            dsb = ds.astype(BF16)
            if by_key:
                dv_ref[p, own] += mm(w.astype(BF16), od, 1, 1)
                dk_ref[p, own] += mm(dsb, qd, 1, 1)
            if by_query:
                qi = i - 2 * me
                o = mm(kv_ref[keys, cols], dsb, 0, 0)
                dq_ref[qi, p] += jnp.concatenate([o[:64, :128], o[64:, 128:]], axis=1)
                if near:
                    for n in range(2):
                        for h in range(2):
                            part = ds[128 * n : 128 * n + 128, 128 * h : 128 * h + 128]
                            near_ref[2 * p + h, :, pl.ds(offs[n], 128)] += part
                else:
                    part = ds[0:8]
                    for a in range(1, 16 * blocks):
                        part = part + ds[8 * a : 8 * a + 8]
                    facc_ref[p] += part

    def one_query(qi, _):
        i = me * 2 + qi
        visit(i, 2 * me, 2, True, True, True)

        def two_keys(t, _):
            split_visit(code_ref, i, 2 * t, lambda j, blocks, near: visit(i, j, blocks, near, True, False))
            return 0

        lax.fori_loop(0, me, two_keys, 0)
        for p in range(PAIRS):
            x = dq_ref[qi, p] * 0.125
            both = jnp.concatenate([x[:, :128], x[:, 128:]], axis=0)
            dqkv_ref[pl.ds(pl.multiple_of(qi * 128, 128), 128), 128 * p : 128 * p + 128] = both.T.astype(BF16)
        return 0

    lax.fori_loop(0, 2, one_query, 0)

    def later(i, _):
        split_visit(code_ref, i, 2 * me, lambda j, blocks, near: visit(i, j, blocks, near, False, True))
        return 0

    lax.fori_loop(2 * me + 2, code_ref.shape[0], later, 0)
    for p in range(PAIRS):
        at = D + 128 * p
        dqkv_ref[:, at : at + 128] = dk_ref[p].astype(BF16)
        dqkv_ref[:, D + at : D + at + 128] = dv_ref[p].astype(BF16)

    for h in range(HEADS):
        x = near_ref[h, :, 0:256]
        g = x[0:8]
        for a in range(1, 16):
            g = g + pltpu.roll(x[8 * a : 8 * a + 8], 256 - 8 * a, 1)
        total = g[0:1]
        for b in range(1, 8):
            total = total + pltpu.roll(g, 256 - b, 1)[b : b + 1]
        dgap_ref[h : h + 1, :] = total
        half = 128 * (h % 2)
        far = jnp.sum(facc_ref[h // 2, :, half : half + 128], axis=0, keepdims=True)
        far = far + jnp.sum(near_ref[h, :, 256:384], axis=0, keepdims=True)
        dfar_ref[h : h + 1, :] = far


def vmem():
    return pl.BlockSpec(memory_space=pltpu.VMEM)


def smem():
    return pl.BlockSpec(memory_space=pltpu.SMEM)


def attention_forward(code, me, qt, kv, gap, far, segc, segr):
    length = kv.shape[0]
    return pl.pallas_call(
        fwd_kernel,
        name="attention_forward",
        out_shape=[
            jax.ShapeDtypeStruct((D, ROWS), F32),
            jax.ShapeDtypeStruct((ROWS, D), BF16),
            jax.ShapeDtypeStruct((HEADS, ROWS), F32),
        ],
        in_specs=[smem(), smem()] + [vmem()] * 6,
        out_specs=[vmem()] * 3,
        scratch_shapes=[
            pltpu.VMEM((HEADS, 128, 512), F32),
            pltpu.VMEM((8, 256), F32),
            pltpu.VMEM((8, 256), F32),
            pltpu.VMEM((PAIRS, 64, 256), F32),
        ],
        compiler_params=pltpu.CompilerParams(vmem_limit_bytes=VMEM_LIMIT),
        cost_estimate=pl.CostEstimate(
            flops=8 * ROWS * length * D,
            bytes_accessed=32 * length * D,
            transcendentals=HEADS * ROWS * length // 2,
        ),
    )(code, me, qt, kv, gap, far, segc, segr)


def attention_backward(code, me, qt, dt, kv, stats, gap, far, segc, segr):
    length = kv.shape[0]
    return pl.pallas_call(
        bwd_kernel,
        name="attention_backward",
        out_shape=[
            jax.ShapeDtypeStruct((ROWS, 3 * D), BF16),
            jax.ShapeDtypeStruct((HEADS, 256), F32),
            jax.ShapeDtypeStruct((HEADS, 128), F32),
        ],
        in_specs=[smem(), smem()] + [vmem()] * 8,
        out_specs=[vmem()] * 3,
        scratch_shapes=[
            pltpu.VMEM((HEADS, 128, 512), F32),
            pltpu.VMEM((HEADS, 128, 512), F32),
            pltpu.VMEM((PAIRS, 8, 256), F32),
            pltpu.VMEM((2, PAIRS, 64, 256), F32),
            pltpu.VMEM((PAIRS, 256, 128), F32),
            pltpu.VMEM((PAIRS, 256, 128), F32),
        ],
        compiler_params=pltpu.CompilerParams(vmem_limit_bytes=VMEM_LIMIT),
        cost_estimate=pl.CostEstimate(
            flops=14 * ROWS * length * D,
            bytes_accessed=64 * length * D,
            transcendentals=HEADS * ROWS * length,
        ),
    )(code, me, qt, dt, kv, stats, gap, far, segc, segr)


def ffn_kernel(x_ref, gain_ref, *refs):
    weights, (out_ref, norm_ref, hidden_ref, slope_ref) = refs[:-4], refs[-4:]
    x = x_ref[...]
    normed = norm_rows(x, gain_ref[...]).astype(BF16)
    norm_ref[...] = normed
    total = x
    piece = weights[0].shape[1] // 2
    for n, ref in enumerate(weights):
        at = slice(n * piece, n * piece + piece)
        hidden, slope = gelu_pair(mm(normed, ref[:, :piece], 1, 0))
        hidden = hidden.astype(BF16)
        hidden_ref[:, at] = hidden
        slope_ref[:, at] = slope
        total = total + mm(hidden, ref[:, piece:], 1, 1)
    out_ref[...] = total


def ffn_forward(x, gain, pieces):
    count = x.shape[0]
    width = sum(w.shape[1] // 2 for w in pieces)
    return pl.pallas_call(
        ffn_kernel,
        name="ffn_forward",
        in_specs=[vmem()] * (2 + len(pieces)),
        out_specs=[vmem()] * 4,
        out_shape=[
            jax.ShapeDtypeStruct((count, D), F32),
            jax.ShapeDtypeStruct((count, D), BF16),
            jax.ShapeDtypeStruct((count, width), BF16),
            jax.ShapeDtypeStruct((count, width), F32),
        ],
        compiler_params=pltpu.CompilerParams(vmem_limit_bytes=VMEM_LIMIT),
        cost_estimate=pl.CostEstimate(
            flops=4 * count * D * width, bytes_accessed=8 * D * width, transcendentals=count * width
        ),
    )(x, gain[None, :], *pieces)


def gelu_pair(u):
    t = jnp.tanh(GELU_SCALE * (u + GELU_CUBE * u * u * u))
    half = 0.5 * (1.0 + t)
    slope = half + 0.5 * u * (1.0 - t * t) * (GELU_SCALE * (1.0 + 3.0 * GELU_CUBE * u * u))
    return u * half, slope


def expert_rows_kernel(rows_ref, dye_ref, cot_ref, win_ref, wout_ref, made_ref, back_ref, gate_ref, made_acc, back_acc):
    step = pl.program_id(1)

    @pl.when(step == 0)
    def _():
        made_acc[...] = jnp.zeros_like(made_acc)
        back_acc[...] = jnp.zeros_like(back_acc)

    win, wout = win_ref[0], wout_ref[0]
    half = rows_ref.shape[1] // 2
    for c in range(2):
        at = slice(half * c, half * c + half)
        hidden, slope = gelu_pair(mm(rows_ref[0, at], win, 1, 0))
        made_acc[at] += mm(hidden.astype(BF16), wout, 1, 0)
        pre_back = (mm(dye_ref[0, at], wout, 1, 1) * slope).astype(BF16)
        back_acc[at] += mm(pre_back, win, 1, 1)

    @pl.when(step == pl.num_programs(1) - 1)
    def _():
        made = made_acc[...].astype(BF16)
        made_ref[0] = made
        back_ref[0] = back_acc[...]
        gate = jnp.sum(cot_ref[0].astype(F32) * made.astype(F32), axis=1, keepdims=True)
        gate_ref[0] = jnp.broadcast_to(gate, gate_ref.shape[1:])


def expert_rows(rows, dye, cot, w_in, w_out):
    count, total, _ = rows.shape
    width, block = w_in.shape[2], 512
    whole = pl.BlockSpec((1, total, D), lambda e, i: (e, 0, 0))
    return pl.pallas_call(
        expert_rows_kernel,
        name="expert_rows",
        grid=(count, width // block),
        in_specs=[
            whole,
            whole,
            whole,
            pl.BlockSpec((1, D, block), lambda e, i: (e, 0, i)),
            pl.BlockSpec((1, block, D), lambda e, i: (e, i, 0)),
        ],
        out_specs=[whole, whole, pl.BlockSpec((1, total, 128), lambda e, i: (e, 0, 0))],
        out_shape=[
            jax.ShapeDtypeStruct(rows.shape, BF16),
            jax.ShapeDtypeStruct(rows.shape, F32),
            jax.ShapeDtypeStruct((count, total, 128), F32),
        ],
        scratch_shapes=[pltpu.VMEM((total, D), F32), pltpu.VMEM((total, D), F32)],
        compiler_params=pltpu.CompilerParams(vmem_limit_bytes=VMEM_LIMIT),
        cost_estimate=pl.CostEstimate(
            flops=8 * count * total * D * width,
            bytes_accessed=16 * count * D * width,
            transcendentals=count * total * width,
        ),
    )(rows, dye, cot, w_in, w_out)


def expert_kernel(rows_ref, dye_ref, win_ref, wout_ref, *rest):
    in_ref, out_ref = rest[-2:]
    total = rows_ref.shape[1]
    step = total // 3
    win, wout = win_ref[0], wout_ref[0]
    for c in range(3):
        rows = rows_ref[0, step * c : step * c + step]
        dye = dye_ref[0, step * c : step * c + step]
        hidden, slope = gelu_pair(mm(rows, win, 1, 0))
        pre_back = (mm(dye, wout, 1, 1) * slope).astype(BF16)
        grad_in = mm(rows, pre_back, 0, 0)
        grad_out = mm(hidden.astype(BF16), dye, 0, 0)
        if c == 0:
            in_ref[0], out_ref[0] = grad_in, grad_out
        else:
            in_ref[0] += grad_in
            out_ref[0] += grad_out


def expert_gradients(rows, dye, w_in, w_out, part, earlier):
    count, total, _ = rows.shape
    width, block = w_in.shape[2], 512
    blocks = width // block
    edges = (0, blocks // 2, blocks // 2 + blocks // 6, blocks)
    first, steps = edges[part], edges[part + 1] - edges[part]
    whole = pl.BlockSpec((1, total, D), lambda e, i: (e, 0, 0))
    by_in = pl.BlockSpec((1, D, block), lambda e, i: (e, 0, i + first))
    by_out = pl.BlockSpec((1, block, D), lambda e, i: (e, i + first, 0))
    return pl.pallas_call(
        expert_kernel,
        name=f"expert_gradients_{part}",
        grid=(count, steps),
        in_specs=[whole, whole, by_in, by_out] + [pl.BlockSpec(memory_space=pl.ANY)] * len(earlier),
        out_specs=[by_in, by_out],
        out_shape=[
            jax.ShapeDtypeStruct(w_in.shape, F32),
            jax.ShapeDtypeStruct(w_out.shape, F32),
        ],
        input_output_aliases={4 + n: n for n in range(len(earlier))},
        compiler_params=pltpu.CompilerParams(vmem_limit_bytes=VMEM_LIMIT),
        cost_estimate=pl.CostEstimate(
            flops=8 * count * total * D * block * steps,
            bytes_accessed=64 * count * D * block * steps,
            transcendentals=count * total * block * steps,
        ),
    )(rows, dye, w_in, w_out, *earlier)


def three_parts(x):
    parts = []
    for _ in range(3):
        parts.append(lax.reduce_precision(x, 8, 7))
        x = x - parts[-1]
    return parts


def block_codes(seg_all, blocks):
    count = blocks.shape[0]
    rows = seg_all.reshape(count, BLK)
    least, most = jnp.min(rows, axis=1), jnp.max(rows, axis=1)
    ids = jnp.arange(count, dtype=jnp.int32)
    gap = ids[:, None] - ids[None, :]
    meet = (most[None, :] >= least[:, None]) & (least[None, :] <= most[:, None])
    live = (gap >= 0) & (blocks == 1) & meet
    same = (
        (least == most)[:, None] & (least == most)[None, :] & (least[:, None] == least[None, :])
    )
    return jnp.where(live, jnp.where(same & (gap >= 2), 1, 2), 0).astype(jnp.int32)


def bias_inputs(table):
    gap = jnp.dot(table, gap_hot().T, precision=PRECISE)
    far = jnp.repeat(table[:, 31].reshape(PAIRS, 2), BLK, axis=1)
    return gap, far


def bias_back(dgap, dfar):
    near = jnp.dot(dgap, gap_hot(), precision=PRECISE)
    last = (jnp.arange(32) == 31).astype(F32)[None, :]
    return near + jnp.sum(dfar, axis=1, keepdims=True) * last


def body(
    tokens, segments, block_sets, routes, qkv_weight, out_weight, ffn_in, ffn_out,
    norm_gains, rel_bias, router, expert_in, expert_out, cotangent,
):
    gather = partial(lax.all_gather, axis_name="grp", axis=0, tiled=True)
    rows = tokens.shape[1]
    me = lax.axis_index("grp").astype(jnp.int32).reshape(1)
    replicas, groups = lax.axis_size("rep"), lax.axis_size("grp")
    mine, core = lax.axis_index("rep"), lax.axis_index("grp") % 2

    def from_replica(x, k):
        return lax.ppermute(x, "rep", [(i, i ^ k) for i in range(replicas)])

    def from_sibling(x):
        return lax.ppermute(x, "grp", [(i, i ^ 1) for i in range(groups)])

    def swapped_cores(got):
        other = from_sibling(jnp.stack(got))
        return [other[k] for k in range(replicas - 1)]

    def layer_quarter(layer, after):
        count = qkv_weight.shape[0] // replicas
        part_qkv = lax.dynamic_slice(
            qkv_weight, (mine * count, layer, 0, 0), (count, 1) + qkv_weight.shape[2:]
        )
        part_out = lax.dynamic_slice(out_weight, (mine * count, layer, 0), (count, 1, D))
        part = jnp.concatenate([part_qkv.reshape(count, 3 * D), part_out.reshape(count, D)], axis=1)
        if after is not None:
            part, _ = lax.optimization_barrier((part, after))
        return lax.all_gather(part, "grp", axis=0)

    def layer_weights(quarter):
        width = quarter.shape[2] // 2
        half = lax.dynamic_slice_in_dim(quarter, core * width, width, 2)
        got = [from_replica(half, k) for k in range(1, replicas)]
        other = swapped_cores(got)
        full = jnp.zeros((groups, replicas) + quarter.shape[1:], BF16)
        full = lax.dynamic_update_slice(full, quarter[:, None], (0, mine, 0, 0))
        for k in range(1, replicas):
            for part, which in ((got[k - 1], core), (other[k - 1], 1 - core)):
                full = lax.dynamic_update_slice(full, part[:, None], (0, mine ^ k, 0, which * width))
        full = full.reshape(-1, 2 * width)
        return full[:, : 3 * D], full[:, 3 * D :]

    quarter_first = layer_quarter(0, None)
    w_first = layer_weights(quarter_first)

    span = ffn_in.shape[1] // replicas
    piece = span // 2
    ffn_own = [lax.dynamic_slice_in_dim(w, mine * span, span, 1) for w in (ffn_in, ffn_out)]
    ffn_own = jnp.concatenate([w[:, h * piece : h * piece + piece] for h in range(2) for w in ffn_own], axis=1)
    seg_row = jnp.pad(segments.astype(BF16), ((0, 7), (0, ffn_own.shape[1] - rows)))
    ffn_own = jnp.concatenate([ffn_own, seg_row], axis=0)
    ffn_own, quarter_first = lax.optimization_barrier((ffn_own, quarter_first))
    ffn_quarter = lax.all_gather(ffn_own, "grp", axis=0)
    seg_all = ffn_quarter[:, ffn_in.shape[0], :rows].astype(jnp.int32).reshape(-1)
    tokens_own, ffn_quarter = lax.optimization_barrier((tokens[0], ffn_quarter))
    x_all = gather(tokens_own)
    ffn_mine = [
        lax.dynamic_slice(ffn_quarter, (0, 0, n * span), (groups, ffn_in.shape[0], span)).reshape(-1, span)
        for n in (core, 1 - core)
    ]
    ffn_peers = [from_replica(ffn_mine[0], k) for k in range(1, replicas)]

    quarter_second = layer_quarter(1, x_all)
    code = block_codes(seg_all, block_sets[0])
    shared = (seg_all[:, None], seg_all.reshape(-1, BLK))
    w_qkv, w_out = [w_first[0]], [w_first[1]]

    def attend(residual, normed, normed_all, layer):
        w = w_qkv[layer]
        qt = mm(w[:, :D], normed, 0, 1).astype(BF16) * jnp.asarray(0.125, BF16)
        kv = mm(normed_all, w[:, D:], 1, 0).astype(BF16)
        gap, far = bias_inputs(rel_bias[layer])
        ctxt, ctxb, lse = attention_forward(code, me, qt, kv, gap, far, *shared)
        branch = mm(ctxb, w_out[layer], 1, 0)
        saved = (residual, normed, normed_all, kv, ctxt, ctxb, lse, gap, far)
        return residual + branch, saved

    def attend_back(grad_out, saved, layer, qt_all, held, cover):
        residual, normed, normed_all, kv, ctxt, ctxb, lse, gap, far = saved
        w, wo = w_qkv[layer], w_out[layer]
        grad_low = grad_out.astype(BF16)
        dctx_own = mm(wo, grad_low, 1, 1).astype(BF16)
        delta = jnp.sum((dctx_own.astype(F32) * ctxt).reshape(HEADS, HEAD, rows), axis=1)
        stats = jnp.stack(three_parts(jnp.concatenate([lse, delta], axis=0)), axis=1)
        stats = stats.reshape(2 * HEADS, 3 * rows).astype(BF16)
        sent = jnp.concatenate([grad_low, stats, jnp.zeros((8, D), BF16)], axis=0)
        got, covered = lax.optimization_barrier((lax.all_gather(sent, "grp", axis=0), cover(sent)))
        grad_all = got[:, :rows].reshape(-1, D)
        stats_all = got[:, rows : rows + 2 * HEADS].reshape(-1, 2 * HEADS, 3, rows)
        stats_all = jnp.sum(stats_all.astype(F32), axis=2)
        dt_all = mm(wo, grad_all, 1, 1).astype(BF16)
        dt_all, held = lax.optimization_barrier((dt_all, held))
        dqkv, dgap, dfar = attention_backward(
            code, me, qt_all, dt_all, kv, stats_all, gap, far, *shared
        )
        normed_grad = mm(dqkv, w, 1, 1)
        _, pull_back = jax.vjp(norm_rows, residual, norm_gains[layer, 0])
        residual_grad, gain_grad = pull_back(normed_grad)
        table_grad = bias_back(dgap, dfar)
        return grad_out + residual_grad, dqkv, gain_grad, table_grad, grad_all, held, covered

    experts_all = router.shape[1]
    per_group = experts_all // groups
    capacity = rows * 2 * 10 // (7 * experts_all) + 1
    slots = (capacity + 16) // 16 * 16
    chosen = routes[0]
    ids = jnp.arange(experts_all, dtype=jnp.int32)
    chosen_hot = (chosen[:, :, None] == ids[None, None, :]).astype(F32)
    flat_hot = chosen_hot.reshape(2 * rows, experts_all)
    before = jnp.tril(jnp.ones((2 * rows, 2 * rows), BF16), -1)
    earlier = mm(before, flat_hot.astype(BF16), 1, 0)
    slot_ids = jnp.sum(earlier * flat_hot, axis=1).astype(jnp.int32)
    place = (chosen.reshape(-1) * slots + slot_ids).reshape(rows, 2)
    lanes = jnp.arange(experts_all * slots, dtype=jnp.int32)
    pick = [(place[:, k][:, None] == lanes[None, :]).astype(BF16) for k in range(2)]
    both = pick[0] + pick[1]

    def exchange(x):
        return lax.all_to_all(
            x.reshape(groups, per_group * slots, D), "grp", split_axis=0, concat_axis=0, tiled=True
        )

    def by_expert(x):
        return x.reshape(groups, per_group, slots, -1).swapaxes(0, 1).reshape(per_group, groups * slots, -1)

    def by_source(x):
        return x.reshape(per_group, groups, slots, -1).swapaxes(0, 1).reshape(groups, per_group * slots, -1)

    def all_replicas(x):
        return lax.all_gather(x, "rep", axis=1, tiled=True)

    x_all, cot_own = lax.optimization_barrier((x_all, cotangent[0]))
    cot_rows = by_expert(exchange(mm(both, cot_own, 0, 0).astype(BF16)))

    stream = tokens[0].astype(F32)
    own_a = norm_rows(stream, norm_gains[0, 0]).astype(BF16)
    all_a = norm_rows(x_all.astype(F32), norm_gains[0, 0]).astype(BF16)
    first_out, saved_a = attend(stream, own_a, all_a, 0)
    first_out, quarter_second, ffn_peers = lax.optimization_barrier(
        (first_out, quarter_second, ffn_peers)
    )
    ffn_others = [from_sibling(x) for x in ffn_peers]
    pieces = ffn_mine + [x for pair in zip(ffn_peers, ffn_others) for x in pair]
    after_ffn, normed_ffn, hidden_ffn, slope_ffn = ffn_forward(first_out, norm_gains[0, 1], pieces)
    after_ffn, cot_rows = lax.optimization_barrier((after_ffn, cot_rows))

    own_b = norm_rows(after_ffn, norm_gains[1, 0]).astype(BF16)
    own_b, quarter_second = lax.optimization_barrier((own_b, quarter_second))
    w_second = layer_weights(quarter_second)
    w_qkv.append(w_second[0])
    w_out.append(w_second[1])
    full_in = jnp.concatenate([x[:, :piece] for x in pieces], axis=1)
    full_down = jnp.concatenate([x[:, piece:] for x in pieces], axis=1)
    all_b, cot_rows, full_in, full_down = lax.optimization_barrier(
        (gather(own_b), cot_rows, full_in, full_down)
    )
    cot_all = all_replicas(cot_rows)
    second_out, saved_b = attend(after_ffn, own_b, all_b, 1)
    normed_moe = norm_rows(second_out, norm_gains[1, 1]).astype(BF16)
    normed_wide = normed_moe.astype(F32)
    router_wide = router.astype(F32)
    logits = jnp.dot(normed_wide, router_wide, precision=PRECISE)

    last_row = (jnp.arange(slots) == slots - 1)[None, :, None]

    def with_scalars(rows_in, values):
        parts = [jnp.pad(part, ((0, 0), (0, 128 - slots))) for part in three_parts(values)]
        info = jnp.concatenate(parts + [jnp.zeros((values.shape[0], D - 384), F32)], axis=1)
        return jnp.where(last_row, info[:, None, :], rows_in).astype(BF16)

    def scalars_of(rows_in):
        info = rows_in[:, slots - 1, :].astype(F32)
        total = info[:, 0:slots] + info[:, 128 : 128 + slots] + info[:, 256 : 256 + slots]
        return jnp.where(jnp.arange(slots)[None, :] == slots - 1, 0.0, total)

    grad_final = cotangent[0].astype(F32)
    selected = jnp.sum(logits[:, None, :] * chosen_hot, axis=-1)
    gate_probs = jax.nn.softmax(selected, axis=-1)
    gate_slots = jnp.sum(
        jnp.where(pick[0] == 1, gate_probs[:, 0:1], 0.0) + jnp.where(pick[1] == 1, gate_probs[:, 1:2], 0.0),
        axis=0,
    ).reshape(experts_all, slots)
    sent = mm(both, normed_moe, 0, 0).reshape(experts_all, slots, D)
    rows_e = by_expert(exchange(with_scalars(sent, gate_slots)))

    def gated(rows_in, cot):
        gates = scalars_of(rows_in.reshape(-1, slots, D)).reshape(per_group, -1, 1)
        return (gates * cot.astype(F32)).astype(BF16)

    dye = gated(rows_e, cot_rows)
    made_rows, rows_grad, gate_back = expert_rows(rows_e, dye, cot_rows, expert_in, expert_out)
    rows_grad = rows_grad.reshape(per_group * groups, slots, D)
    rows_grad = with_scalars(rows_grad, gate_back[:, :, 0].reshape(-1, slots))
    queries_all = [
        mm(w_qkv[n][:, :D], all_rows, 0, 1).astype(BF16) * jnp.asarray(0.125, BF16)
        for n, all_rows in enumerate((all_a, all_b))
    ]
    rows_e, cot_all = lax.optimization_barrier((rows_e, cot_all))
    rows_all = all_replicas(rows_e)
    dye_all = gated(rows_all, cot_all)
    back_grad, queries_all, dye_all = lax.optimization_barrier(
        (exchange(by_source(rows_grad)), queries_all, dye_all)
    )
    back_slots = scalars_of(back_grad.reshape(experts_all, slots, D)).reshape(1, -1)
    back_grad = back_grad.reshape(experts_all * slots, D)
    gate_grad = jnp.stack(
        [jnp.sum(jnp.where(pick[k] == 1, back_slots, 0.0), axis=1) for k in range(2)], axis=-1
    )
    select_grad = gate_probs * (gate_grad - jnp.sum(gate_probs * gate_grad, axis=-1, keepdims=True))
    logit_grad = jnp.sum(select_grad[:, :, None] * chosen_hot, axis=1)
    normed_moe_grad = jnp.dot(logit_grad, router_wide.T, precision=PRECISE) + mm(both, back_grad, 1, 0)
    _, pull_moe = jax.vjp(norm_rows, second_out, norm_gains[1, 1])
    moe_resid_grad, moe_gain_grad = pull_moe(normed_moe_grad)
    grad_second = grad_final + moe_resid_grad
    router_part = jnp.dot(normed_wide.T, logit_grad, precision=PRECISE)

    def finish(made):
        returned = exchange(by_source(made)).reshape(experts_all * slots, D)
        picked = [mm(pick[k], returned, 1, 0) for k in range(2)]
        return second_out + gate_probs[:, 0:1] * picked[0] + gate_probs[:, 1:2] * picked[1]


    def expert_half(part, earlier, extra=()):
        def run(sent):
            rows_in, _, _ = lax.optimization_barrier((rows_all, sent, extra))
            return tuple(expert_gradients(rows_in, dye_all, expert_in, expert_out, part, earlier))

        return run

    back_b = attend_back(grad_second, saved_b, 1, queries_all[1], made_rows, expert_half(0, ()))
    grad_ffn, dqkv_b, gain_grad_b, table_grad_b, _, made_held, expert_sums = back_b
    final_out = finish(made_held)
    grad_ffn, final_out = lax.optimization_barrier((grad_ffn, final_out))
    down_low = grad_ffn.astype(BF16)
    down_part = mm(down_low, hidden_ffn, 0, 0)
    hidden_ffn_grad = mm(down_low, full_down, 1, 0)
    pre_ffn_grad = (hidden_ffn_grad * slope_ffn).astype(BF16)
    in_part = mm(normed_ffn, pre_ffn_grad, 0, 0)
    normed_ffn_grad = mm(pre_ffn_grad, full_in, 1, 1)
    _, pull_ffn = jax.vjp(norm_rows, first_out, norm_gains[0, 1])
    ffn_resid_grad, ffn_gain_grad = pull_ffn(normed_ffn_grad)
    grad_first = grad_ffn + ffn_resid_grad
    def packed(parts):
        return jnp.concatenate([part.astype(BF16) for part in parts], axis=1)

    def halves(k, which):
        at = k * span + which * piece
        return packed([x[:, at : at + piece] for x in (down_part, in_part)])

    their_half = jnp.stack([halves(k, 1) for k in range(replicas)])
    theirs = from_sibling(their_half)
    ffn_parts = [
        (halves(k, 0).astype(F32) + theirs[k].astype(F32)).astype(BF16) for k in range(replicas)
    ]

    def cover_a(sent):
        dq, _ = lax.optimization_barrier((dqkv_b, sent))
        part_b = packed(
            [
                mm(own_b, dq, 0, 0),
                mm(saved_b[5], grad_second.astype(BF16), 0, 0),
                mm(saved_a[5], grad_first.astype(BF16), 0, 0),
            ]
        )
        return expert_half(1, expert_sums, their_half)(sent), part_b, ffn_parts

    back_a = attend_back(grad_first, saved_a, 0, queries_all[0], (), cover_a)
    grad_tokens, dqkv_a, gain_grad_a, table_grad_a, grad_all_a, _, covered_a = back_a
    expert_sums, parts_b, ffn_parts = covered_a
    ffn_got = [from_replica(ffn_parts[k], k) for k in range(1, replicas)]
    parts_b, _ = lax.optimization_barrier((parts_b, grad_all_a))
    parts_a = mm(own_a, dqkv_a, 0, 0).astype(BF16)
    shard_b = lax.psum_scatter(parts_b, "grp", scatter_dimension=0, tiled=True)
    parts_a, shard_b, ffn_got = lax.optimization_barrier((parts_a, shard_b, ffn_got))
    shard_a = lax.psum_scatter(parts_a, "grp", scatter_dimension=0, tiled=True)
    expert_in_sum, expert_out_sum = expert_half(2, expert_sums)(parts_a)

    def over_replicas(x):
        half = x.shape[0] // 2

        def add(v, mask):
            return (v.astype(F32) + from_replica(v, mask).astype(F32)).astype(BF16)

        first = [1 << b for b in range(replicas.bit_length() - 1)]
        top, low = x[:half], x[half:]
        for a, b in zip(first, first[::-1]):
            top, low = add(top, a), add(low, b)
        return jnp.concatenate([top, low], axis=0).astype(F32)

    ffn_total = ffn_parts[0].astype(F32)
    for x in ffn_got:
        ffn_total = ffn_total + x.astype(F32)
    ffn_total = ffn_total.astype(BF16)
    shard_a, ffn_total = lax.optimization_barrier((shard_a, ffn_total))
    same_core = [list(range(c, groups, 2)) for c in range(2)]
    band = lax.psum_scatter(
        ffn_total, "grp", scatter_dimension=0, tiled=True, axis_index_groups=same_core
    )
    band = band.reshape(2, -1, band.shape[1])
    kept = lax.dynamic_index_in_dim(band, core, 0, False)
    other = from_sibling(lax.dynamic_index_in_dim(band, 1 - core, 0, False))
    low, high = jnp.where(core == 0, kept, other), jnp.where(core == 0, other, kept)
    ffn_shard = jnp.concatenate([low[:, piece:], high[:, piece:], low[:, :piece], high[:, :piece]], axis=1)
    ffn_peers = [ffn_shard] + [from_replica(ffn_shard, k) for k in range(1, replicas)]

    def quarter_of(q):
        x = ffn_peers[0]
        for k in range(1, replicas):
            x = jnp.where(mine ^ k == q, ffn_peers[k], x)
        return x.astype(F32)

    ffn_sums = [quarter_of(q) for q in range(replicas)]
    in_sum = jnp.concatenate([x[:, :span] for x in ffn_sums], axis=1)
    down_sum = jnp.concatenate([x[:, span:] for x in ffn_sums], axis=1)
    total_b = shard_b.astype(F32)
    for k in range(1, replicas):
        total_b = total_b + from_replica(shard_b, k).astype(F32)
    qkv_b, out_b, out_a = total_b[:, : 3 * D], total_b[:, 3 * D : 4 * D], total_b[:, 4 * D :]
    qkv_a = over_replicas(shard_a)
    qkv_sum = jnp.stack([qkv_a, qkv_b], axis=1).reshape(qkv_weight.shape)
    out_sum = jnp.stack([out_a, out_b], axis=1)
    gain_all = jnp.stack(
        [jnp.stack([gain_grad_a, ffn_gain_grad]), jnp.stack([gain_grad_b, moe_gain_grad])]
    )
    table_all = jnp.stack([table_grad_a, table_grad_b])
    small = [gain_all, table_all, router_part]
    flat = jnp.concatenate([x.reshape(-1, BLK) for x in small], axis=0)
    flat, expert_out_sum, ffn_total = lax.optimization_barrier((flat, expert_out_sum, ffn_total))
    for axis, count in (("rep", replicas), ("grp", groups)):
        for bit in range(count.bit_length() - 1):
            flat = flat + lax.ppermute(flat, axis, [(i, i ^ (1 << bit)) for i in range(count)])
    sizes = [x.size // BLK for x in small]
    cut = [flat[sum(sizes[:n]) : sum(sizes[: n + 1])].reshape(x.shape) for n, x in enumerate(small)]
    gain_sum, table_sum, router_sum = cut
    return (
        final_out[None], grad_tokens[None], qkv_sum, out_sum, in_sum, down_sum,
        gain_sum, table_sum, router_sum, expert_in_sum, expert_out_sum,
    )


def solution(mesh):
    return jax.shard_map(
        body,
        mesh=mesh,
        in_specs=(
            P("rep", "grp", None),
            P("rep", "grp"),
            P("rep", None, None),
            P("rep", "grp", None),
            P("grp", None, None, None),
            P("grp", None, None),
            P("grp", None),
            P("grp", None),
            P(),
            P(),
            P(),
            P("grp", None, None),
            P("grp", None, None),
            P("rep", "grp", None),
        ),
        out_specs=(
            P("rep", "grp", None),
            P("rep", "grp", None),
            P("grp", None, None, None),
            P("grp", None, None),
            P("grp", None),
            P("grp", None),
            P(),
            P(),
            P(),
            P("grp", None, None),
            P("grp", None, None),
        ),
        check_vma=False,
    )
```

```python
from functools import partial

import jax
import jax.numpy as jnp
from jax import lax
from jax.experimental import pallas as pl
from jax.experimental.pallas import tpu as pltpu
from jax.sharding import PartitionSpec as P

D = 768
HEADS = 12
HEAD = 64
PAIRS = 6
BLK = 128
ROWS = 256

BUCKET_EDGES = (18, 20, 23, 26, 30, 34, 39, 45, 51, 58, 66, 76, 86, 98, 112)
PRECISE = lax.Precision.HIGHEST
norm_eps = 1e-06
GELU_SCALE = 0.7978845608028654
GELU_CUBE = 0.044715
NEG = -1e30
VMEM_LIMIT = 60 * 1024 * 1024
F32 = jnp.float32
BF16 = jnp.bfloat16


def mm(a, b, ca, cb):
    return lax.dot_general(a, b, (((ca,), (cb,)), ((), ())), preferred_element_type=F32)


def norm_rows(residual, gain_vec):
    return (
        residual
        * lax.rsqrt(jnp.mean(residual * residual, axis=-1, keepdims=True) + norm_eps)
        * gain_vec
    )


def bucket_of(pos_gap):
    clipped = jnp.maximum(pos_gap, 0)
    bucket = jnp.minimum(clipped, 16)
    for edge_at in BUCKET_EDGES:
        bucket = bucket + (clipped >= edge_at).astype(jnp.int32)
    return bucket


def gap_hot():
    gaps = jnp.arange(2 * BLK, dtype=jnp.int32)
    return (bucket_of(gaps)[:, None] == jnp.arange(32, dtype=jnp.int32)[None, :]).astype(F32)


def pair_diag(ref, p, off):
    x = ref[128 * p : 128 * p + 128, pl.ds(off, 128)]
    z = jnp.zeros((64, 128), x.dtype)
    top = jnp.concatenate([x[:64], z], axis=0)
    low = jnp.concatenate([z, x[64:]], axis=0)
    return jnp.concatenate([top, low], axis=1)


def fill_tiles(gap_ref, far_ref, tile_ref):
    rows = lax.broadcasted_iota(jnp.int32, (128, 128), 0)
    cols = lax.broadcasted_iota(jnp.int32, (128, 128), 1)
    causal = cols >= rows
    for h in range(HEADS):
        x = jnp.broadcast_to(gap_ref[h : h + 1, :], (128, 256))
        r = pltpu.roll(x, 0, 1, stride=1, stride_axis=0)
        tile_ref[h, :, 0:128] = jnp.where(causal, r[:, :128], NEG)
        tile_ref[h, :, 128:256] = r[:, 128:]
        half = 128 * (h % 2)
        tile_ref[h, :, 256:384] = jnp.broadcast_to(
            far_ref[h // 2 : h // 2 + 1, half : half + 128], (128, 128)
        )
    tile_ref[:, :, 384:512] = jnp.full((HEADS, 128, 128), NEG, F32)


def tile_ids(code_ref, i, j):
    pick = [jnp.where(code_ref[i, j + n] == 0, 3, jnp.clip(i - j - n, 0, 2)) for n in range(2)]
    return [pl.multiple_of(t * 128, 128) for t in pick]


def pair_tiles(tile_ref, p, offs):
    cols = [
        jnp.concatenate([tile_ref[2 * p + h, :, pl.ds(off, 128)] for off in offs], axis=0)
        for h in range(2)
    ]
    return jnp.concatenate(cols, axis=1)


def seg_ok(segc_ref, segr_ref, i, j, count):
    kcol = segc_ref[pl.ds(pl.multiple_of(j * 128, 128), count), :]
    ok = kcol == segr_ref[pl.ds(i, 1), :]
    return jnp.concatenate([ok, ok], axis=1)


def split_visit(code_ref, i, j, visit):
    one, two = code_ref[i, j], code_ref[i, j + 1]
    near = (one == 2) | (two == 2)

    @pl.when(near)
    def _():
        visit(j, 2, True)

    @pl.when(jnp.logical_not(near) & (one + two == 2))
    def _():
        visit(j, 2, False)

    @pl.when(jnp.logical_not(near) & (one + two == 1))
    def _():
        visit(j + two, 1, False)


def fwd_kernel(
    code_ref, me_ref, qt_ref, kv_ref, gap_ref, far_ref, segc_ref, segr_ref,
    ctxt_ref, ctxb_ref, lse_ref, tile_ref, m_ref, l_ref, acc_ref,
):
    fill_tiles(gap_ref, far_ref, tile_ref)
    me = me_ref[0]

    def one_query(qi, _):
        i = me * 2 + qi
        qoff = pl.multiple_of(qi * 128, 128)
        m_ref[...] = jnp.full_like(m_ref, NEG)
        l_ref[...] = jnp.zeros_like(l_ref)
        acc_ref[...] = jnp.zeros_like(acc_ref)

        def visit(j, near):
            keys = pl.ds(pl.multiple_of(j * 128, 128), 128)
            if near:
                off = pl.multiple_of(jnp.minimum(i - j, 2) * 128, 128)
                ok = seg_ok(segc_ref, segr_ref, i, j, 128)
            for p in range(PAIRS):
                cols = slice(128 * p, 128 * p + 128)
                vcols = slice(D + 128 * p, D + 128 * p + 128)
                s = mm(kv_ref[keys, cols], pair_diag(qt_ref, p, qoff), 1, 0)
                if near:
                    s = jnp.where(ok, s + pair_tiles(tile_ref, p, [off]), NEG)
                else:
                    s = s + far_ref[p : p + 1, :]
                m_old = m_ref[p : p + 1, :]
                m_new = jnp.maximum(m_old, jnp.max(s, axis=0, keepdims=True))
                w = jnp.exp(s - m_new)
                shrink = jnp.exp(m_old - m_new)
                m_ref[p : p + 1, :] = m_new
                l_ref[p : p + 1, :] = l_ref[p : p + 1, :] * shrink + jnp.sum(
                    w, axis=0, keepdims=True
                )
                o = mm(kv_ref[keys, vcols], w.astype(BF16), 0, 0)
                o = jnp.concatenate([o[:64, :128], o[64:, 128:]], axis=1)
                acc_ref[p] = acc_ref[p] * shrink + o

        visit(i, True)

        def one_key(j, _):
            code = code_ref[i, j]

            @pl.when(code == 1)
            def _():
                visit(j, False)

            @pl.when(code == 2)
            def _():
                visit(j, True)

            return 0

        lax.fori_loop(0, i, one_key, 0)
        for p in range(PAIRS):
            total = l_ref[p : p + 1, :]
            ctx = acc_ref[p] * (1.0 / total)
            both = jnp.concatenate([ctx[:, :128], ctx[:, 128:]], axis=0)
            ctxt_ref[128 * p : 128 * p + 128, pl.ds(qoff, 128)] = both
            ctxb_ref[pl.ds(qoff, 128), 128 * p : 128 * p + 128] = both.T.astype(BF16)
            lse = m_ref[p : p + 1, :] + jnp.log(total)
            lse_ref[2 * p : 2 * p + 1, pl.ds(qoff, 128)] = lse[:, :128]
            lse_ref[2 * p + 1 : 2 * p + 2, pl.ds(qoff, 128)] = lse[:, 128:]
        return 0

    lax.fori_loop(0, 2, one_query, 0)


def bwd_kernel(
    code_ref, me_ref, qt_ref, dt_ref, kv_ref, stat_ref, gap_ref, far_ref, segc_ref, segr_ref,
    dqkv_ref, dgap_ref, dfar_ref,
    tile_ref, near_ref, facc_ref, dq_ref, dk_ref, dv_ref,
):
    fill_tiles(gap_ref, far_ref, tile_ref)
    near_ref[...] = jnp.zeros_like(near_ref)
    facc_ref[...] = jnp.zeros_like(facc_ref)
    dq_ref[...] = jnp.zeros_like(dq_ref)
    dk_ref[...] = jnp.zeros_like(dk_ref)
    dv_ref[...] = jnp.zeros_like(dv_ref)
    me = me_ref[0]

    def lanes(first, p, i):
        g, at = i // 2, first + 2 * p
        off = pl.multiple_of((i % 2) * 128, 128)
        return jnp.concatenate(
            [stat_ref[g, at : at + 1, pl.ds(off, 128)], stat_ref[g, at + 1 : at + 2, pl.ds(off, 128)]],
            axis=1,
        )

    def visit(i, j, blocks, near, by_query, by_key):
        keys = pl.ds(pl.multiple_of(j * 128, 128), 128 * blocks)
        own = pl.ds(pl.multiple_of((j - 2 * me) * 128, 128), 128 * blocks)
        qoff = pl.multiple_of(i * 128, 128)
        if near:
            offs = tile_ids(code_ref, i, j)
            ok = seg_ok(segc_ref, segr_ref, i, j, 256)
        for p in range(PAIRS):
            cols = slice(128 * p, 128 * p + 128)
            vcols = slice(D + 128 * p, D + 128 * p + 128)
            qd, od = pair_diag(qt_ref, p, qoff), pair_diag(dt_ref, p, qoff)
            s = mm(kv_ref[keys, cols], qd, 1, 0)
            lse = lanes(0, p, i)
            if near:
                w = jnp.exp(jnp.where(ok, s + pair_tiles(tile_ref, p, offs) - lse, NEG))
            else:
                w = jnp.exp(s + (far_ref[p : p + 1, :] - lse))
            dp = mm(kv_ref[keys, vcols], od, 1, 0)
            ds = w * (dp - lanes(HEADS, p, i))
            dsb = ds.astype(BF16)
            if by_key:
                dv_ref[p, own] += mm(w.astype(BF16), od, 1, 1)
                dk_ref[p, own] += mm(dsb, qd, 1, 1)
            if by_query:
                qi = i - 2 * me
                o = mm(kv_ref[keys, cols], dsb, 0, 0)
                dq_ref[qi, p] += jnp.concatenate([o[:64, :128], o[64:, 128:]], axis=1)
                if near:
                    for n in range(2):
                        for h in range(2):
                            part = ds[128 * n : 128 * n + 128, 128 * h : 128 * h + 128]
                            near_ref[2 * p + h, :, pl.ds(offs[n], 128)] += part
                else:
                    part = ds[0:8]
                    for a in range(1, 16 * blocks):
                        part = part + ds[8 * a : 8 * a + 8]
                    facc_ref[p] += part

    def one_query(qi, _):
        i = me * 2 + qi
        visit(i, 2 * me, 2, True, True, True)

        def two_keys(t, _):
            split_visit(code_ref, i, 2 * t, lambda j, blocks, near: visit(i, j, blocks, near, True, False))
            return 0

        lax.fori_loop(0, me, two_keys, 0)
        for p in range(PAIRS):
            x = dq_ref[qi, p] * 0.125
            both = jnp.concatenate([x[:, :128], x[:, 128:]], axis=0)
            dqkv_ref[pl.ds(pl.multiple_of(qi * 128, 128), 128), 128 * p : 128 * p + 128] = both.T.astype(BF16)
        return 0

    lax.fori_loop(0, 2, one_query, 0)

    def later(i, _):
        split_visit(code_ref, i, 2 * me, lambda j, blocks, near: visit(i, j, blocks, near, False, True))
        return 0

    lax.fori_loop(2 * me + 2, code_ref.shape[0], later, 0)
    for p in range(PAIRS):
        at = D + 128 * p
        dqkv_ref[:, at : at + 128] = dk_ref[p].astype(BF16)
        dqkv_ref[:, D + at : D + at + 128] = dv_ref[p].astype(BF16)

    for h in range(HEADS):
        x = near_ref[h, :, 0:256]
        g = x[0:8]
        for a in range(1, 16):
            g = g + pltpu.roll(x[8 * a : 8 * a + 8], 256 - 8 * a, 1)
        total = g[0:1]
        for b in range(1, 8):
            total = total + pltpu.roll(g, 256 - b, 1)[b : b + 1]
        dgap_ref[h : h + 1, :] = total
        half = 128 * (h % 2)
        far = jnp.sum(facc_ref[h // 2, :, half : half + 128], axis=0, keepdims=True)
        far = far + jnp.sum(near_ref[h, :, 256:384], axis=0, keepdims=True)
        dfar_ref[h : h + 1, :] = far


def vmem():
    return pl.BlockSpec(memory_space=pltpu.VMEM)


def smem():
    return pl.BlockSpec(memory_space=pltpu.SMEM)


def attention_forward(code, me, qt, kv, gap, far, segc, segr):
    length = kv.shape[0]
    return pl.pallas_call(
        fwd_kernel,
        name="attention_forward",
        out_shape=[
            jax.ShapeDtypeStruct((D, ROWS), F32),
            jax.ShapeDtypeStruct((ROWS, D), BF16),
            jax.ShapeDtypeStruct((HEADS, ROWS), F32),
        ],
        in_specs=[smem(), smem()] + [vmem()] * 6,
        out_specs=[vmem()] * 3,
        scratch_shapes=[
            pltpu.VMEM((HEADS, 128, 512), F32),
            pltpu.VMEM((8, 256), F32),
            pltpu.VMEM((8, 256), F32),
            pltpu.VMEM((PAIRS, 64, 256), F32),
        ],
        compiler_params=pltpu.CompilerParams(vmem_limit_bytes=VMEM_LIMIT),
        cost_estimate=pl.CostEstimate(
            flops=8 * ROWS * length * D,
            bytes_accessed=32 * length * D,
            transcendentals=HEADS * ROWS * length // 2,
        ),
    )(code, me, qt, kv, gap, far, segc, segr)


def attention_backward(code, me, qt, dt, kv, stats, gap, far, segc, segr):
    length = kv.shape[0]
    return pl.pallas_call(
        bwd_kernel,
        name="attention_backward",
        out_shape=[
            jax.ShapeDtypeStruct((ROWS, 3 * D), BF16),
            jax.ShapeDtypeStruct((HEADS, 256), F32),
            jax.ShapeDtypeStruct((HEADS, 128), F32),
        ],
        in_specs=[smem(), smem()] + [vmem()] * 8,
        out_specs=[vmem()] * 3,
        scratch_shapes=[
            pltpu.VMEM((HEADS, 128, 512), F32),
            pltpu.VMEM((HEADS, 128, 512), F32),
            pltpu.VMEM((PAIRS, 8, 256), F32),
            pltpu.VMEM((2, PAIRS, 64, 256), F32),
            pltpu.VMEM((PAIRS, 256, 128), F32),
            pltpu.VMEM((PAIRS, 256, 128), F32),
        ],
        compiler_params=pltpu.CompilerParams(vmem_limit_bytes=VMEM_LIMIT),
        cost_estimate=pl.CostEstimate(
            flops=14 * ROWS * length * D,
            bytes_accessed=64 * length * D,
            transcendentals=HEADS * ROWS * length,
        ),
    )(code, me, qt, dt, kv, stats, gap, far, segc, segr)


def ffn_kernel(x_ref, gain_ref, *refs):
    weights, (out_ref, norm_ref, hidden_ref, slope_ref) = refs[:-4], refs[-4:]
    x = x_ref[...]
    normed = norm_rows(x, gain_ref[...]).astype(BF16)
    norm_ref[...] = normed
    total = x
    piece = weights[0].shape[1] // 2
    for n, ref in enumerate(weights):
        at = slice(n * piece, n * piece + piece)
        hidden, slope = gelu_pair(mm(normed, ref[:, :piece], 1, 0))
        hidden = hidden.astype(BF16)
        hidden_ref[:, at] = hidden
        slope_ref[:, at] = slope
        total = total + mm(hidden, ref[:, piece:], 1, 1)
    out_ref[...] = total


def ffn_forward(x, gain, pieces):
    count = x.shape[0]
    width = sum(w.shape[1] // 2 for w in pieces)
    return pl.pallas_call(
        ffn_kernel,
        name="ffn_forward",
        in_specs=[vmem()] * (2 + len(pieces)),
        out_specs=[vmem()] * 4,
        out_shape=[
            jax.ShapeDtypeStruct((count, D), F32),
            jax.ShapeDtypeStruct((count, D), BF16),
            jax.ShapeDtypeStruct((count, width), BF16),
            jax.ShapeDtypeStruct((count, width), F32),
        ],
        compiler_params=pltpu.CompilerParams(vmem_limit_bytes=VMEM_LIMIT),
        cost_estimate=pl.CostEstimate(
            flops=4 * count * D * width, bytes_accessed=8 * D * width, transcendentals=count * width
        ),
    )(x, gain[None, :], *pieces)


def gelu_pair(u):
    t = jnp.tanh(GELU_SCALE * (u + GELU_CUBE * u * u * u))
    half = 0.5 * (1.0 + t)
    slope = half + 0.5 * u * (1.0 - t * t) * (GELU_SCALE * (1.0 + 3.0 * GELU_CUBE * u * u))
    return u * half, slope


def expert_rows_kernel(rows_ref, dye_ref, cot_ref, win_ref, wout_ref, made_ref, back_ref, gate_ref, made_acc, back_acc):
    step = pl.program_id(1)

    @pl.when(step == 0)
    def _():
        made_acc[...] = jnp.zeros_like(made_acc)
        back_acc[...] = jnp.zeros_like(back_acc)

    win, wout = win_ref[0], wout_ref[0]
    half = rows_ref.shape[1] // 2
    for c in range(2):
        at = slice(half * c, half * c + half)
        hidden, slope = gelu_pair(mm(rows_ref[0, at], win, 1, 0))
        made_acc[at] += mm(hidden.astype(BF16), wout, 1, 0)
        pre_back = (mm(dye_ref[0, at], wout, 1, 1) * slope).astype(BF16)
        back_acc[at] += mm(pre_back, win, 1, 1)

    @pl.when(step == pl.num_programs(1) - 1)
    def _():
        made = made_acc[...].astype(BF16)
        made_ref[0] = made
        back_ref[0] = back_acc[...]
        gate = jnp.sum(cot_ref[0].astype(F32) * made.astype(F32), axis=1, keepdims=True)
        gate_ref[0] = jnp.broadcast_to(gate, gate_ref.shape[1:])


def expert_rows(rows, dye, cot, w_in, w_out):
    count, total, _ = rows.shape
    width, block = w_in.shape[2], 512
    whole = pl.BlockSpec((1, total, D), lambda e, i: (e, 0, 0))
    return pl.pallas_call(
        expert_rows_kernel,
        name="expert_rows",
        grid=(count, width // block),
        in_specs=[
            whole,
            whole,
            whole,
            pl.BlockSpec((1, D, block), lambda e, i: (e, 0, i)),
            pl.BlockSpec((1, block, D), lambda e, i: (e, i, 0)),
        ],
        out_specs=[whole, whole, pl.BlockSpec((1, total, 128), lambda e, i: (e, 0, 0))],
        out_shape=[
            jax.ShapeDtypeStruct(rows.shape, BF16),
            jax.ShapeDtypeStruct(rows.shape, F32),
            jax.ShapeDtypeStruct((count, total, 128), F32),
        ],
        scratch_shapes=[pltpu.VMEM((total, D), F32), pltpu.VMEM((total, D), F32)],
        compiler_params=pltpu.CompilerParams(vmem_limit_bytes=VMEM_LIMIT),
        cost_estimate=pl.CostEstimate(
            flops=8 * count * total * D * width,
            bytes_accessed=16 * count * D * width,
            transcendentals=count * total * width,
        ),
    )(rows, dye, cot, w_in, w_out)


def expert_kernel(rows_ref, dye_ref, win_ref, wout_ref, *rest):
    in_ref, out_ref = rest[-2:]
    total = rows_ref.shape[1]
    step = total // 3
    win, wout = win_ref[0], wout_ref[0]
    for c in range(3):
        rows = rows_ref[0, step * c : step * c + step]
        dye = dye_ref[0, step * c : step * c + step]
        hidden, slope = gelu_pair(mm(rows, win, 1, 0))
        pre_back = (mm(dye, wout, 1, 1) * slope).astype(BF16)
        grad_in = mm(rows, pre_back, 0, 0)
        grad_out = mm(hidden.astype(BF16), dye, 0, 0)
        if c == 0:
            in_ref[0], out_ref[0] = grad_in, grad_out
        else:
            in_ref[0] += grad_in
            out_ref[0] += grad_out


def expert_gradients(rows, dye, w_in, w_out, part, earlier):
    count, total, _ = rows.shape
    width, block = w_in.shape[2], 512
    blocks = width // block
    edges = (0, blocks // 2, blocks // 2 + blocks // 6, blocks)
    first, steps = edges[part], edges[part + 1] - edges[part]
    whole = pl.BlockSpec((1, total, D), lambda e, i: (e, 0, 0))
    by_in = pl.BlockSpec((1, D, block), lambda e, i: (e, 0, i + first))
    by_out = pl.BlockSpec((1, block, D), lambda e, i: (e, i + first, 0))
    return pl.pallas_call(
        expert_kernel,
        name=f"expert_gradients_{part}",
        grid=(count, steps),
        in_specs=[whole, whole, by_in, by_out] + [pl.BlockSpec(memory_space=pl.ANY)] * len(earlier),
        out_specs=[by_in, by_out],
        out_shape=[
            jax.ShapeDtypeStruct(w_in.shape, F32),
            jax.ShapeDtypeStruct(w_out.shape, F32),
        ],
        input_output_aliases={4 + n: n for n in range(len(earlier))},
        compiler_params=pltpu.CompilerParams(vmem_limit_bytes=VMEM_LIMIT),
        cost_estimate=pl.CostEstimate(
            flops=8 * count * total * D * block * steps,
            bytes_accessed=64 * count * D * block * steps,
            transcendentals=count * total * block * steps,
        ),
    )(rows, dye, w_in, w_out, *earlier)


def three_parts(x):
    parts = []
    for _ in range(3):
        parts.append(lax.reduce_precision(x, 8, 7))
        x = x - parts[-1]
    return parts


def block_codes(seg_all, blocks):
    count = blocks.shape[0]
    rows = seg_all.reshape(count, BLK)
    least, most = jnp.min(rows, axis=1), jnp.max(rows, axis=1)
    ids = jnp.arange(count, dtype=jnp.int32)
    gap = ids[:, None] - ids[None, :]
    meet = (most[None, :] >= least[:, None]) & (least[None, :] <= most[:, None])
    live = (gap >= 0) & (blocks == 1) & meet
    same = (
        (least == most)[:, None] & (least == most)[None, :] & (least[:, None] == least[None, :])
    )
    return jnp.where(live, jnp.where(same & (gap >= 2), 1, 2), 0).astype(jnp.int32)


def bias_inputs(table):
    gap = jnp.dot(table, gap_hot().T, precision=PRECISE)
    far = jnp.repeat(table[:, 31].reshape(PAIRS, 2), BLK, axis=1)
    return gap, far


def bias_back(dgap, dfar):
    near = jnp.dot(dgap, gap_hot(), precision=PRECISE)
    last = (jnp.arange(32) == 31).astype(F32)[None, :]
    return near + jnp.sum(dfar, axis=1, keepdims=True) * last


def body(
    tokens, segments, block_sets, routes, qkv_weight, out_weight, ffn_in, ffn_out,
    norm_gains, rel_bias, router, expert_in, expert_out, cotangent,
):
    gather = partial(lax.all_gather, axis_name="grp", axis=0, tiled=True)
    rows = tokens.shape[1]
    me = lax.axis_index("grp").astype(jnp.int32).reshape(1)
    replicas, groups = lax.axis_size("rep"), lax.axis_size("grp")
    mine, core = lax.axis_index("rep"), lax.axis_index("grp") % 2

    def from_replica(x, k):
        return lax.ppermute(x, "rep", [(i, i ^ k) for i in range(replicas)])

    def from_sibling(x):
        return lax.ppermute(x, "grp", [(i, i ^ 1) for i in range(groups)])

    def swapped_cores(got):
        other = from_sibling(jnp.stack(got))
        return [other[k] for k in range(replicas - 1)]

    def layer_quarter(layer, after):
        count = qkv_weight.shape[0] // replicas
        part_qkv = lax.dynamic_slice(
            qkv_weight, (mine * count, layer, 0, 0), (count, 1) + qkv_weight.shape[2:]
        )
        part_out = lax.dynamic_slice(out_weight, (mine * count, layer, 0), (count, 1, D))
        part = jnp.concatenate([part_qkv.reshape(count, 3 * D), part_out.reshape(count, D)], axis=1)
        if after is not None:
            part, _ = lax.optimization_barrier((part, after))
        return lax.all_gather(part, "grp", axis=0)

    def layer_weights(quarter):
        width = quarter.shape[2] // 2
        half = lax.dynamic_slice_in_dim(quarter, core * width, width, 2)
        got = [from_replica(half, k) for k in range(1, replicas)]
        other = swapped_cores(got)
        full = jnp.zeros((groups, replicas) + quarter.shape[1:], BF16)
        full = lax.dynamic_update_slice(full, quarter[:, None], (0, mine, 0, 0))
        for k in range(1, replicas):
            for part, which in ((got[k - 1], core), (other[k - 1], 1 - core)):
                full = lax.dynamic_update_slice(full, part[:, None], (0, mine ^ k, 0, which * width))
        full = full.reshape(-1, 2 * width)
        return full[:, : 3 * D], full[:, 3 * D :]

    quarter_first = layer_quarter(0, None)
    w_first = layer_weights(quarter_first)

    span = ffn_in.shape[1] // replicas
    piece = span // 2
    ffn_own = [lax.dynamic_slice_in_dim(w, mine * span, span, 1) for w in (ffn_in, ffn_out)]
    ffn_own = jnp.concatenate([w[:, h * piece : h * piece + piece] for h in range(2) for w in ffn_own], axis=1)
    seg_row = jnp.pad(segments.astype(BF16), ((0, 7), (0, ffn_own.shape[1] - rows)))
    ffn_own = jnp.concatenate([ffn_own, seg_row], axis=0)
    ffn_own, quarter_first = lax.optimization_barrier((ffn_own, quarter_first))
    ffn_quarter = lax.all_gather(ffn_own, "grp", axis=0)
    seg_all = ffn_quarter[:, ffn_in.shape[0], :rows].astype(jnp.int32).reshape(-1)
    tokens_own, ffn_quarter = lax.optimization_barrier((tokens[0], ffn_quarter))
    x_all = gather(tokens_own)
    ffn_mine = [
        lax.dynamic_slice(ffn_quarter, (0, 0, n * span), (groups, ffn_in.shape[0], span)).reshape(-1, span)
        for n in (core, 1 - core)
    ]
    ffn_peers = [from_replica(ffn_mine[0], k) for k in range(1, replicas)]

    quarter_second = layer_quarter(1, x_all)
    code = block_codes(seg_all, block_sets[0])
    shared = (seg_all[:, None], seg_all.reshape(-1, BLK))
    w_qkv, w_out = [w_first[0]], [w_first[1]]

    def attend(residual, normed, normed_all, layer):
        w = w_qkv[layer]
        qt = mm(w[:, :D], normed, 0, 1).astype(BF16) * jnp.asarray(0.125, BF16)
        kv = mm(normed_all, w[:, D:], 1, 0).astype(BF16)
        gap, far = bias_inputs(rel_bias[layer])
        ctxt, ctxb, lse = attention_forward(code, me, qt, kv, gap, far, *shared)
        branch = mm(ctxb, w_out[layer], 1, 0)
        saved = (residual, normed, normed_all, kv, ctxt, ctxb, lse, gap, far)
        return residual + branch, saved

    def attend_back(grad_out, saved, layer, qt_all, held, cover, late):
        residual, normed, normed_all, kv, ctxt, ctxb, lse, gap, far = saved
        w, wo = w_qkv[layer], w_out[layer]
        grad_low = grad_out.astype(BF16)
        dctx_own = mm(wo, grad_low, 1, 1).astype(BF16)
        delta = jnp.sum((dctx_own.astype(F32) * ctxt).reshape(HEADS, HEAD, rows), axis=1)
        stats = jnp.stack(three_parts(jnp.concatenate([lse, delta], axis=0)), axis=1)
        stats = stats.reshape(2 * HEADS, 3 * rows).astype(BF16)
        sent = jnp.concatenate([grad_low, stats, jnp.zeros((8, D), BF16)], axis=0)
        got, covered = lax.optimization_barrier((lax.all_gather(sent, "grp", axis=0), cover(sent)))
        grad_all = got[:, :rows].reshape(-1, D)
        stats_all = got[:, rows : rows + 2 * HEADS].reshape(-1, 2 * HEADS, 3, rows)
        stats_all = jnp.sum(stats_all.astype(F32), axis=2)
        dt_all = mm(wo, grad_all, 1, 1).astype(BF16)
        dt_all, held = lax.optimization_barrier((dt_all, held))
        dqkv, dgap, dfar = attention_backward(
            code, me, qt_all, dt_all, kv, stats_all, gap, far, *shared
        )
        dqkv, done = lax.optimization_barrier((dqkv, late(held)))
        normed_grad = mm(dqkv, w, 1, 1)
        _, pull_back = jax.vjp(norm_rows, residual, norm_gains[layer, 0])
        residual_grad, gain_grad = pull_back(normed_grad)
        table_grad = bias_back(dgap, dfar)
        return grad_out + residual_grad, dqkv, gain_grad, table_grad, grad_all, held, covered, done

    experts_all = router.shape[1]
    per_group = experts_all // groups
    capacity = rows * 2 * 10 // (7 * experts_all) + 1
    slots = (capacity + 16) // 16 * 16
    chosen = routes[0]
    ids = jnp.arange(experts_all, dtype=jnp.int32)
    chosen_hot = (chosen[:, :, None] == ids[None, None, :]).astype(F32)
    flat_hot = chosen_hot.reshape(2 * rows, experts_all)
    before = jnp.tril(jnp.ones((2 * rows, 2 * rows), BF16), -1)
    earlier = mm(before, flat_hot.astype(BF16), 1, 0)
    slot_ids = jnp.sum(earlier * flat_hot, axis=1).astype(jnp.int32)
    place = (chosen.reshape(-1) * slots + slot_ids).reshape(rows, 2)
    lanes = jnp.arange(experts_all * slots, dtype=jnp.int32)
    pick = [(place[:, k][:, None] == lanes[None, :]).astype(BF16) for k in range(2)]
    both = pick[0] + pick[1]

    def exchange(x):
        return lax.all_to_all(
            x.reshape(groups, per_group * slots, D), "grp", split_axis=0, concat_axis=0, tiled=True
        )

    def by_expert(x):
        return x.reshape(groups, per_group, slots, -1).swapaxes(0, 1).reshape(per_group, groups * slots, -1)

    def by_source(x):
        return x.reshape(per_group, groups, slots, -1).swapaxes(0, 1).reshape(groups, per_group * slots, -1)

    def all_replicas(x):
        return lax.all_gather(x, "rep", axis=1, tiled=True)

    x_all, cot_own = lax.optimization_barrier((x_all, cotangent[0]))
    cot_rows = by_expert(exchange(mm(both, cot_own, 0, 0).astype(BF16)))

    stream = tokens[0].astype(F32)
    own_a = norm_rows(stream, norm_gains[0, 0]).astype(BF16)
    all_a = norm_rows(x_all.astype(F32), norm_gains[0, 0]).astype(BF16)
    first_out, saved_a = attend(stream, own_a, all_a, 0)
    first_out, quarter_second, ffn_peers = lax.optimization_barrier(
        (first_out, quarter_second, ffn_peers)
    )
    ffn_others = [from_sibling(x) for x in ffn_peers]
    pieces = ffn_mine + [x for pair in zip(ffn_peers, ffn_others) for x in pair]
    after_ffn, normed_ffn, hidden_ffn, slope_ffn = ffn_forward(first_out, norm_gains[0, 1], pieces)
    after_ffn, cot_rows = lax.optimization_barrier((after_ffn, cot_rows))

    own_b = norm_rows(after_ffn, norm_gains[1, 0]).astype(BF16)
    own_b, quarter_second = lax.optimization_barrier((own_b, quarter_second))
    w_second = layer_weights(quarter_second)
    w_qkv.append(w_second[0])
    w_out.append(w_second[1])
    full_in = jnp.concatenate([x[:, :piece] for x in pieces], axis=1)
    full_down = jnp.concatenate([x[:, piece:] for x in pieces], axis=1)
    all_b, cot_rows, full_in, full_down = lax.optimization_barrier(
        (gather(own_b), cot_rows, full_in, full_down)
    )
    cot_all = all_replicas(cot_rows)
    second_out, saved_b = attend(after_ffn, own_b, all_b, 1)
    normed_moe = norm_rows(second_out, norm_gains[1, 1]).astype(BF16)
    normed_wide = normed_moe.astype(F32)
    router_wide = router.astype(F32)
    logits = jnp.dot(normed_wide, router_wide, precision=PRECISE)

    last_row = (jnp.arange(slots) == slots - 1)[None, :, None]

    def with_scalars(rows_in, values):
        parts = [jnp.pad(part, ((0, 0), (0, 128 - slots))) for part in three_parts(values)]
        info = jnp.concatenate(parts + [jnp.zeros((values.shape[0], D - 384), F32)], axis=1)
        return jnp.where(last_row, info[:, None, :], rows_in).astype(BF16)

    def scalars_of(rows_in):
        info = rows_in[:, slots - 1, :].astype(F32)
        total = info[:, 0:slots] + info[:, 128 : 128 + slots] + info[:, 256 : 256 + slots]
        return jnp.where(jnp.arange(slots)[None, :] == slots - 1, 0.0, total)

    grad_final = cotangent[0].astype(F32)
    selected = jnp.sum(logits[:, None, :] * chosen_hot, axis=-1)
    gate_probs = jax.nn.softmax(selected, axis=-1)
    gate_slots = jnp.sum(
        jnp.where(pick[0] == 1, gate_probs[:, 0:1], 0.0) + jnp.where(pick[1] == 1, gate_probs[:, 1:2], 0.0),
        axis=0,
    ).reshape(experts_all, slots)
    sent = mm(both, normed_moe, 0, 0).reshape(experts_all, slots, D)
    rows_e = by_expert(exchange(with_scalars(sent, gate_slots)))

    def gated(rows_in, cot):
        gates = scalars_of(rows_in.reshape(-1, slots, D)).reshape(per_group, -1, 1)
        return (gates * cot.astype(F32)).astype(BF16)

    dye = gated(rows_e, cot_rows)
    made_rows, rows_grad, gate_back = expert_rows(rows_e, dye, cot_rows, expert_in, expert_out)
    rows_grad = rows_grad.reshape(per_group * groups, slots, D)
    rows_grad = with_scalars(rows_grad, gate_back[:, :, 0].reshape(-1, slots))
    queries_all = [
        mm(w_qkv[n][:, :D], all_rows, 0, 1).astype(BF16) * jnp.asarray(0.125, BF16)
        for n, all_rows in enumerate((all_a, all_b))
    ]
    rows_e, cot_all = lax.optimization_barrier((rows_e, cot_all))
    rows_all = all_replicas(rows_e)
    dye_all = gated(rows_all, cot_all)
    back_grad, queries_all, dye_all = lax.optimization_barrier(
        (exchange(by_source(rows_grad)), queries_all, dye_all)
    )
    back_slots = scalars_of(back_grad.reshape(experts_all, slots, D)).reshape(1, -1)
    back_grad = back_grad.reshape(experts_all * slots, D)
    gate_grad = jnp.stack(
        [jnp.sum(jnp.where(pick[k] == 1, back_slots, 0.0), axis=1) for k in range(2)], axis=-1
    )
    select_grad = gate_probs * (gate_grad - jnp.sum(gate_probs * gate_grad, axis=-1, keepdims=True))
    logit_grad = jnp.sum(select_grad[:, :, None] * chosen_hot, axis=1)
    normed_moe_grad = jnp.dot(logit_grad, router_wide.T, precision=PRECISE) + mm(both, back_grad, 1, 0)
    _, pull_moe = jax.vjp(norm_rows, second_out, norm_gains[1, 1])
    moe_resid_grad, moe_gain_grad = pull_moe(normed_moe_grad)
    grad_second = grad_final + moe_resid_grad
    router_part = jnp.dot(normed_wide.T, logit_grad, precision=PRECISE)

    def finish(made):
        returned = exchange(by_source(made)).reshape(experts_all * slots, D)
        picked = [mm(pick[k], returned, 1, 0) for k in range(2)]
        return second_out + gate_probs[:, 0:1] * picked[0] + gate_probs[:, 1:2] * picked[1]


    def expert_half(part, earlier, extra=()):
        def run(sent):
            rows_in, _, _ = lax.optimization_barrier((rows_all, sent, extra))
            return tuple(expert_gradients(rows_in, dye_all, expert_in, expert_out, part, earlier))

        return run

    held_b = (made_rows, mm(saved_b[5], grad_second.astype(BF16), 0, 0).astype(BF16))

    def late_b(held):
        return lax.psum_scatter(held[1], "grp", scatter_dimension=0, tiled=True)

    back_b = attend_back(grad_second, saved_b, 1, queries_all[1], held_b, expert_half(0, ()), late_b)
    grad_ffn, dqkv_b, gain_grad_b, table_grad_b, _, held_b, expert_sums, shard_out = back_b
    made_held = held_b[0]
    final_out = finish(made_held)
    grad_ffn, final_out = lax.optimization_barrier((grad_ffn, final_out))
    down_low = grad_ffn.astype(BF16)
    down_part = mm(down_low, hidden_ffn, 0, 0)
    hidden_ffn_grad = mm(down_low, full_down, 1, 0)
    pre_ffn_grad = (hidden_ffn_grad * slope_ffn).astype(BF16)
    in_part = mm(normed_ffn, pre_ffn_grad, 0, 0)
    normed_ffn_grad = mm(pre_ffn_grad, full_in, 1, 1)
    _, pull_ffn = jax.vjp(norm_rows, first_out, norm_gains[0, 1])
    ffn_resid_grad, ffn_gain_grad = pull_ffn(normed_ffn_grad)
    grad_first = grad_ffn + ffn_resid_grad
    def packed(parts):
        return jnp.concatenate([part.astype(BF16) for part in parts], axis=1)

    def halves(k, which):
        at = k * span + which * piece
        return packed([x[:, at : at + piece] for x in (down_part, in_part)])

    their_half = jnp.stack([halves(k, 1) for k in range(replicas)])
    theirs = from_sibling(their_half)
    ffn_parts = [
        (halves(k, 0).astype(F32) + theirs[k].astype(F32)).astype(BF16) for k in range(replicas)
    ]

    def cover_a(sent):
        dq, _ = lax.optimization_barrier((dqkv_b, sent))
        part_b = packed(
            [
                mm(own_b, dq, 0, 0),
                mm(saved_a[5], grad_first.astype(BF16), 0, 0),
            ]
        )
        return expert_half(1, expert_sums, their_half)(sent), part_b, ffn_parts

    back_a = attend_back(grad_first, saved_a, 0, queries_all[0], (), cover_a, lambda held: ())
    grad_tokens, dqkv_a, gain_grad_a, table_grad_a, grad_all_a, _, covered_a, _ = back_a
    expert_sums, parts_b, ffn_parts = covered_a
    ffn_got = [from_replica(ffn_parts[k], k) for k in range(1, replicas)]
    parts_b, _ = lax.optimization_barrier((parts_b, grad_all_a))
    parts_a = mm(own_a, dqkv_a, 0, 0).astype(BF16)
    shard_b = lax.psum_scatter(parts_b, "grp", scatter_dimension=0, tiled=True)
    parts_a, shard_b, ffn_got = lax.optimization_barrier((parts_a, shard_b, ffn_got))
    shard_a = lax.psum_scatter(parts_a, "grp", scatter_dimension=0, tiled=True)
    expert_in_sum, expert_out_sum = expert_half(2, expert_sums)(parts_a)

    def over_replicas(x):
        half = x.shape[0] // 2

        def add(v, mask):
            return (v.astype(F32) + from_replica(v, mask).astype(F32)).astype(BF16)

        first = [1 << b for b in range(replicas.bit_length() - 1)]
        top, low = x[:half], x[half:]
        for a, b in zip(first, first[::-1]):
            top, low = add(top, a), add(low, b)
        return jnp.concatenate([top, low], axis=0).astype(F32)

    ffn_total = ffn_parts[0].astype(F32)
    for x in ffn_got:
        ffn_total = ffn_total + x.astype(F32)
    ffn_total = ffn_total.astype(BF16)
    shard_a, ffn_total = lax.optimization_barrier((shard_a, ffn_total))
    same_core = [list(range(c, groups, 2)) for c in range(2)]
    band = lax.psum_scatter(
        ffn_total, "grp", scatter_dimension=0, tiled=True, axis_index_groups=same_core
    )
    band = band.reshape(2, -1, band.shape[1])
    kept = lax.dynamic_index_in_dim(band, core, 0, False)
    other = from_sibling(lax.dynamic_index_in_dim(band, 1 - core, 0, False))
    low, high = jnp.where(core == 0, kept, other), jnp.where(core == 0, other, kept)
    ffn_shard = jnp.concatenate([low[:, piece:], high[:, piece:], low[:, :piece], high[:, :piece]], axis=1)
    ffn_peers = [ffn_shard] + [from_replica(ffn_shard, k) for k in range(1, replicas)]

    def quarter_of(q):
        x = ffn_peers[0]
        for k in range(1, replicas):
            x = jnp.where(mine ^ k == q, ffn_peers[k], x)
        return x.astype(F32)

    ffn_sums = [quarter_of(q) for q in range(replicas)]
    in_sum = jnp.concatenate([x[:, :span] for x in ffn_sums], axis=1)
    down_sum = jnp.concatenate([x[:, span:] for x in ffn_sums], axis=1)
    shard_b = jnp.concatenate([shard_b[:, : 3 * D], shard_out, shard_b[:, 3 * D :]], axis=1)
    total_b = shard_b.astype(F32)
    for k in range(1, replicas):
        total_b = total_b + from_replica(shard_b, k).astype(F32)
    qkv_b, out_b, out_a = total_b[:, : 3 * D], total_b[:, 3 * D : 4 * D], total_b[:, 4 * D :]
    qkv_a = over_replicas(shard_a)
    qkv_sum = jnp.stack([qkv_a, qkv_b], axis=1).reshape(qkv_weight.shape)
    out_sum = jnp.stack([out_a, out_b], axis=1)
    gain_all = jnp.stack(
        [jnp.stack([gain_grad_a, ffn_gain_grad]), jnp.stack([gain_grad_b, moe_gain_grad])]
    )
    table_all = jnp.stack([table_grad_a, table_grad_b])
    small = [gain_all, table_all, router_part]
    flat = jnp.concatenate([x.reshape(-1, BLK) for x in small], axis=0)
    flat, expert_out_sum, ffn_total = lax.optimization_barrier((flat, expert_out_sum, ffn_total))
    for axis, count in (("rep", replicas), ("grp", groups)):
        for bit in range(count.bit_length() - 1):
            flat = flat + lax.ppermute(flat, axis, [(i, i ^ (1 << bit)) for i in range(count)])
    sizes = [x.size // BLK for x in small]
    cut = [flat[sum(sizes[:n]) : sum(sizes[: n + 1])].reshape(x.shape) for n, x in enumerate(small)]
    gain_sum, table_sum, router_sum = cut
    return (
        final_out[None], grad_tokens[None], qkv_sum, out_sum, in_sum, down_sum,
        gain_sum, table_sum, router_sum, expert_in_sum, expert_out_sum,
    )


def solution(mesh):
    return jax.shard_map(
        body,
        mesh=mesh,
        in_specs=(
            P("rep", "grp", None),
            P("rep", "grp"),
            P("rep", None, None),
            P("rep", "grp", None),
            P("grp", None, None, None),
            P("grp", None, None),
            P("grp", None),
            P("grp", None),
            P(),
            P(),
            P(),
            P("grp", None, None),
            P("grp", None, None),
            P("rep", "grp", None),
        ),
        out_specs=(
            P("rep", "grp", None),
            P("rep", "grp", None),
            P("grp", None, None, None),
            P("grp", None, None),
            P("grp", None),
            P("grp", None),
            P(),
            P(),
            P(),
            P("grp", None, None),
            P("grp", None, None),
        ),
        check_vma=False,
    )
```
